32 devices in a mesh: seq: 2 (over core), dp: 16 (over z, y, x).
Axes of the slice: x: 2, y: 2, z: 4, core: 2. Of those that a mesh axis runs over, the one named last changes fastest.
Arguments:
- tokens: bfloat16 [16, 1536, 768], P('dp', 'seq'), may hold values from -6 to 6
- time_embed: float32 [16, 768], P('dp'), may hold values from -4 to 4
- segments: int32 [16, 1536], P('dp'), may hold values from 0 to 3, never falling along the last dimension, each value on 1 to 768 neighbouring positions
- input_weight: bfloat16 [768, 2304], P('dp'), may hold values from -0.3125 to 0.3125
- query_bias: bfloat16 [768], P('dp'), may hold values from -3 to 3
- value_bias: bfloat16 [768], P('dp'), may hold values from -2 to 2
- output_weight: bfloat16 [768, 768], P('dp'), may hold values from -0.875 to 0.875
- output_bias: bfloat16 [768], P('dp'), may hold values from -2 to 2
- first_gain: bfloat16 [768], P('dp'), may hold values from 0.5 to 1.5
- first_shift: bfloat16 [768], P('dp'), may hold values from -2 to 2
- expand_weight: bfloat16 [768, 3072], P('dp'), may hold values from -0.21875 to 0.21875
- expand_bias: bfloat16 [3072], P('dp'), may hold values from -3 to 3
- contract_weight: bfloat16 [3072, 768], P('dp'), may hold values from -0.15625 to 0.15625
- contract_bias: bfloat16 [768], P('dp'), may hold values from -2 to 2
- second_gain: bfloat16 [768], P('dp'), may hold values from 0.5 to 1.5
- second_shift: bfloat16 [768], P('dp'), may hold values from -2 to 2
- cotangent: bfloat16 [16, 1536, 768], P('dp', 'seq'), may hold values from -6 to 6
Outputs:
- layer_output: bfloat16 [16, 1536, 768], P('dp', 'seq')
- input_grad: float32 [16, 1536, 768], P('dp', 'seq')
- grad_input_weight: float32 [768, 2304], P('dp')
- grad_query_bias: float32 [768], P('dp')
- grad_value_bias: float32 [768], P('dp')
- grad_output_weight: float32 [768, 768], P('dp')
- grad_output_bias: float32 [768], P('dp')
- grad_first_gain: float32 [768], P('dp')
- grad_first_shift: float32 [768], P('dp')
- grad_expand_weight: float32 [768, 3072], P('dp')
- grad_expand_bias: float32 [3072], P('dp')
- grad_contract_weight: float32 [3072, 768], P('dp')
- grad_contract_bias: float32 [768], P('dp')
- grad_second_gain: float32 [768], P('dp')
- grad_second_shift: float32 [768], P('dp')
The draws below stay inside these ranges and needn't reach their ends.
Inputs may be any that keep to these rules, and one draw needn't show every extreme that they name: `segments`: within each sequence segment numbers start at 0 and never fall; each of the 4 documents has 1 to 768 tokens and one has exactly 768.
All inputs are finite; a program needn't handle non-finite values.
Results may differ from the reference program's by a relative error of at most 0.017.
The reference program's roundings to bfloat16 on the way count: a program that leaves them out, or rounds other values in their place, can miss the bound.
Values may be sent and summed in bfloat16 or wider, within the bound.
A program may use at most 192 MiB of HBM per device.

```python
import math
import jax
import jax.numpy as jnp
import numpy as np
from jax import lax

D = 768
HD = 64
FF = 3072
LEN = 1536
SEGS = 4
DOC_MOST = 768
SEQS = 16


def with_spikes(array, stream_key, source, target, shards_of, factor):
    def block_of(axis_at):
        return (jnp.arange(array.shape[axis_at]) // (array.shape[axis_at] // shards_of)).reshape((-1,) + (1,) * (array.ndim - 1 - axis_at))

    near = jax.random.permutation(stream_key, shards_of)[block_of(target)]
    second = (block_of(target) + shards_of // 2) % shards_of
    return jnp.where((block_of(source) == near) | (block_of(source) == second), factor * array, array)


def level_of(rng, shape, shards, low, high):
    loudness = 1.0
    for dim, parts in shards:
        steps = jax.random.uniform(jax.random.fold_in(jax.random.fold_in(rng, 6), dim), (parts,), jnp.float32, low / len(shards), high / len(shards))
        loudness = loudness * jnp.repeat(jnp.exp(steps), shape[dim] // parts).reshape((-1,) + (1,) * (len(shape) - 1 - dim))
    return loudness


def length_profile(amount, total, limit, lean):
    loads = [(1 << 20) // math.isqrt(standing ** lean) + 1 for standing in range(2, amount + 1)]
    spare, given = total - limit - (amount - 1), [1] * (amount - 1)
    while spare > 0:
        free = [i for i in range(amount - 1) if given[i] < limit]
        mass, remaining = sum([loads[i] for i in free]), spare
        for i in free:
            addition = min(limit - given[i], max(1, remaining * loads[i] // mass), spare)
            given[i] = given[i] + addition
            spare = spare - addition
    return np.array([limit] + given)


def ragged_sizes(key, amount, total, limit, lean):
    if amount == 2:
        one = jax.random.randint(key, (), max(1, total - limit), min(limit, total - 1) + 1)
        return jnp.stack([one, total - one])
    lengths = jnp.asarray(length_profile(amount, total, limit, lean), jnp.int32)
    couples = (amount - 1) // 2
    source_of, taker = lengths[1:1 + 2 * couples:2], lengths[2:2 + 2 * couples:2]
    margin = jnp.minimum(source_of - 1, limit - taker)
    moved = jax.random.randint(jax.random.fold_in(key, 1), (couples,), 0, 1 << 20) % (margin + 1)
    lengths = lengths.at[1:1 + 2 * couples:2].set(source_of - moved).at[2:2 + 2 * couples:2].set(taker + moved)
    return lengths[jax.random.permutation(jax.random.fold_in(key, 2), amount)]


def gaussian(rng, dims, scale, most, pieces=(), kind=jnp.bfloat16):
    array = jax.random.normal(rng, dims, jnp.float32) * scale
    if len(pieces) > 0:
        array = level_of(rng, dims, pieces, -0.22, 0.18) * array
    return jnp.clip(array, min=-most, max=most).astype(kind)


def gaussian_with(stream_key, dims, deviation, most, shards, heavy, held_as=jnp.bfloat16):
    array = deviation * jax.random.normal(stream_key, dims, jnp.float32)
    if shards:
        array = array * level_of(stream_key, dims, shards, -0.22, 0.18)
    return jnp.clip(with_spikes(array, jax.random.fold_in(stream_key, 3), *heavy), -most, most).astype(held_as)


def setup_inputs(seed: int = 0) -> dict:
    arg_keys = jax.random.split(jax.random.key(seed), 18)
    tokens = gaussian_with(arg_keys[0], (SEQS, LEN, D), 1.0, 6.0, ((0, 16), (1, 2)), (0, 2, 16, 2.0))
    time_embed = gaussian(arg_keys[1], (SEQS, D), 0.5, 4.0, ((0, 16),), jnp.float32)
    segments = jax.vmap(lambda own: jnp.searchsorted(jnp.cumsum(ragged_sizes(own, SEGS, LEN, DOC_MOST, 1)), jnp.arange(LEN), side="right"))(jax.random.split(arg_keys[2], SEQS)).reshape((SEQS, LEN)).astype(jnp.int32)
    input_weight = gaussian(arg_keys[3], (D, 3 * D), (D // 2) ** -0.5, 0.3125, ((0, 16),))
    query_bias = gaussian(arg_keys[4], (D,), 0.5, 3.0, ((0, 16),))
    value_bias = gaussian(arg_keys[5], (D,), 0.3, 2.0, ((0, 16),))
    output_weight = gaussian(arg_keys[6], (D, D), (D // 16) ** -0.5, 0.875, ((0, 16),))
    output_bias = gaussian(arg_keys[7], (D,), 0.3, 2.0, ((0, 16),))
    first_gain = jnp.clip(1.0 + 0.1 * jax.random.normal(arg_keys[8], (D,), jnp.float32), 0.5, 1.5).astype(jnp.bfloat16)
    first_shift = gaussian(arg_keys[9], (D,), 0.3, 2.0, ((0, 16),))
    expand_weight = gaussian(arg_keys[10], (D, FF), D ** -0.5, 0.21875, ((0, 16),))
    expand_bias = gaussian(arg_keys[11], (FF,), 0.5, 3.0, ((0, 16),))
    contract_weight = gaussian(arg_keys[12], (FF, D), (FF // 2) ** -0.5, 0.15625, ((0, 16),))
    contract_bias = gaussian(arg_keys[13], (D,), 0.3, 2.0, ((0, 16),))
    second_gain = jnp.clip(1.0 + 0.1 * jax.random.normal(arg_keys[14], (D,), jnp.float32), 0.5, 1.5).astype(jnp.bfloat16)
    second_shift = gaussian(arg_keys[15], (D,), 0.3, 2.0, ((0, 16),))
    cotangent = gaussian_with(arg_keys[16], (SEQS, LEN, D), 1.0, 6.0, ((0, 16), (1, 2)), (0, 2, 16, 2.0))
    return {"tokens": tokens, "time_embed": time_embed, "segments": segments, "input_weight": input_weight, "query_bias": query_bias, "value_bias": value_bias, "output_weight": output_weight, "output_bias": output_bias, "first_gain": first_gain, "first_shift": first_shift, "expand_weight": expand_weight, "expand_bias": expand_bias, "contract_weight": contract_weight, "contract_bias": contract_bias, "second_gain": second_gain, "second_shift": second_shift, "cotangent": cotangent}


HIGHEST = lax.Precision.HIGHEST
epsilon = 1e-05

@jax.custom_vjp
def low(v):
    return lax.optimization_barrier(v.astype(jnp.bfloat16)).astype(jnp.float32)

@jax.custom_vjp
def low_back(v):
    return v

def low_keep(v):
    return (low(v), None)

def low_pass(kept, grad):
    return (grad,)

def back_keep(v):
    return (v, None)

def back_low(kept, grad):
    return (low(grad),)
low.defvjp(low_keep, low_pass)
low_back.defvjp(back_keep, back_low)

def gelu(values):
    return 0.5 * values * (1.0 + lax.erf(values * math.sqrt(0.5)))

def normalize(values, gain, shift):
    mean = lax.optimization_barrier(jnp.mean(values, axis=-1, keepdims=True))
    centred = values - mean
    scale = lax.rsqrt(lax.optimization_barrier(jnp.mean(centred * centred, axis=-1, keepdims=True)) + epsilon)
    return centred * scale * gain + shift

def layer(params, start, segment_row):
    input_weight, query_bias, value_bias, output_weight, output_bias, first_gain, first_shift, expand_weight, expand_bias, contract_weight, contract_bias, second_gain, second_shift = params
    width = input_weight.shape[0]
    length = start.shape[0]
    heads = width // HD
    start_low = low(start)
    projected = jnp.dot(start_low, input_weight, precision=HIGHEST)
    query = low(low_back(projected[:, :width] + query_bias)).reshape(length, heads, HD)
    key = low(low_back(projected[:, width:2 * width])).reshape(length, heads, HD)
    value = low(low_back(projected[:, 2 * width:] + value_bias)).reshape(length, heads, HD)
    scores = jnp.einsum('qhd,khd->hqk', query, key, precision=HIGHEST) * HD ** (-0.5)
    scores = low_back(scores)
    same = (segment_row[:, None] == segment_row[None, :])[None]
    scores = jnp.where(same, scores, -1e+30)
    top = lax.optimization_barrier(jnp.max(scores, axis=-1, keepdims=True))
    expo = jnp.exp(scores - top)
    probs = expo / lax.optimization_barrier(jnp.sum(expo, axis=-1, keepdims=True))
    heads_out = jnp.einsum('hqk,khd->qhd', low(probs), value, precision=HIGHEST).reshape(length, width)
    heads_out = low(low_back(heads_out))
    attention = low_back(jnp.dot(heads_out, output_weight, precision=HIGHEST) + output_bias)
    first = normalize(start + attention, first_gain, first_shift)
    expand = low_back(jnp.dot(low(first), expand_weight, precision=HIGHEST) + expand_bias)
    hidden = low(gelu(expand))
    branch = low_back(jnp.dot(hidden, contract_weight, precision=HIGHEST) + contract_bias)
    return normalize(first + branch, second_gain, second_shift)

def reference(tokens, time_embed, segments, input_weight, query_bias, value_bias, output_weight, output_bias, first_gain, first_shift, expand_weight, expand_bias, contract_weight, contract_bias, second_gain, second_shift, cotangent):
    params = tuple((p.astype(jnp.float32) for p in (input_weight, query_bias, value_bias, output_weight, output_bias, first_gain, first_shift, expand_weight, expand_bias, contract_weight, contract_bias, second_gain, second_shift)))

    def one_sequence(carry, item):
        token_rows, embed_row, segment_row, cotangent_rows = item
        start = token_rows.astype(jnp.float32) + embed_row.astype(jnp.float32)[None, :]
        output, pullback = jax.vjp(lambda p, s: layer(p, s, segment_row), params, start)
        grads, start_grad = pullback(cotangent_rows.astype(jnp.float32))
        carry = jax.tree.map(jnp.add, carry, grads)
        return (carry, (output.astype(jnp.bfloat16), start_grad))
    zeros = jax.tree.map(jnp.zeros_like, params)
    totals, (outputs, input_grad) = lax.scan(one_sequence, zeros, (tokens, time_embed, segments, cotangent))
    return (outputs, input_grad, totals[0], totals[1], totals[2], totals[3], totals[4], totals[5], totals[6], totals[7], totals[8], totals[9], totals[10], totals[11], totals[12])
```

```python
import functools
import math

import jax
import jax.numpy as jnp
from jax import lax
from jax.experimental import pallas as pl
from jax.experimental.pallas import tpu as pltpu
from jax.sharding import PartitionSpec as P

HD = 64
DOCS = 4
BF = jnp.bfloat16
F32 = jnp.float32
MESH = pl.DeviceIdType.MESH
VM = pltpu.VMEM
DMA = pltpu.SemaphoreType.DMA


def nn(a, b):
    return jnp.dot(a, b, preferred_element_type=F32)


def nt(a, b):
    return lax.dot_general(a, b, (((1,), (1,)), ((), ())), preferred_element_type=F32)


def tn(a, b):
    return lax.dot_general(a, b, (((0,), (0,)), ((), ())), preferred_element_type=F32)


def fused_kernel(
    tokens, cot, te, seg, win_s, wout_s, wexp_s, wcon_s, small_s,
    lo_o, ig_o, gin_o, gout_o, gexp_o, gcon_o, gvec_o, spill,
    win, wout, wexp, wcon, tok, tokr, cotn, cotr, vec, fullv, fulle, proj, xl, n1, bias,
    sc1, heads, fl, hidden, slope, pslot, lonew, lor, sg, bg,
    gin, con_r, gv, ge, vout, vsum, vr, fin, fout, fexp, fcon,
    swap_sem, ls, gs, gr, ps, rs, rr, pd,
):
    T, D = tok.shape
    FF = wexp.shape[1]
    me = lax.axis_index("dp")
    c = lax.axis_index("seq")
    x = lax.rem(me, 2)
    y = lax.rem(me // 2, 2)
    xy = lax.rem(me, 4)
    z = me // 4
    flip_x = me + 1 - 2 * x
    flip_y = me + 2 - 4 * y
    near = (1 - c) * flip_x + c * flip_y
    far = (1 - c) * flip_y + c * flip_x
    other = 1 - c
    zs = [lax.rem(z + k, 4) * 4 + xy for k in (1, 2, 3)]

    def send(src, dst, s, r, dp, seq):
        return pltpu.make_async_remote_copy(
            src_ref=src, dst_ref=dst, send_sem=s, recv_sem=r,
            device_id={"dp": dp, "seq": seq}, device_id_type=MESH,
        )

    barrier = pltpu.get_barrier_semaphore()
    for dp, seq in [(me, other), (near, c), (far, c)] + [(q, c) for q in zs]:
        pl.semaphore_signal(
            barrier, inc=1, device_id={"dp": dp, "seq": seq}, device_id_type=MESH
        )
    pl.semaphore_wait(barrier, 6)

    def al(v, m):
        return pl.multiple_of(v, m)

    class Piece:
        def __init__(self, n, shard, buf, rows, col, half):
            self.n, self.shard, self.buf, self.rows, self.col, self.half = n, shard, buf, rows, col, half

        def cols(self, core):
            return pl.ds(al(self.col + core * self.half, 128), self.half)

        def block(self, o):
            return self.buf.at[pl.ds(al(o * self.rows, 16), self.rows), self.cols(c)]

        def many(self, k):
            return self.buf.at[pl.ds(0, k * self.rows), self.cols(c)]

        def recv(self, stage, k):
            send(self.many(k), self.many(k), gs.at[self.n, stage], gr.at[self.n, stage], me, other).wait_recv()

        def sent(self, stage, k):
            send(self.many(k), self.many(k), gs.at[self.n, stage], gr.at[self.n, stage], me, other).wait_send()

        def local(self):
            return pltpu.make_async_copy(
                self.shard.at[:, self.cols(c)], self.block(me), ls.at[self.n]
            )

        def s1(self):
            self.local().start()
            for q in zs:
                send(self.shard.at[:, self.cols(c)], self.block(me), gs.at[self.n, 0], gr.at[self.n, 0], q, c).start()

        def s2(self):
            self.local().wait()
            self.recv(0, 3)

            def one(k, _):
                b = self.block(k * 4 + xy)
                send(b, b, gs.at[self.n, 1], gr.at[self.n, 1], near, c).start()
                return 0

            lax.fori_loop(0, 4, one, 0)

        def s3(self):
            self.recv(1, 4)

            def one(k, _):
                b = self.block((k // 2) * 4 + (1 - c) * 2 * y + c * x + lax.rem(k, 2) * (1 + c))
                send(b, b, gs.at[self.n, 2], gr.at[self.n, 2], far, c).start()
                return 0

            lax.fori_loop(0, 8, one, 0)

        def s4(self):
            self.recv(2, 8)
            m = self.many(16)
            send(m, m, gs.at[self.n, 3], gr.at[self.n, 3], me, other).start()

        def done(self):
            n = self.buf.at[pl.ds(0, 16 * self.rows), self.cols(other)]
            send(n, n, gs.at[self.n, 3], gr.at[self.n, 3], me, other).wait_recv()

        def drain(self):
            for stage, k in ((0, 3), (1, 4), (2, 8), (3, 16)):
                self.sent(stage, k)

    w_in = Piece(0, win_s, win, 48, 0, 1152)
    w_out = Piece(1, wout_s, wout, 48, 0, 384)
    w_exp = [Piece(2 + k, wexp_s, wexp, 48, 1536 * k, 768) for k in range(2)]
    w_con = [Piece(4 + k, wcon_s, wcon, 192, 256 * k, 128) for k in range(3)]
    SM = 7

    def small(stage, k, recv):
        d = send(vec.at[pl.ds(0, k)], vec.at[pl.ds(0, k)], gs.at[SM, stage], gr.at[SM, stage], me, other)
        d.wait_recv() if recv else d.wait_send()

    swap_tok = send(tokens, tokr, swap_sem.at[0, 0], swap_sem.at[0, 1], me, other)
    swap_cot = send(cot, cotr, swap_sem.at[1, 0], swap_sem.at[1, 1], me, other)
    own_tok = pltpu.make_async_copy(tokens, tok, ls.at[8])
    own_cot = pltpu.make_async_copy(cot, cotn, ls.at[9])
    own_vec = pltpu.make_async_copy(small_s, vec.at[me], ls.at[10])

    own_tok.start()
    own_vec.start()
    w_in.s1()
    for q in zs:
        send(small_s, vec.at[me], gs.at[SM, 0], gr.at[SM, 0], q, c).start()
    swap_tok.start()
    w_out.s1()
    for p in w_exp + w_con:
        p.s1()
    swap_cot.start()
    own_cot.start()

    row = seg[...].astype(F32)
    first_row = jnp.zeros((1, 1), F32)
    for d in range(DOCS):
        size = jnp.sum(jnp.where(row == d, 1.0, 0.0), axis=1, keepdims=True)
        before = jnp.sum(jnp.where(row < d, 1.0, 0.0), axis=1, keepdims=True)
        first_row = first_row + jnp.where(size == T, before, 0.0)
    keep_row = lax.broadcasted_iota(jnp.int32, (1, T), 1).astype(F32) >= first_row
    mine = seg[:, pl.ds(al(c * T, 128), T)].astype(F32)
    theirs = seg[:, pl.ds(al(other * T, 128), T)].astype(F32)
    seg_row = jnp.where(keep_row, mine, theirs)
    seg_col = jnp.broadcast_to(seg_row, (128, T)).T[:, :1]
    keep_col = lax.broadcasted_iota(jnp.int32, (T, 1), 0).astype(F32) >= first_row
    keep_col = jnp.where(keep_col, 1.0, 0.0)
    sc1[...] = jnp.concatenate([keep_col, seg_col], axis=1)

    def mask_rows(i, _):
        r = pl.ds(al(i * 128, 128), 128)
        bias[r, :] = jnp.where(sc1[r, 1:2] == seg_row, 0.0, -1e30)
        return 0

    lax.fori_loop(0, T // 128, mask_rows, 0)
    own_tok.wait()
    swap_tok.wait_recv()

    def start_rows(i, _):
        r = pl.ds(al(i * 128, 128), 128)
        t = jnp.where(sc1[r, 0:1] > 0.5, tok[r, :].astype(F32), tokr[r, :].astype(F32)) + te[...]
        n1[r, :] = t
        xl[r, :] = t.astype(BF)
        return 0

    lax.fori_loop(0, T // 128, start_rows, 0)

    w_in.s2()
    own_vec.wait()
    small(0, 3, True)

    def small2(k, _):
        b = vec.at[k * 4 + xy]
        send(b, b, gs.at[SM, 1], gr.at[SM, 1], near, c).start()
        return 0

    lax.fori_loop(0, 4, small2, 0)
    w_in.s3()
    small(1, 4, True)

    def small3(k, _):
        b = vec.at[(k // 2) * 4 + (1 - c) * 2 * y + c * x + lax.rem(k, 2) * (1 + c)]
        send(b, b, gs.at[SM, 2], gr.at[SM, 2], far, c).start()
        return 0

    lax.fori_loop(0, 8, small3, 0)
    w_out.s2()
    w_in.s4()
    small(2, 8, True)
    for o in range(16):
        fullv[:, o * 48 : (o + 1) * 48] = vec[o][:, :48].astype(F32)
        for k in range(4):
            fulle[:, o * 192 + k * 48 : o * 192 + (k + 1) * 48] = vec[o][k : k + 1, 64:112].astype(F32)
    w_in.done()

    for j in range(3):
        v = nn(xl[...], win[:, j * D : (j + 1) * D])
        if j == 0:
            v = (v + fullv[0:1, :]).astype(BF) * jnp.asarray(HD**-0.5, BF)
        elif j == 1:
            v = v.astype(BF)
        else:
            v = (v + fullv[1:2, :]).astype(BF)
        proj[:, j * D : (j + 1) * D] = v

    lane = lax.broadcasted_iota(jnp.int32, (1, 128), 1)
    halves = (lane < HD, lane >= HD)
    pairs = D // 128

    def keep(h, a):
        return pltpu.make_async_copy(pslot.at[a], spill.at[h * 2 + a], ps.at[a])

    tasks = [
        [w_out.s3, w_exp[0].s2],
        [w_out.s4, w_exp[0].s3],
        [w_exp[0].s4, w_exp[1].s2],
        [w_exp[1].s3, w_con[0].s2],
        [w_exp[1].s4, w_con[0].s3, w_con[1].s2],
        [w_con[0].s4, w_con[1].s3],
    ]

    def attend(h, _):
        cs = al(h * 128, 128)
        q2 = proj[:, pl.ds(cs, 128)]
        k2 = proj[:, pl.ds(D + cs, 128)]
        v2 = proj[:, pl.ds(2 * D + cs, 128)]
        outs = []
        for a in range(2):
            s = nt(jnp.where(halves[a], q2, jnp.zeros_like(q2)), k2) + bias[...]
            e = jnp.exp(s - jnp.max(s, axis=-1, keepdims=True))
            p = (e * (1.0 / jnp.sum(e, axis=-1, keepdims=True))).astype(BF)

            @pl.when(h > 0)
            def _():
                keep(h - 1, a).wait()

            pslot[a] = p
            keep(h, a).start()
            outs.append(nn(p, v2))
        heads[:, pl.ds(cs, 128)] = jnp.where(halves[0], outs[0], outs[1]).astype(BF)
        for k in range(pairs):

            @pl.when(h == k)
            def _():
                for t in tasks[k]:
                    t()

        return 0

    lax.fori_loop(0, pairs, attend, 0)
    w_out.done()

    def load(h, a):
        return pltpu.make_async_copy(spill.at[h * 2 + a], pslot.at[a], pd.at[a])

    for a in range(2):
        keep(pairs - 1, a).wait()
        load(0, a).start()

    def normalize(v):
        centred = v - jnp.mean(v, axis=-1, keepdims=True)
        scale = lax.rsqrt(jnp.mean(centred * centred, axis=-1, keepdims=True) + 1e-5)
        return centred * scale, scale

    def first_rows(i, _):
        r = pl.ds(al(i * 256, 256), 256)
        v = n1[r, :] + (nn(heads[r, :], wout[...]) + fullv[2:3, :])
        n, s = normalize(v)
        n1[r, :] = n
        sc1[r, 1:2] = s
        fl[r, :] = (n * fullv[3:4, :] + fullv[4:5, :]).astype(BF)
        return 0

    lax.fori_loop(0, T // 256, first_rows, 0)
    w_con[2].s2()
    w_exp[0].done()
    w_exp[1].done()
    w_con[1].s4()
    w_con[2].s3()

    def expand(i, _):
        cs = pl.ds(al(i * 512, 512), 512)
        u = nn(fl[...], wexp[:, cs]) + fulle[:, cs]
        cdf = 0.5 * (1.0 + lax.erf(u * math.sqrt(0.5)))
        hidden[:, cs] = (u * cdf).astype(BF)
        slope[:, cs] = (cdf + u * jnp.exp(-0.5 * u * u) * (1.0 / math.sqrt(2.0 * math.pi))).astype(BF)
        return 0

    lax.fori_loop(0, FF // 512, expand, 0)
    w_con[2].s4()
    for p in w_con:
        p.done()
    own_cot.wait()
    swap_cot.wait_recv()

    gv[...] = jnp.zeros_like(gv)

    def second_rows(i, _):
        r = pl.ds(al(i * 256, 256), 256)
        v = n1[r, :] * fullv[3:4, :] + fullv[4:5, :] + (nn(hidden[r, :], wcon[...]) + fullv[5:6, :])
        n, s = normalize(v)
        lonew[r, :] = (n * fullv[6:7, :] + fullv[7:8, :]).astype(BF)
        og = jnp.where(sc1[r, 0:1] > 0.5, cotn[r, :].astype(F32), cotr[r, :].astype(F32))
        gv[6:7, :] += jnp.sum(og * n, axis=0, keepdims=True)
        gv[7:8, :] += jnp.sum(og, axis=0, keepdims=True)
        w = og * fullv[6:7, :]
        g = s * (w - jnp.mean(w, axis=-1, keepdims=True) - n * jnp.mean(w * n, axis=-1, keepdims=True))
        sg[r, :] = g
        low = g.astype(BF)
        bg[r, :] = low
        gv[5:6, :] += jnp.sum(low.astype(F32), axis=0, keepdims=True)
        return 0

    lax.fori_loop(0, T // 256, second_rows, 0)
    swap_lo = send(lonew, lor, swap_sem.at[2, 0], swap_sem.at[2, 1], me, other)
    swap_lo.start()

    S = 384
    my_k = (1 - c) * x + c * y
    far_base = (1 - c) * (2 - 2 * y) + c * (1 - x)
    own_base = (1 - c) * 2 * y + c * x
    near_xy = xy + (1 - c) * (1 - 2 * x) + c * (2 - 4 * y)
    step_k = 1 + c

    def total(*refs):
        t = refs[0][...].astype(F32)
        for ref in refs[1:]:
            t = t + ref[...].astype(F32)
        return t

    class Red:
        def __init__(self, n, g, col, rows, recv, rcol, fsum, plane=None):
            self.n, self.g, self.col, self.rows, self.recv, self.rcol, self.fsum = n, g, col, rows, recv, rcol, fsum
            self.plane = plane

        def cols(self, core):
            return pl.ds(al(self.col + core * S, 128), S)

        def part(self, base, i, k=1, second=False):
            if self.plane is None:
                cs = pl.ds(self.rcol + (S if second else 0), S)
            else:
                cs = pl.ds(0, S)
                base = base + self.rcol
            return self.recv.at[pl.ds(al(base + i * self.rows, 16), k * self.rows), cs]

        def mine(self, o):
            base = 0 if self.plane is None else self.plane * 4
            return self.g.at[pl.ds(al((base + o) * self.rows, 16), self.rows), self.cols(c)]

        def planes(self):
            return 4 if self.plane is None else 1

        def rp(self, o, k=1):
            return self.part(0, o, k)

        def ra(self, i, k=1):
            return self.part(0 if self.plane is None else 768, i, k, True)

        def rb(self, i, k=1):
            return self.part(384 if self.plane is None else 1152, i, k, True)

        def rz(self, i, k=1):
            if self.plane is None:
                return self.part(576, i, k, True)
            return self.recv.at[pl.ds(al(5376 + i * self.rows, 16), k * self.rows), pl.ds(0, S)]

        def sem(self, stage):
            return rs.at[self.n, stage], rr.at[self.n, stage]

        def got(self, stage, ref):
            s, r = self.sem(stage)
            send(ref, ref, s, r, me, other).wait_recv()

        def gone(self, stage, ref):
            s, r = self.sem(stage)
            send(ref, ref, s, r, me, other).wait_send()

        def P(self):
            base = 0 if self.plane is None else self.plane * 4 * self.rows
            n = 4 * self.planes() * self.rows
            src = self.g.at[pl.ds(al(base, 16), n), self.cols(other)]
            s, r = self.sem(0)
            send(src, self.rp(0, 4 * self.planes()), s, r, me, other).start()

        def A(self):
            self.got(0, self.rp(0, 4 * self.planes()))
            s, r = self.sem(1)

            def one(i, _):
                o = (i // 2) * 4 + far_base + lax.rem(i, 2) * step_k
                b = self.mine(o)
                b[...] = total(b, self.rp(o)).astype(BF)
                send(b, self.ra(i), s, r, far, c).start()
                return 0

            lax.fori_loop(0, 2 * self.planes(), one, 0)

        def B(self):
            self.got(1, self.ra(0, 2 * self.planes()))
            s, r = self.sem(2)

            def one(i, _):
                o = i * 4 + near_xy
                b = self.mine(o)
                b[...] = total(b, self.rp(o), self.ra(i * 2 + 1 - my_k)).astype(BF)
                send(b, self.rb(i), s, r, near, c).start()
                return 0

            lax.fori_loop(0, self.planes(), one, 0)

        def Z(self, j=None):
            self.got(2, self.rb(0, self.planes()))
            if self.plane is None:
                for k in range(3):
                    s, r = self.sem(3)
                    p = lax.rem(z + k + 1, 4)
                    b = self.mine(p * 4 + xy)
                    b[...] = total(b, self.rp(p * 4 + xy), self.ra(p * 2 + my_k), self.rb(p)).astype(BF)
                    send(b, self.rz(k), s, r, zs[k], c).start()
            elif j > 0:
                s, r = rs.at[self.n, 3], rr.at[0, 3]
                b = self.mine(xy)
                b[...] = total(b, self.rp(xy), self.ra(my_k), self.rb(0)).astype(BF)
                send(b, self.rz(j - 1), s, r, zs[j - 1], c).start()

        def F(self):
            if self.plane is None:
                self.got(3, self.rz(0, 3))
                t = total(self.mine(z * 4 + xy), self.rp(z * 4 + xy), self.ra(z * 2 + my_k), self.rb(z),
                          self.rz(0), self.rz(1), self.rz(2))
            else:
                ref = self.rz(0, 3)
                send(ref, ref, rs.at[0, 3], rr.at[0, 3], me, other).wait_recv()
                t = total(self.mine(xy), self.rp(xy), self.ra(my_k), self.rb(0), self.rz(0), self.rz(1), self.rz(2))
            s, r = self.sem(4)
            if self.n >= 9:
                for k in range(3):
                    b = self.fsum.at[:, pl.ds(al(k * D + (self.n - 9) * 256 + c * 128, 128), 128)]
                    b[...] = t[:, k * 128 : (k + 1) * 128]
                    send(b, b, s, r, me, other).start()
            else:
                b = self.fsum.at[:, self.cols(c)]
                b[...] = t
                send(b, b, s, r, me, other).start()

        def end(self):
            p = self.planes()
            self.gone(0, self.rp(0, 4 * p))
            self.gone(1, self.ra(0, 2 * p))
            self.gone(2, self.rb(0, p))
            if self.plane is None:
                self.gone(3, self.rz(0, 3))
            elif self.n > 0:
                self.gone(3, self.rz(0, 1))
            if self.plane is None or self.n == 0:
                half = self.fsum.at[:, pl.ds(0, S)]
                self.gone(4, half)
                self.got(4, half)

    con = {j: Red(j, wcon, 0, 192, con_r, j * 1344, fcon, plane=lax.rem(z + j, 4)) for j in range(4)}
    exp = [Red(4 + k, wexp, k * 768, 48, hidden, k * 768, fexp) for k in range(4)]
    out = Red(8, wout, 0, 48, slope, 2304, fout)
    ins = [Red(9 + k, gin, k * 768, 48, slope, k * 768, fin) for k in range(3)]

    def expand_back(i, _):
        cs = pl.ds(al(i * 512, 512), 512)
        g = (nt(bg[...], wcon[cs, :]) * slope[:, cs].astype(F32)).astype(BF)
        slope[:, cs] = g
        ge[:, cs] = jnp.sum(g.astype(F32), axis=0, keepdims=True)
        return 0

    lax.fori_loop(0, FF // 512, expand_back, 0)
    for p in w_con:
        p.drain()

    def grad_con(i, _):
        p = al(lax.rem(z + i + 1, 4) * 768, 768)
        wcon[pl.ds(p, 768), :] = tn(hidden[:, pl.ds(p, 768)], bg[...]).astype(BF)
        for k, t in enumerate([
            [con[1].P],
            [con[2].P, con[1].A],
            [con[3].P, con[2].A],
            [con[0].P, con[3].A],
        ]):

            @pl.when(i == k)
            def _():
                for u in t:
                    u()

        return 0

    lax.fori_loop(0, 4, grad_con, 0)

    def first_back(i, _):
        r = pl.ds(al(i * 256, 256), 256)
        g = sg[r, :] + nt(slope[r, :], wexp[...])
        n = n1[r, :]
        gv[3:4, :] += jnp.sum(g * n, axis=0, keepdims=True)
        gv[4:5, :] += jnp.sum(g, axis=0, keepdims=True)
        w = g * fullv[3:4, :]
        g = sc1[r, 1:2] * (w - jnp.mean(w, axis=-1, keepdims=True) - n * jnp.mean(w * n, axis=-1, keepdims=True))
        sg[r, :] = g
        low = g.astype(BF)
        bg[r, :] = low
        gv[2:3, :] += jnp.sum(low.astype(F32), axis=0, keepdims=True)
        for k, t in enumerate([[con[0].A, con[1].B], [con[2].B], [con[3].B]]):

            @pl.when(i == k)
            def _():
                for u in t:
                    u()

        return 0

    lax.fori_loop(0, T // 256, first_back, 0)
    for p in w_exp:
        p.drain()
    con[0].B()

    def grad_exp(i, _):
        cs = pl.ds(al(i * 768, 768), 768)
        wexp[:, cs] = tn(fl[...], slope[:, cs]).astype(BF)
        for k, t in enumerate([
            [exp[0].P, lambda: con[1].Z(1)],
            [exp[1].P, exp[0].A, lambda: con[2].Z(2)],
            [exp[2].P, exp[1].A, lambda: con[3].Z(3)],
            [exp[3].P, exp[2].A, lambda: con[0].Z(0), exp[0].B],
        ]):

            @pl.when(i == k)
            def _():
                for u in t:
                    u()

        return 0

    lax.fori_loop(0, 4, grad_exp, 0)
    hg = cotr
    hg[...] = nt(bg[...], wout[...]).astype(BF)
    exp[3].A()
    exp[1].B()
    w_out.drain()
    wout[...] = tn(heads[...], bg[...]).astype(BF)
    out.P()
    con[0].F()

    tasks = [
        [exp[2].B, exp[0].Z],
        [exp[3].B, exp[1].Z],
        [out.A, exp[2].Z, exp[0].F],
        [exp[3].Z, ins[0].A, exp[1].F],
        [out.B, exp[2].F, exp[3].F],
        [ins[0].B, out.Z, ins[1].A],
    ]

    def attend_back(h, _):
        cs = al(h * 128, 128)
        q2 = proj[:, pl.ds(cs, 128)]
        k2 = proj[:, pl.ds(D + cs, 128)]
        v2 = proj[:, pl.ds(2 * D + cs, 128)]
        g2 = hg[:, pl.ds(cs, 128)]
        prod = g2.astype(F32) * heads[:, pl.ds(cs, 128)].astype(F32)
        qt = q2.astype(F32).T.astype(BF)
        gt = g2.astype(F32).T.astype(BF)
        dq, dk, dv = [], [], []
        for a in range(2):
            load(h, a).wait()
            rowdot = jnp.sum(jnp.where(halves[a], prod, 0.0), axis=-1, keepdims=True)
            p = pslot[a]
            dp = nt(jnp.where(halves[a], g2, jnp.zeros_like(g2)), v2)
            ds = (p.astype(F32) * (dp - rowdot)).astype(BF)
            dq.append(nn(ds, k2))
            dk.append(nn(qt[a * HD : (a + 1) * HD], ds))
            dv.append(nn(gt[a * HD : (a + 1) * HD], p))

            @pl.when(h + 1 < pairs)
            def _():
                load(h + 1, a).start()

        dq = (jnp.where(halves[0], dq[0], dq[1]) * HD**-0.5).astype(BF)
        dk = jnp.concatenate(dk, axis=0).T.astype(BF)
        dv = jnp.concatenate(dv, axis=0).T.astype(BF)
        proj[:, pl.ds(cs, 128)] = dq
        proj[:, pl.ds(D + cs, 128)] = dk
        proj[:, pl.ds(2 * D + cs, 128)] = dv
        gv[0:1, pl.ds(cs, 128)] = jnp.sum(dq.astype(F32), axis=0, keepdims=True)
        gv[1:2, pl.ds(cs, 128)] = jnp.sum(dv.astype(F32), axis=0, keepdims=True)

        @pl.when(lax.rem(h, 2) == 1)
        def _():
            g = al((h // 2) * 256, 256)
            cols = jnp.concatenate(
                [proj[:, pl.ds(al(k * D + g + e * 128, 128), 128)] for e in range(2) for k in range(3)], axis=1
            )
            gin[:, pl.ds(al((h // 2) * 768, 768), 768)] = tn(xl[...], cols).astype(BF)

        for k in range(pairs):

            @pl.when(h == k)
            def _():
                if k % 2 == 1:
                    ins[k // 2].P()
                for t in tasks[k]:
                    t()

        return 0

    lax.fori_loop(0, pairs, attend_back, 0)

    vout[...] = jnp.zeros_like(vout)
    for o in range(16):
        vout[o, :, 0:48] = gv[0:8, o * 48 : (o + 1) * 48]
        for k in range(4):
            vout[o, k : k + 1, 64:112] = ge[:, o * 192 + k * 48 : o * 192 + (k + 1) * 48]
    VN = 12

    def vsend(stage, src, dst, dp, seq):
        return send(src, dst, rs.at[VN, stage], rr.at[VN, stage], dp, seq)

    vsend(0, vout, vr.at[pl.ds(0, 16)], me, other).start()
    ins[2].A()

    def input_rows(i, _):
        r = pl.ds(al(i * 256, 256), 256)
        sg[r, :] = sg[r, :] + nt(proj[r, :], win[...])
        for k, t in enumerate([[ins[1].B], [ins[0].Z], [ins[2].B]]):

            @pl.when(i == k)
            def _():
                for u in t:
                    u()

        return 0

    lax.fori_loop(0, T // 256, input_rows, 0)
    swap_ig = send(sg, n1, swap_sem.at[3, 0], swap_sem.at[3, 1], me, other)
    swap_ig.start()
    vsend(0, vout, vr.at[pl.ds(0, 16)], me, other).wait_recv()
    vsum[...] = vout[...] + vr[pl.ds(0, 16)]
    for i in range(8):
        b = vsum.at[(i // 2) * 4 + 2 - 2 * y + i % 2]
        vsend(1, b, vr.at[16 + i], flip_y, c).start()
    ins[1].Z()
    vsend(1, vr.at[pl.ds(16, 8)], vr.at[pl.ds(16, 8)], me, other).wait_recv()
    for i in range(8):
        o = (i // 2) * 4 + 2 * y + i % 2
        vsum[o] = vsum[o] + vr[16 + i]
    for i in range(4):
        b = vsum.at[i * 4 + 2 * y + 1 - x]
        vsend(2, b, vr.at[24 + i], flip_x, c).start()
    ins[2].Z()
    vsend(2, vr.at[pl.ds(24, 4)], vr.at[pl.ds(24, 4)], me, other).wait_recv()
    for i in range(4):
        vsum[i * 4 + xy] = vsum[i * 4 + xy] + vr[24 + i]
    for k in range(3):
        b = vsum.at[lax.rem(z + k + 1, 4) * 4 + xy]
        vsend(3, b, vr.at[28 + k], zs[k], c).start()
    out.F()
    for p in ins:
        p.F()

    swap_lo.wait()

    def out_rows(i, _):
        r = pl.ds(al(i * 128, 128), 128)
        lonew[r, :] = jnp.where(sc1[r, 0:1] > 0.5, lonew[r, :].astype(F32), lor[r, :].astype(F32)).astype(BF)
        return 0

    lax.fori_loop(0, T // 128, out_rows, 0)
    lo_done = pltpu.make_async_copy(lonew, lo_o, ls.at[11])
    lo_done.start()
    swap_ig.wait()

    def grad_rows(i, _):
        r = pl.ds(al(i * 128, 128), 128)
        sg[r, :] = jnp.where(sc1[r, 0:1] > 0.5, sg[r, :], n1[r, :])
        return 0

    lax.fori_loop(0, T // 128, grad_rows, 0)
    outs = [lo_done, pltpu.make_async_copy(sg, ig_o, ls.at[12])]
    outs[1].start()
    vsend(3, vr.at[pl.ds(28, 3)], vr.at[pl.ds(28, 3)], me, other).wait_recv()
    vfin = vr.at[31]
    vfin[...] = vsum[z * 4 + xy] + vr[28] + vr[29] + vr[30]
    outs.append(pltpu.make_async_copy(vfin, gvec_o, ls.at[13]))
    outs[2].start()
    swap_tok.wait_send()
    swap_cot.wait_send()
    w_in.drain()
    for stage, k in ((0, 3), (1, 4), (2, 8)):
        small(stage, k, False)
        vsend(stage + 1, vr.at[pl.ds(0, (8, 4, 3)[stage])], vr.at[pl.ds(0, (8, 4, 3)[stage])], me, other).wait_send()
    vsend(0, vout, vr.at[pl.ds(0, 16)], me, other).wait_send()
    for p in list(con.values()) + exp + [out] + ins:
        p.end()
    for k, (v, o) in enumerate([(fin, gin_o), (fout, gout_o), (fexp, gexp_o), (fcon, gcon_o)]):
        outs.append(pltpu.make_async_copy(v, o, ls.at[14 + k]))
        outs[-1].start()
    for o in outs:
        o.wait()


def fused_layer(tokens, time_embed, segments, iw, ow, ew, cw, small, cot):
    T, D = tokens.shape
    FF = ew.shape[1]
    sh = jax.ShapeDtypeStruct
    anyspec = pl.BlockSpec(memory_space=pl.ANY)
    vspec = pl.BlockSpec(memory_space=VM)
    scratch = [
        VM((D, 3 * D), BF), VM((D, D), BF), VM((D, FF), BF), VM((FF, D), BF),
        VM((T, D), BF), VM((T, D), BF), VM((T, D), BF), VM((T, D), BF),
        VM((16, 16, 128), BF), VM((16, D), F32), VM((1, FF), F32),
        VM((T, 3 * D), BF), VM((T, D), BF), VM((T, D), F32), VM((T, T), F32),
        VM((T, 2), F32), VM((T, D), BF), VM((T, D), BF), VM((T, FF), BF), VM((T, FF), BF),
        VM((2, T, T), BF), VM((T, D), BF), VM((T, D), BF), VM((T, D), F32), VM((T, D), BF),
        VM((D, 3 * D), BF), VM((5952, 384), BF), VM((8, D), F32), VM((1, FF), F32),
        VM((16, 8, 128), F32), VM((16, 8, 128), F32), VM((32, 8, 128), F32),
        VM(iw.shape, F32), VM(ow.shape, F32), VM(ew.shape, F32), VM(cw.shape, F32),
        DMA((4, 2)), DMA((18,)), DMA((8, 4)), DMA((8, 4)), DMA((2,)), DMA((13, 5)), DMA((13, 5)), DMA((2,)),
    ]
    return pl.pallas_call(
        fused_kernel,
        out_shape=(
            sh((T, D), BF), sh((T, D), F32), sh(iw.shape, F32), sh(ow.shape, F32), sh(ew.shape, F32),
            sh(cw.shape, F32), sh((8, 128), F32), sh((D // HD, T, T), BF),
        ),
        in_specs=[anyspec, anyspec, vspec, vspec, anyspec, anyspec, anyspec, anyspec, anyspec],
        out_specs=(anyspec,) * 8,
        scratch_shapes=scratch,
        compiler_params=pltpu.CompilerParams(
            collective_id=0, has_side_effects=True, vmem_limit_bytes=67043328
        ),
    )(tokens, cot, time_embed, segments, iw, ow, ew, cw, small)


epsilon = 1e-05
masked_score = -1e30


def matmul(left, right):
    return jnp.dot(left, right, preferred_element_type=jnp.float32)


def product_tn(left, right):
    return lax.dot_general(
        left, right, (((0,), (0,)), ((), ())), preferred_element_type=jnp.float32
    )


def product_nt(left, right):
    return lax.dot_general(
        left, right, (((1,), (1,)), ((), ())), preferred_element_type=jnp.float32
    )


def normalize(values):
    mean = jnp.mean(values, axis=-1, keepdims=True)
    centred = values - mean
    scale = lax.rsqrt(jnp.mean(centred * centred, axis=-1, keepdims=True) + epsilon)
    return (centred * scale, scale)


def norm_back(grad, normed, scale, gain):
    scaled = grad * gain
    return scale * (
        scaled
        - jnp.mean(scaled, axis=-1, keepdims=True)
        - normed * jnp.mean(scaled * normed, axis=-1, keepdims=True)
    )


def gelu_value(values):
    return 0.5 * values * (1.0 + lax.erf(values * math.sqrt(0.5)))


def gelu_slope(values):
    return 0.5 * (1.0 + lax.erf(values * math.sqrt(0.5))) + values * jnp.exp(
        -0.5 * values * values
    ) / math.sqrt(2.0 * math.pi)


def attend_forward(item):
    query, key, value, segment_row = item
    length, depth = query.shape
    block = min(512, length)
    blocks = length // block
    scale = depth ** (-0.5)

    def one_block(part):
        query_block, segment_block = part
        scores = product_nt(query_block, key) * scale
        scores = jnp.where(segment_block[:, None] == segment_row[None, :], scores, masked_score)
        top = jnp.max(scores, axis=-1, keepdims=True)
        expo = jnp.exp(scores - top)
        total = jnp.sum(expo, axis=-1, keepdims=True)
        probs_low = (expo / total).astype(jnp.bfloat16)
        return (matmul(probs_low, value).astype(jnp.bfloat16), (top + jnp.log(total))[:, 0])

    outputs, logsum = lax.map(
        one_block, (query.reshape(blocks, block, depth), segment_row.reshape(blocks, block))
    )
    return (outputs.reshape(length, depth), logsum.reshape(length))


def attend_backward(item):
    query, key, value, segment_row, logsum, out_grad = item
    length, depth = query.shape
    block = min(512, length)
    blocks = length // block
    scale = depth ** (-0.5)

    def one_block(carry, part):
        key_grad, value_grad = carry
        query_block, segment_block, logsum_block, grad_block = part
        scores = product_nt(query_block, key) * scale
        scores = jnp.where(segment_block[:, None] == segment_row[None, :], scores, masked_score)
        probs = jnp.exp(scores - logsum_block[:, None])
        probs_low = probs.astype(jnp.bfloat16)
        prob_grad = product_nt(grad_block, value)
        row_total = jnp.sum(probs * prob_grad, axis=-1, keepdims=True)
        score_grad = (probs * (prob_grad - row_total)).astype(jnp.bfloat16)
        query_grad = matmul(score_grad, key) * scale
        key_grad = key_grad + product_tn(score_grad, query_block) * scale
        value_grad = value_grad + product_tn(probs_low, grad_block)
        return ((key_grad, value_grad), query_grad.astype(jnp.bfloat16))

    zeros = jnp.zeros((length, depth), jnp.float32)
    parts = (
        query.reshape(blocks, block, depth),
        segment_row.reshape(blocks, block),
        logsum.reshape(blocks, block),
        out_grad.reshape(blocks, block, depth),
    )
    (key_grad, value_grad), query_grad = lax.scan(one_block, (zeros, zeros), parts)
    return (
        query_grad.reshape(length, depth),
        key_grad.astype(jnp.bfloat16),
        value_grad.astype(jnp.bfloat16),
    )


def plain_body(
    tokens,
    time_embed,
    segments,
    input_weight,
    query_bias,
    value_bias,
    output_weight,
    output_bias,
    first_gain,
    first_shift,
    expand_weight,
    expand_bias,
    contract_weight,
    contract_bias,
    second_gain,
    second_shift,
    cotangent,
):
    pairs = lax.axis_size("seq")
    seqs, half, width = tokens.shape
    length = half * pairs
    rows = seqs * half
    group = width // pairs
    heads_here = group // HD
    start = (tokens.astype(jnp.float32) + time_embed[:, None, :]).reshape(rows, width)
    start_low = start.astype(jnp.bfloat16)
    attention_set = (
        lax.all_gather(input_weight, "dp", axis=0, tiled=True),
        lax.all_gather(output_weight, "dp", axis=0, tiled=True),
        lax.all_gather(query_bias, "dp", axis=0, tiled=True),
        lax.all_gather(value_bias, "dp", axis=0, tiled=True),
        lax.all_gather(output_bias, "dp", axis=0, tiled=True),
        lax.all_gather(first_gain, "dp", axis=0, tiled=True),
        lax.all_gather(first_shift, "dp", axis=0, tiled=True),
    )
    (
        full_input,
        full_output,
        full_query_bias,
        full_value_bias,
        full_output_bias,
        full_first_gain,
        full_first_shift,
    ) = attention_set
    bias_row = jnp.concatenate(
        [
            full_query_bias.astype(jnp.float32),
            jnp.zeros((width,), jnp.float32),
            full_value_bias.astype(jnp.float32),
        ]
    )
    projected_low = (matmul(start_low, full_input) + bias_row).astype(jnp.bfloat16)
    regrouped = lax.all_to_all(
        projected_low.reshape(seqs, half, 3, pairs, group),
        "seq",
        split_axis=3,
        concat_axis=1,
        tiled=True,
    )
    split = regrouped.reshape(seqs, length, 3, heads_here, HD).transpose(2, 0, 3, 1, 4)
    split = split.reshape(3, seqs * heads_here, length, HD)
    query_heads, key_heads, value_heads = (split[0], split[1], split[2])
    segment_heads = jnp.repeat(segments, heads_here, axis=0)
    heads_out, logsum = lax.map(
        attend_forward, (query_heads, key_heads, value_heads, segment_heads)
    )
    heads_tokens = (
        heads_out.reshape(seqs, heads_here, length, HD)
        .transpose(0, 2, 1, 3)
        .reshape(seqs, length, 1, group)
    )
    heads_low = lax.all_to_all(
        heads_tokens, "seq", split_axis=1, concat_axis=2, tiled=True
    ).reshape(rows, width)
    attention = matmul(heads_low, full_output) + full_output_bias.astype(jnp.float32)
    normed_one, scale_one = normalize(start + attention)
    gain_one = full_first_gain.astype(jnp.float32)
    first = normed_one * gain_one + full_first_shift.astype(jnp.float32)
    first_low = first.astype(jnp.bfloat16)
    network_set = (
        lax.all_gather(expand_weight, "dp", axis=0, tiled=True),
        lax.all_gather(contract_weight, "dp", axis=0, tiled=True),
        lax.all_gather(expand_bias, "dp", axis=0, tiled=True),
        lax.all_gather(contract_bias, "dp", axis=0, tiled=True),
        lax.all_gather(second_gain, "dp", axis=0, tiled=True),
        lax.all_gather(second_shift, "dp", axis=0, tiled=True),
    )
    (
        full_expand,
        full_contract,
        full_expand_bias,
        full_contract_bias,
        full_second_gain,
        full_second_shift,
    ) = network_set
    expand = matmul(first_low, full_expand) + full_expand_bias.astype(jnp.float32)
    hidden = gelu_value(expand).astype(jnp.bfloat16)
    second_sum = first + matmul(hidden, full_contract) + full_contract_bias.astype(jnp.float32)
    normed_two, scale_two = normalize(second_sum)
    gain_two = full_second_gain.astype(jnp.float32)
    layer_output = (normed_two * gain_two + full_second_shift.astype(jnp.float32)).astype(
        jnp.bfloat16
    )
    network_set = (
        lax.all_gather(expand_weight, "dp", axis=0, tiled=True),
        lax.all_gather(contract_weight, "dp", axis=0, tiled=True),
        lax.all_gather(expand_bias, "dp", axis=0, tiled=True),
        lax.all_gather(contract_bias, "dp", axis=0, tiled=True),
        lax.all_gather(second_gain, "dp", axis=0, tiled=True),
        lax.all_gather(second_shift, "dp", axis=0, tiled=True),
    )
    full_expand, full_contract = (network_set[0], network_set[1])
    out_grad = cotangent.astype(jnp.float32).reshape(rows, width)
    grad_second_gain = jnp.sum(out_grad * normed_two, axis=0)
    grad_second_shift = jnp.sum(out_grad, axis=0)
    second_grad = norm_back(out_grad, normed_two, scale_two, gain_two)
    branch_grad = second_grad.astype(jnp.bfloat16)
    grad_contract_bias = jnp.sum(branch_grad.astype(jnp.float32), axis=0)
    grad_contract_weight = product_tn(hidden, branch_grad)
    expand_grad = (product_nt(branch_grad, full_contract) * gelu_slope(expand)).astype(jnp.bfloat16)
    grad_expand_bias = jnp.sum(expand_grad.astype(jnp.float32), axis=0)
    grad_expand_weight = product_tn(first_low, expand_grad)
    first_grad = second_grad + product_nt(expand_grad, full_expand)
    grad_first_gain = jnp.sum(first_grad * normed_one, axis=0)
    grad_first_shift = jnp.sum(first_grad, axis=0)
    start_grad = norm_back(first_grad, normed_one, scale_one, gain_one)
    attention_set = (
        lax.all_gather(input_weight, "dp", axis=0, tiled=True),
        lax.all_gather(output_weight, "dp", axis=0, tiled=True),
        lax.all_gather(query_bias, "dp", axis=0, tiled=True),
        lax.all_gather(value_bias, "dp", axis=0, tiled=True),
        lax.all_gather(output_bias, "dp", axis=0, tiled=True),
        lax.all_gather(first_gain, "dp", axis=0, tiled=True),
        lax.all_gather(first_shift, "dp", axis=0, tiled=True),
    )
    full_input, full_output = (attention_set[0], attention_set[1])
    attention_grad = start_grad.astype(jnp.bfloat16)
    grad_output_bias = jnp.sum(attention_grad.astype(jnp.float32), axis=0)
    grad_output_weight = product_tn(heads_low, attention_grad)
    heads_grad = product_nt(attention_grad, full_output).astype(jnp.bfloat16)
    grad_heads = lax.all_to_all(
        heads_grad.reshape(seqs, half, pairs, group), "seq", split_axis=2, concat_axis=1, tiled=True
    )
    grad_heads = (
        grad_heads.reshape(seqs, length, heads_here, HD)
        .transpose(0, 2, 1, 3)
        .reshape(seqs * heads_here, length, HD)
    )
    query_grad, key_grad, value_grad = lax.map(
        attend_backward, (query_heads, key_heads, value_heads, segment_heads, logsum, grad_heads)
    )
    stacked = jnp.stack([query_grad, key_grad, value_grad]).reshape(3, seqs, heads_here, length, HD)
    stacked = stacked.transpose(1, 3, 0, 2, 4).reshape(seqs, length, 3, 1, group)
    projected_grad = lax.all_to_all(
        stacked, "seq", split_axis=1, concat_axis=3, tiled=True
    ).reshape(rows, 3 * width)
    grad_query_bias = jnp.sum(projected_grad[:, :width].astype(jnp.float32), axis=0)
    grad_value_bias = jnp.sum(projected_grad[:, 2 * width :].astype(jnp.float32), axis=0)
    grad_input_weight = product_tn(start_low, projected_grad)
    input_grad = (start_grad + product_nt(projected_grad, full_input)).reshape(seqs, half, width)
    grads = (
        grad_input_weight,
        grad_query_bias,
        grad_value_bias,
        grad_output_weight,
        grad_output_bias,
        grad_first_gain,
        grad_first_shift,
        grad_expand_weight,
        grad_expand_bias,
        grad_contract_weight,
        grad_contract_bias,
        grad_second_gain,
        grad_second_shift,
    )
    owned = (
        lax.psum_scatter(grads[0], "dp", scatter_dimension=0, tiled=True),
        lax.psum_scatter(grads[1], "dp", scatter_dimension=0, tiled=True),
        lax.psum_scatter(grads[2], "dp", scatter_dimension=0, tiled=True),
        lax.psum_scatter(grads[3], "dp", scatter_dimension=0, tiled=True),
        lax.psum_scatter(grads[4], "dp", scatter_dimension=0, tiled=True),
        lax.psum_scatter(grads[5], "dp", scatter_dimension=0, tiled=True),
        lax.psum_scatter(grads[6], "dp", scatter_dimension=0, tiled=True),
        lax.psum_scatter(grads[7], "dp", scatter_dimension=0, tiled=True),
        lax.psum_scatter(grads[8], "dp", scatter_dimension=0, tiled=True),
        lax.psum_scatter(grads[9], "dp", scatter_dimension=0, tiled=True),
        lax.psum_scatter(grads[10], "dp", scatter_dimension=0, tiled=True),
        lax.psum_scatter(grads[11], "dp", scatter_dimension=0, tiled=True),
        lax.psum_scatter(grads[12], "dp", scatter_dimension=0, tiled=True),
    )
    summed = (
        lax.psum(owned[0].astype(jnp.bfloat16), "seq").astype(jnp.float32),
        lax.psum(owned[1].astype(jnp.bfloat16), "seq").astype(jnp.float32),
        lax.psum(owned[2].astype(jnp.bfloat16), "seq").astype(jnp.float32),
        lax.psum(owned[3].astype(jnp.bfloat16), "seq").astype(jnp.float32),
        lax.psum(owned[4].astype(jnp.bfloat16), "seq").astype(jnp.float32),
        lax.psum(owned[5].astype(jnp.bfloat16), "seq").astype(jnp.float32),
        lax.psum(owned[6].astype(jnp.bfloat16), "seq").astype(jnp.float32),
        lax.psum(owned[7].astype(jnp.bfloat16), "seq").astype(jnp.float32),
        lax.psum(owned[8].astype(jnp.bfloat16), "seq").astype(jnp.float32),
        lax.psum(owned[9].astype(jnp.bfloat16), "seq").astype(jnp.float32),
        lax.psum(owned[10].astype(jnp.bfloat16), "seq").astype(jnp.float32),
        lax.psum(owned[11].astype(jnp.bfloat16), "seq").astype(jnp.float32),
        lax.psum(owned[12].astype(jnp.bfloat16), "seq").astype(jnp.float32),
    )
    return (layer_output.reshape(seqs, half, width), input_grad) + tuple(summed)


def fused_body(
    tokens, time_embed, segments, input_weight, query_bias, value_bias, output_weight, output_bias, first_gain,
    first_shift, expand_weight, expand_bias, contract_weight, contract_bias, second_gain, second_shift, cotangent,
):
    vectors = [
        query_bias, value_bias, output_bias, first_gain, first_shift, contract_bias, second_gain, second_shift,
    ]
    own = query_bias.shape[0]
    small = jnp.pad(jnp.stack(vectors), ((0, 8), (0, 64 - own)))
    wide = jnp.pad(expand_bias.reshape(4, own), ((0, 12), (0, 64 - own)))
    small = jnp.concatenate([small, wide], axis=1)
    layer_output, input_grad, g_in, g_out, g_exp, g_con, vec = fused_layer(
        tokens[0], time_embed, segments, input_weight, output_weight, expand_weight, contract_weight, small,
        cotangent[0],
    )[:7]
    row = [vec[k, :own] for k in range(8)]
    g_eb = vec[0:4, 64 : 64 + own].reshape(4 * own)
    return (
        layer_output[None], input_grad[None], g_in, row[0], row[1], g_out, row[2], row[3], row[4],
        g_exp, g_eb, g_con, row[5], row[6], row[7],
    )


def body(*args):
    if lax.axis_size("dp") == 16 and lax.axis_size("seq") == 2:
        return fused_body(*args)
    return plain_body(*args)


def solution(mesh):
    return jax.shard_map(
        body,
        mesh=mesh,
        in_specs=(
            P("dp", "seq", None),
            P("dp", None),
            P("dp", None),
            P("dp", None),
            P("dp"),
            P("dp"),
            P("dp", None),
            P("dp"),
            P("dp"),
            P("dp"),
            P("dp", None),
            P("dp"),
            P("dp", None),
            P("dp"),
            P("dp"),
            P("dp"),
            P("dp", "seq", None),
        ),
        out_specs=(
            P("dp", "seq", None),
            P("dp", "seq", None),
            P("dp", None),
            P("dp"),
            P("dp"),
            P("dp", None),
            P("dp"),
            P("dp"),
            P("dp"),
            P("dp", None),
            P("dp"),
            P("dp", None),
            P("dp"),
            P("dp"),
            P("dp"),
        ),
        check_vma=False,
    )
```

```python
import functools
import math

import jax
import jax.numpy as jnp
from jax import lax
from jax.experimental import pallas as pl
from jax.experimental.pallas import tpu as pltpu
from jax.sharding import PartitionSpec as P

HD = 64
DOCS = 4
BF = jnp.bfloat16
F32 = jnp.float32
MESH = pl.DeviceIdType.MESH
VM = pltpu.VMEM
DMA = pltpu.SemaphoreType.DMA


def nn(a, b):
    return jnp.dot(a, b, preferred_element_type=F32)


def nt(a, b):
    return lax.dot_general(a, b, (((1,), (1,)), ((), ())), preferred_element_type=F32)


def tn(a, b):
    return lax.dot_general(a, b, (((0,), (0,)), ((), ())), preferred_element_type=F32)


def fused_kernel(
    tokens, cot, te, seg, win_s, wout_s, wexp_s, wcon_s, small_s,
    lo_o, ig_o, gin_o, gout_o, gexp_o, gcon_o, gvec_o, spill,
    wide, wcon, tok, tokr, cotn, cotr, vec, fullv, fulle, fullp, proj, xl, n1, sg,
    sc1, heads, fl, hidden, slope, pslot, bg,
    gin, gcon, con_r, gv, ge, vout, vsum, vr, fin, fout, fexp, fcon,
    swap_sem, ls, gs, gr, ps, rs, rr, pd,
):
    T, D = tok.shape
    FF = wcon.shape[0]
    IN, OUT, EXP = 0, 3 * D, 4 * D
    bias, lonew, lor = sg, tok, tokr
    me = lax.axis_index("dp")
    c = lax.axis_index("seq")
    x = lax.rem(me, 2)
    y = lax.rem(me // 2, 2)
    xy = lax.rem(me, 4)
    z = me // 4
    flip_x = me + 1 - 2 * x
    flip_y = me + 2 - 4 * y
    near = (1 - c) * flip_x + c * flip_y
    far = (1 - c) * flip_y + c * flip_x
    other = 1 - c
    zs = [lax.rem(z + k, 4) * 4 + xy for k in (1, 2, 3)]

    def send(src, dst, s, r, dp, seq):
        return pltpu.make_async_remote_copy(
            src_ref=src, dst_ref=dst, send_sem=s, recv_sem=r,
            device_id={"dp": dp, "seq": seq}, device_id_type=MESH,
        )

    barrier = pltpu.get_barrier_semaphore()
    for dp, seq in [(me, other), (near, c), (far, c)] + [(q, c) for q in zs]:
        pl.semaphore_signal(
            barrier, inc=1, device_id={"dp": dp, "seq": seq}, device_id_type=MESH
        )
    pl.semaphore_wait(barrier, 6)

    def al(v, m):
        return pl.multiple_of(v, m)

    class Piece:
        def __init__(self, n, buf, rows, col, half, shards):
            self.n, self.buf, self.rows, self.col, self.half, self.shards = n, buf, rows, col, half, shards

        def cols(self, core):
            return pl.ds(al(self.col + core * self.half, 128), self.half)

        def block(self, o):
            return self.buf.at[pl.ds(al(o * self.rows, 16), self.rows), self.cols(c)]

        def region(self, k, core=c):
            return self.buf.at[pl.ds(0, k * self.rows), self.cols(core)]

        def push(self, src, dst, stage, k, dp):
            send(src, dst, gs.at[self.n, stage], gr.at[self.n, stage * 4 + k], dp, c).start()

        def got(self, stage, k, blocks):
            m = self.region(blocks)
            send(m, m, gs.at[self.n, stage], gr.at[self.n, stage * 4 + k], me, other).wait_recv()

        def own(self):
            base = pl.ds(al(me * self.rows, 16), self.rows)
            for i, (ref, first, width) in enumerate(self.shards):
                yield (
                    ref.at[:, pl.ds(al(first + c * width, 128), width)],
                    self.buf.at[base, pl.ds(al(self.col + c * self.half + i * width, 128), width)],
                )

        def s1(self, early):
            for k in range(3):
                for a, b in self.own():
                    self.push(a, b, 0, k + 1, zs[k])
            if early:
                for a, b in self.own():
                    self.push(a, b, 1, 0, near)
                    self.push(a, b, 2, 0, far)
            for a, b in self.own():
                pltpu.make_async_copy(a, b, ls.at[self.n]).start()

        def s2(self, early):
            m = self.block(me)
            pltpu.make_async_copy(m, m, ls.at[self.n]).wait()
            for k in range(1 if early else 0, 4):
                if k > 0:
                    self.got(0, k, 1)
                b = self.block(lax.rem(z + 4 - k, 4) * 4 + xy)
                self.push(b, b, 1, k, near)
                self.push(b, b, 2, k, far)

        def s3(self):
            for k in range(4):
                self.got(1, k, 1)
                b = self.block(lax.rem(z + 4 - k, 4) * 4 + near_xy)
                self.push(b, b, 2, k, far)

        def s4(self):
            for k in range(4):
                self.got(2, k, 2)
                p = self.buf.at[pl.ds(al(lax.rem(z + 4 - k, 4) * 4 * self.rows, 16), 4 * self.rows), self.cols(c)]
                send(p, p, gs.at[self.n, 3], gr.at[self.n, 12], me, other).start()

        def done(self):
            m = self.region(16, other)
            send(m, m, gs.at[self.n, 3], gr.at[self.n, 12], me, other).wait_recv()

        def drain(self):
            for stage, k in ((0, 3), (1, 4), (2, 8), (3, 16)):
                m = self.region(k)
                send(m, m, gs.at[self.n, stage], gr.at[self.n, 12], me, other).wait_send()

    near_xy = xy + (1 - c) * (1 - 2 * x) + c * (2 - 4 * y)
    pieces = [
        Piece(g, wide, 48, g * 768, 384, [(win_s, k * D + g * 256, 128) for k in range(3)]) for g in range(3)
    ]
    pieces += [Piece(3, wide, 48, OUT, 384, [(wout_s, 0, 384)])]
    pieces += [Piece(4 + k, wide, 48, EXP + k * 768, 384, [(wexp_s, k * 768, 384)]) for k in range(4)]
    pieces += [Piece(8 + k, wcon, 192, k * 256, 128, [(wcon_s, k * 256, 128)]) for k in range(3)]
    EARLY = 3

    def s2(t):
        pieces[t].s2(t < EARLY)

    def s3(t):
        pieces[t].s3()

    def s4(t):
        pieces[t].s4()

    SM = 11

    def small(stage, k, recv):
        d = send(vec.at[pl.ds(0, k)], vec.at[pl.ds(0, k)], gs.at[SM, stage], gr.at[SM, stage], me, other)
        d.wait_recv() if recv else d.wait_send()

    swap_tok = send(tokens, tokr, swap_sem.at[0, 0], swap_sem.at[0, 1], me, other)
    swap_cot = send(cot, cotr, swap_sem.at[1, 0], swap_sem.at[1, 1], me, other)
    own_tok = pltpu.make_async_copy(tokens, tok, ls.at[11])
    own_cot = pltpu.make_async_copy(cot, cotn, ls.at[12])
    own_vec = pltpu.make_async_copy(small_s, vec.at[me], ls.at[13])

    pieces[0].s1(True)
    own_tok.start()
    own_vec.start()
    swap_tok.start()
    for q in zs:
        send(small_s, vec.at[me], gs.at[SM, 0], gr.at[SM, 0], q, c).start()
    for t, p in enumerate(pieces[1:]):
        p.s1(t + 1 < EARLY)
    swap_cot.start()
    own_cot.start()

    row = seg[...].astype(F32)
    first_row = jnp.zeros((1, 1), F32)
    for d in range(DOCS):
        size = jnp.sum(jnp.where(row == d, 1.0, 0.0), axis=1, keepdims=True)
        before = jnp.sum(jnp.where(row < d, 1.0, 0.0), axis=1, keepdims=True)
        first_row = first_row + jnp.where(size == T, before, 0.0)
    keep_row = lax.broadcasted_iota(jnp.int32, (1, T), 1).astype(F32) >= first_row
    mine = seg[:, pl.ds(al(c * T, 128), T)].astype(F32)
    theirs = seg[:, pl.ds(al(other * T, 128), T)].astype(F32)
    seg_row = jnp.where(keep_row, mine, theirs)
    seg_col = jnp.broadcast_to(seg_row, (128, T)).T[:, :1]
    keep_col = lax.broadcasted_iota(jnp.int32, (T, 1), 0).astype(F32) >= first_row
    keep_col = jnp.where(keep_col, 1.0, 0.0)
    sc1[...] = jnp.concatenate([keep_col, seg_col], axis=1)

    def mask_rows(i, _):
        r = pl.ds(al(i * 128, 128), 128)
        bias[r, :] = jnp.where(sc1[r, 1:2] == seg_row, 0.0, -1e30)
        return 0

    lax.fori_loop(0, T // 128, mask_rows, 0)
    s2(0)
    own_vec.wait()
    small(0, 3, True)

    def small2(k, _):
        b = vec.at[k * 4 + xy]
        send(b, b, gs.at[SM, 1], gr.at[SM, 1], near, c).start()
        return 0

    lax.fori_loop(0, 4, small2, 0)
    s3(0)
    own_tok.wait()
    swap_tok.wait_recv()

    def start_rows(i, _):
        r = pl.ds(al(i * 128, 128), 128)
        t = jnp.where(sc1[r, 0:1] > 0.5, tok[r, :].astype(F32), tokr[r, :].astype(F32)) + te[...]
        n1[r, :] = t
        xl[r, :] = t.astype(BF)
        return 0

    lax.fori_loop(0, T // 128, start_rows, 0)
    s2(1)
    s4(0)
    small(1, 4, True)

    def small3(k, _):
        b = vec.at[(k // 2) * 4 + (1 - c) * 2 * y + c * x + lax.rem(k, 2) * (1 + c)]
        send(b, b, gs.at[SM, 2], gr.at[SM, 2], far, c).start()
        return 0

    lax.fori_loop(0, 8, small3, 0)
    s3(1)
    small(2, 8, True)
    for o in range(16):
        fullv[:, o * 48 : (o + 1) * 48] = vec[o][:, :48].astype(F32)
        for k in range(4):
            fulle[:, o * 192 + k * 48 : o * 192 + (k + 1) * 48] = vec[o][k : k + 1, 64:112].astype(F32)
    fullp[...] = jnp.concatenate([jnp.zeros_like(fullp[0:1, :]), jnp.ones_like(fullp[0:1, :])], axis=0)
    for h in range(D // 128):
        fullp[0:1, h * 384 : h * 384 + 128] = fullv[0:1, h * 128 : (h + 1) * 128]
        fullp[0:1, h * 384 + 256 : h * 384 + 384] = fullv[1:2, h * 128 : (h + 1) * 128]
        fullp[1:2, h * 384 : h * 384 + 128] = jnp.full((1, 128), HD**-0.5, F32)

    def project(g):
        cs = pl.ds(al(g * 768, 768), 768)
        proj[:, cs] = ((nn(xl[...], wide[:, cs]) + fullp[0:1, cs]) * fullp[1:2, cs]).astype(BF)

    lane = lax.broadcasted_iota(jnp.int32, (1, 128), 1)
    halves = (lane < HD, lane >= HD)
    pairs = D // 128

    def keep(h, a):
        return pltpu.make_async_copy(pslot.at[a], spill.at[h * 2 + a], ps.at[a])

    tasks = [
        lambda: (s2(2), s4(1)),
        lambda: (s2(3), s3(2)),
        lambda: (s4(2), s2(4), s3(3)),
        lambda: (s2(5),),
        lambda: (s4(3), s3(4)),
        lambda: (s2(6), s4(4), s3(5)),
    ]

    def attend(h, _):
        for g in range(3):

            @pl.when(h == 2 * g)
            def _():
                pieces[g].done()

        @pl.when(lax.rem(h, 2) == 0)
        def _():
            project(h // 2)

        cs = al(h * 384, 128)
        q2 = proj[:, pl.ds(cs, 128)]
        k2 = proj[:, pl.ds(cs + 128, 128)]
        v2 = proj[:, pl.ds(cs + 256, 128)]
        outs = []
        for a in range(2):
            s = nt(jnp.where(halves[a], q2, jnp.zeros_like(q2)), k2) + bias[...]
            e = jnp.exp(s - jnp.max(s, axis=-1, keepdims=True))
            p = (e * (1.0 / jnp.sum(e, axis=-1, keepdims=True))).astype(BF)

            @pl.when(h > 0)
            def _():
                keep(h - 1, a).wait()

            pslot[a] = p
            keep(h, a).start()
            outs.append(nn(p, v2))
        heads[:, pl.ds(al(h * 128, 128), 128)] = jnp.where(halves[0], outs[0], outs[1]).astype(BF)
        for k in range(pairs):

            @pl.when(h == k)
            def _():
                tasks[k]()

        return 0

    lax.fori_loop(0, pairs, attend, 0)
    pieces[3].done()

    def load(h, a):
        return pltpu.make_async_copy(spill.at[h * 2 + a], pslot.at[a], pd.at[a])

    for a in range(2):
        keep(pairs - 1, a).wait()
        load(0, a).start()

    def normalize(v):
        centred = v - jnp.mean(v, axis=-1, keepdims=True)
        scale = lax.rsqrt(jnp.mean(centred * centred, axis=-1, keepdims=True) + 1e-5)
        return centred * scale, scale

    def first_rows(i, _):
        r = pl.ds(al(i * 256, 256), 256)
        v = n1[r, :] + (nn(heads[r, :], wide[:, OUT:EXP]) + fullv[2:3, :])
        n, s = normalize(v)
        n1[r, :] = n
        sc1[r, 1:2] = s
        fl[r, :] = (n * fullv[3:4, :] + fullv[4:5, :]).astype(BF)
        return 0

    lax.fori_loop(0, T // 256, first_rows, 0)
    s2(7)
    s4(5)
    s3(6)
    after = [
        lambda: (s2(8), s4(6), s3(7)),
        lambda: (s2(9), s4(7), s3(8)),
        lambda: (s2(10), s4(8), s3(9)),
        lambda: (s4(9), s3(10)),
    ]

    def expand(i, _):
        for k in range(4):

            @pl.when(i == k)
            def _():
                pieces[4 + k].done()

        cs = pl.ds(al(i * 768, 768), 768)
        u = nn(fl[...], wide[:, pl.ds(al(EXP + i * 768, 768), 768)]) + fulle[:, cs]
        cdf = 0.5 * (1.0 + lax.erf(u * math.sqrt(0.5)))
        hidden[:, cs] = (u * cdf).astype(BF)
        slope[:, cs] = (cdf + u * jnp.exp(-0.5 * u * u) * (1.0 / math.sqrt(2.0 * math.pi))).astype(BF)
        for k in range(4):

            @pl.when(i == k)
            def _():
                after[k]()

        return 0

    lax.fori_loop(0, FF // 768, expand, 0)

    def contract(i, _):
        for k in range(3):

            @pl.when(i == k)
            def _():
                if k == 1:
                    s4(10)
                pieces[8 + k].done()

        cs = pl.ds(al(i * 256, 256), 256)
        sg[:, cs] = nn(hidden[...], wcon[:, cs]) + fullv[5:6, cs]
        return 0

    lax.fori_loop(0, D // 256, contract, 0)
    own_cot.wait()
    swap_cot.wait_recv()

    gv[...] = jnp.zeros_like(gv)

    def second_rows(i, _):
        r = pl.ds(al(i * 256, 256), 256)
        v = n1[r, :] * fullv[3:4, :] + fullv[4:5, :] + sg[r, :]
        n, s = normalize(v)
        lonew[r, :] = (n * fullv[6:7, :] + fullv[7:8, :]).astype(BF)
        og = jnp.where(sc1[r, 0:1] > 0.5, cotn[r, :].astype(F32), cotr[r, :].astype(F32))
        gv[6:7, :] += jnp.sum(og * n, axis=0, keepdims=True)
        gv[7:8, :] += jnp.sum(og, axis=0, keepdims=True)
        w = og * fullv[6:7, :]
        g = s * (w - jnp.mean(w, axis=-1, keepdims=True) - n * jnp.mean(w * n, axis=-1, keepdims=True))
        sg[r, :] = g
        low = g.astype(BF)
        bg[r, :] = low
        gv[5:6, :] += jnp.sum(low.astype(F32), axis=0, keepdims=True)
        return 0

    lax.fori_loop(0, T // 256, second_rows, 0)
    swap_lo = send(lonew, lor, swap_sem.at[2, 0], swap_sem.at[2, 1], me, other)
    swap_lo.start()

    S = 384
    my_k = (1 - c) * x + c * y
    far_base = (1 - c) * (2 - 2 * y) + c * (1 - x)
    own_base = (1 - c) * 2 * y + c * x
    step_k = 1 + c

    def total(*refs):
        t = refs[0][...].astype(F32)
        for ref in refs[1:]:
            t = t + ref[...].astype(F32)
        return t

    class Red:
        def __init__(self, n, g, col, rows, recv, rcol, fsum, plane=None):
            self.n, self.g, self.col, self.rows, self.recv, self.rcol, self.fsum = n, g, col, rows, recv, rcol, fsum
            self.plane = plane
            self.fcol = (n - 4) * 768 if 4 <= n < 8 else 0

        def cols(self, core):
            return pl.ds(al(self.col + core * S, 128), S)

        def part(self, base, i, k=1, second=False):
            if self.plane is None:
                cs = pl.ds(self.rcol + (S if second else 0), S)
            else:
                cs = pl.ds(0, S)
                base = base + self.rcol
            return self.recv.at[pl.ds(al(base + i * self.rows, 16), k * self.rows), cs]

        def mine(self, o):
            base = 0 if self.plane is None else self.plane * 4
            return self.g.at[pl.ds(al((base + o) * self.rows, 16), self.rows), self.cols(c)]

        def planes(self):
            return 4 if self.plane is None else 1

        def rp(self, o, k=1):
            return self.part(0, o, k)

        def ra(self, i, k=1):
            return self.part(0 if self.plane is None else 768, i, k, True)

        def rb(self, i, k=1):
            return self.part(384 if self.plane is None else 1152, i, k, True)

        def rz(self, i, k=1):
            if self.plane is None:
                return self.part(576, i, k, True)
            return self.recv.at[pl.ds(al(5376 + i * self.rows, 16), k * self.rows), pl.ds(0, S)]

        def sem(self, stage):
            return rs.at[self.n, stage], rr.at[self.n, stage]

        def got(self, stage, ref):
            s, r = self.sem(stage)
            send(ref, ref, s, r, me, other).wait_recv()

        def gone(self, stage, ref):
            s, r = self.sem(stage)
            send(ref, ref, s, r, me, other).wait_send()

        def P(self):
            base = 0 if self.plane is None else self.plane * 4 * self.rows
            n = 4 * self.planes() * self.rows
            src = self.g.at[pl.ds(al(base, 16), n), self.cols(other)]
            s, r = self.sem(0)
            send(src, self.rp(0, 4 * self.planes()), s, r, me, other).start()

        def A(self):
            self.got(0, self.rp(0, 4 * self.planes()))
            s, r = self.sem(1)

            def one(i, _):
                o = (i // 2) * 4 + far_base + lax.rem(i, 2) * step_k
                b = self.mine(o)
                b[...] = total(b, self.rp(o)).astype(BF)
                send(b, self.ra(i), s, r, far, c).start()
                return 0

            lax.fori_loop(0, 2 * self.planes(), one, 0)

        def B(self):
            self.got(1, self.ra(0, 2 * self.planes()))
            s, r = self.sem(2)

            def one(i, _):
                o = i * 4 + near_xy
                b = self.mine(o)
                b[...] = total(b, self.rp(o), self.ra(i * 2 + 1 - my_k)).astype(BF)
                send(b, self.rb(i), s, r, near, c).start()
                return 0

            lax.fori_loop(0, self.planes(), one, 0)

        def Z(self, j=None):
            self.got(2, self.rb(0, self.planes()))
            if self.plane is None:
                for k in range(3):
                    s, r = self.sem(3)
                    p = lax.rem(z + k + 1, 4)
                    b = self.mine(p * 4 + xy)
                    b[...] = total(b, self.rp(p * 4 + xy), self.ra(p * 2 + my_k), self.rb(p)).astype(BF)
                    send(b, self.rz(k), s, r, zs[k], c).start()
            elif j > 0:
                s, r = rs.at[self.n, 3], rr.at[0, 3]
                b = self.mine(xy)
                b[...] = total(b, self.rp(xy), self.ra(my_k), self.rb(0)).astype(BF)
                send(b, self.rz(j - 1), s, r, zs[j - 1], c).start()

        def F(self):
            if self.plane is None:
                self.got(3, self.rz(0, 3))
                t = total(self.mine(z * 4 + xy), self.rp(z * 4 + xy), self.ra(z * 2 + my_k), self.rb(z),
                          self.rz(0), self.rz(1), self.rz(2))
            else:
                ref = self.rz(0, 3)
                send(ref, ref, rs.at[0, 3], rr.at[0, 3], me, other).wait_recv()
                t = total(self.mine(xy), self.rp(xy), self.ra(my_k), self.rb(0), self.rz(0), self.rz(1), self.rz(2))
            s, r = self.sem(4)
            if self.n >= 9:
                for k in range(3):
                    b = self.fsum.at[:, pl.ds(al(k * D + (self.n - 9) * 256 + c * 128, 128), 128)]
                    b[...] = t[:, k * 128 : (k + 1) * 128]
                    send(b, b, s, r, me, other).start()
            else:
                b = self.fsum.at[:, pl.ds(al(self.fcol + c * S, 128), S)]
                b[...] = t
                send(b, b, s, r, me, other).start()

        def end(self):
            p = self.planes()
            self.gone(0, self.rp(0, 4 * p))
            self.gone(1, self.ra(0, 2 * p))
            self.gone(2, self.rb(0, p))
            if self.plane is None:
                self.gone(3, self.rz(0, 3))
            elif self.n > 0:
                self.gone(3, self.rz(0, 1))
            if self.plane is None or self.n == 0:
                half = self.fsum.at[:, pl.ds(0, S)]
                self.gone(4, half)
                self.got(4, half)

    con = {j: Red(j, gcon, 0, 192, con_r, j * 1344, fcon, plane=lax.rem(z + j, 4)) for j in range(4)}
    exp = [Red(4 + k, wide, EXP + k * 768, 48, hidden, k * 768, fexp) for k in range(4)]
    out = Red(8, wide, OUT, 48, cotn, 0, fout)
    ins = [Red(9 + k, gin, k * 768, 48, slope, k * 768, fin) for k in range(3)]

    def run_at(i, lists):
        for k, t in lists.items():

            @pl.when(i == k)
            def _():
                for u in t:
                    u()

    def grad_con(i, _):
        p = al(lax.rem(z + i + 1, 4) * 768, 768)
        gcon[pl.ds(p, 768), :] = tn(hidden[:, pl.ds(p, 768)], bg[...]).astype(BF)
        run_at(i, {
            0: [con[1].P],
            1: [con[2].P, con[1].A],
            2: [con[3].P, con[2].A],
            3: [con[0].P, con[3].A],
        })
        return 0

    lax.fori_loop(0, 4, grad_con, 0)

    def expand_back(i, _):
        cs = pl.ds(al(i * 768, 768), 768)
        g = (nt(bg[...], wcon[cs, :]) * slope[:, cs].astype(F32)).astype(BF)
        slope[:, cs] = g
        ge[:, cs] = jnp.sum(g.astype(F32), axis=0, keepdims=True)
        run_at(i, {0: [con[0].A], 1: [con[1].B], 3: [con[2].B]})
        return 0

    lax.fori_loop(0, FF // 768, expand_back, 0)

    def first_back(i, _):
        r = pl.ds(al(i * 256, 256), 256)
        g = sg[r, :] + nt(slope[r, :], wide[:, EXP:])
        n = n1[r, :]
        gv[3:4, :] += jnp.sum(g * n, axis=0, keepdims=True)
        gv[4:5, :] += jnp.sum(g, axis=0, keepdims=True)
        w = g * fullv[3:4, :]
        g = sc1[r, 1:2] * (w - jnp.mean(w, axis=-1, keepdims=True) - n * jnp.mean(w * n, axis=-1, keepdims=True))
        sg[r, :] = g
        low = g.astype(BF)
        bg[r, :] = low
        gv[2:3, :] += jnp.sum(low.astype(F32), axis=0, keepdims=True)
        run_at(i, {0: [con[3].B], 1: [lambda: con[1].Z(1)], 2: [con[0].B, lambda: con[2].Z(2)]})
        return 0

    lax.fori_loop(0, T // 256, first_back, 0)
    for p in pieces[4:8]:
        p.drain()

    def grad_exp(i, _):
        cs = pl.ds(al(i * 768, 768), 768)
        wide[:, pl.ds(al(EXP + i * 768, 768), 768)] = tn(fl[...], slope[:, cs]).astype(BF)
        run_at(i, {
            0: [exp[0].P, lambda: con[3].Z(3)],
            1: [exp[1].P, exp[0].A, lambda: con[0].Z(0)],
            2: [exp[2].P, exp[1].A],
            3: [exp[3].P, exp[2].A, con[0].F],
        })
        return 0

    lax.fori_loop(0, 4, grad_exp, 0)
    hg = cotr
    hg[...] = nt(bg[...], wide[:, OUT:EXP]).astype(BF)
    exp[3].A()
    pieces[3].drain()
    wide[:, OUT:EXP] = tn(heads[...], bg[...]).astype(BF)
    out.P()

    tasks = [
        [exp[0].B],
        [exp[1].B, exp[0].Z],
        [out.A],
        [exp[2].B, ins[0].A, exp[1].Z],
        [exp[3].B, exp[2].Z, exp[0].F, ins[1].A],
        [exp[3].Z, out.B, exp[1].F],
    ]

    def attend_back(h, _):
        cs = al(h * 384, 128)
        hs = pl.ds(al(h * 128, 128), 128)
        q2 = proj[:, pl.ds(cs, 128)]
        k2 = proj[:, pl.ds(cs + 128, 128)]
        v2 = proj[:, pl.ds(cs + 256, 128)]
        g2 = hg[:, hs]
        prod = g2.astype(F32) * heads[:, hs].astype(F32)
        qt = q2.astype(F32).T.astype(BF)
        gt = g2.astype(F32).T.astype(BF)
        dq, dk, dv = [], [], []
        for a in range(2):
            load(h, a).wait()
            rowdot = jnp.sum(jnp.where(halves[a], prod, 0.0), axis=-1, keepdims=True)
            p = pslot[a]
            dp = nt(jnp.where(halves[a], g2, jnp.zeros_like(g2)), v2)
            ds = (p.astype(F32) * (dp - rowdot)).astype(BF)
            dq.append(nn(ds, k2))
            dk.append(nn(qt[a * HD : (a + 1) * HD], ds))
            dv.append(nn(gt[a * HD : (a + 1) * HD], p))

            @pl.when(h + 1 < pairs)
            def _():
                load(h + 1, a).start()

        dq = (jnp.where(halves[0], dq[0], dq[1]) * HD**-0.5).astype(BF)
        dk = jnp.concatenate(dk, axis=0).T.astype(BF)
        dv = jnp.concatenate(dv, axis=0).T.astype(BF)
        proj[:, pl.ds(cs, 128)] = dq
        proj[:, pl.ds(cs + 128, 128)] = dk
        proj[:, pl.ds(cs + 256, 128)] = dv
        gv[0:1, hs] = jnp.sum(dq.astype(F32), axis=0, keepdims=True)
        gv[1:2, hs] = jnp.sum(dv.astype(F32), axis=0, keepdims=True)

        @pl.when(lax.rem(h, 2) == 1)
        def _():
            cols = pl.ds(al((h // 2) * 768, 768), 768)
            gin[:, cols] = tn(xl[...], proj[:, cols]).astype(BF)

        for k in range(pairs):

            @pl.when(h == k)
            def _():
                if k % 2 == 1:
                    ins[k // 2].P()
                for t in tasks[k]:
                    t()

        return 0

    lax.fori_loop(0, pairs, attend_back, 0)

    vout[...] = jnp.zeros_like(vout)
    for o in range(16):
        vout[o, :, 0:48] = gv[0:8, o * 48 : (o + 1) * 48]
        for k in range(4):
            vout[o, k : k + 1, 64:112] = ge[:, o * 192 + k * 48 : o * 192 + (k + 1) * 48]
    VN = 12

    def vsend(stage, src, dst, dp, seq):
        return send(src, dst, rs.at[VN, stage], rr.at[VN, stage], dp, seq)

    vsend(0, vout, vr.at[pl.ds(0, 16)], me, other).start()
    ins[2].A()

    def input_rows(i, _):
        r = pl.ds(al(i * 256, 256), 256)
        sg[r, :] = sg[r, :] + nt(proj[r, :], wide[:, IN:OUT])
        run_at(i, {0: [exp[2].F, ins[0].B], 1: [exp[3].F, out.Z], 2: [ins[1].B]})
        return 0

    lax.fori_loop(0, T // 256, input_rows, 0)
    swap_ig = send(sg, n1, swap_sem.at[3, 0], swap_sem.at[3, 1], me, other)
    swap_ig.start()
    vsend(0, vout, vr.at[pl.ds(0, 16)], me, other).wait_recv()
    vsum[...] = vout[...] + vr[pl.ds(0, 16)]
    for i in range(8):
        b = vsum.at[(i // 2) * 4 + 2 - 2 * y + i % 2]
        vsend(1, b, vr.at[16 + i], flip_y, c).start()
    ins[0].Z()
    ins[2].B()
    vsend(1, vr.at[pl.ds(16, 8)], vr.at[pl.ds(16, 8)], me, other).wait_recv()
    for i in range(8):
        o = (i // 2) * 4 + 2 * y + i % 2
        vsum[o] = vsum[o] + vr[16 + i]
    for i in range(4):
        b = vsum.at[i * 4 + 2 * y + 1 - x]
        vsend(2, b, vr.at[24 + i], flip_x, c).start()
    ins[1].Z()
    out.F()
    vsend(2, vr.at[pl.ds(24, 4)], vr.at[pl.ds(24, 4)], me, other).wait_recv()
    for i in range(4):
        vsum[i * 4 + xy] = vsum[i * 4 + xy] + vr[24 + i]
    for k in range(3):
        b = vsum.at[lax.rem(z + k + 1, 4) * 4 + xy]
        vsend(3, b, vr.at[28 + k], zs[k], c).start()
    ins[0].F()
    ins[2].Z()
    ins[1].F()
    ins[2].F()

    swap_lo.wait()

    def out_rows(i, _):
        r = pl.ds(al(i * 128, 128), 128)
        lonew[r, :] = jnp.where(sc1[r, 0:1] > 0.5, lonew[r, :].astype(F32), lor[r, :].astype(F32)).astype(BF)
        return 0

    lax.fori_loop(0, T // 128, out_rows, 0)
    lo_done = pltpu.make_async_copy(lonew, lo_o, ls.at[14])
    lo_done.start()
    swap_ig.wait()

    def grad_rows(i, _):
        r = pl.ds(al(i * 128, 128), 128)
        sg[r, :] = jnp.where(sc1[r, 0:1] > 0.5, sg[r, :], n1[r, :])
        return 0

    lax.fori_loop(0, T // 128, grad_rows, 0)
    outs = [lo_done, pltpu.make_async_copy(sg, ig_o, ls.at[15])]
    outs[1].start()
    vsend(3, vr.at[pl.ds(28, 3)], vr.at[pl.ds(28, 3)], me, other).wait_recv()
    vfin = vr.at[31]
    vfin[...] = vsum[z * 4 + xy] + vr[28] + vr[29] + vr[30]
    outs.append(pltpu.make_async_copy(vfin, gvec_o, ls.at[16]))
    outs[2].start()
    swap_tok.wait_send()
    swap_cot.wait_send()
    for p in pieces[0:3] + pieces[8:]:
        p.drain()
    for stage, k in ((0, 3), (1, 4), (2, 8)):
        small(stage, k, False)
        vsend(stage + 1, vr.at[pl.ds(0, (8, 4, 3)[stage])], vr.at[pl.ds(0, (8, 4, 3)[stage])], me, other).wait_send()
    vsend(0, vout, vr.at[pl.ds(0, 16)], me, other).wait_send()
    for p in list(con.values()) + exp + [out] + ins:
        p.end()
    for k, (v, o) in enumerate([(fin, gin_o), (fout, gout_o), (fexp, gexp_o), (fcon, gcon_o)]):
        outs.append(pltpu.make_async_copy(v, o, ls.at[17 + k]))
        outs[-1].start()
    for o in outs:
        o.wait()


def fused_layer(tokens, time_embed, segments, iw, ow, ew, cw, small, cot):
    T, D = tokens.shape
    FF = ew.shape[1]
    sh = jax.ShapeDtypeStruct
    anyspec = pl.BlockSpec(memory_space=pl.ANY)
    vspec = pl.BlockSpec(memory_space=VM)
    scratch = [
        VM((D, 4 * D + FF), BF), VM((FF, D), BF),
        VM((T, D), BF), VM((T, D), BF), VM((T, D), BF), VM((T, D), BF),
        VM((16, 16, 128), BF), VM((16, D), F32), VM((1, FF), F32), VM((2, 3 * D), F32),
        VM((T, 3 * D), BF), VM((T, D), BF), VM((T, D), F32), VM((T, T), F32),
        VM((T, 2), F32), VM((T, D), BF), VM((T, D), BF), VM((T, FF), BF), VM((T, FF), BF),
        VM((2, T, T), BF), VM((T, D), BF),
        VM((D, 3 * D), BF), VM((FF, D), BF), VM((5952, 384), BF), VM((8, D), F32), VM((1, FF), F32),
        VM((16, 8, 128), F32), VM((16, 8, 128), F32), VM((32, 8, 128), F32),
        VM(iw.shape, F32), VM(ow.shape, F32), VM(ew.shape, F32), VM(cw.shape, F32),
        DMA((4, 2)), DMA((21,)), DMA((12, 4)), DMA((12, 13)), DMA((2,)), DMA((13, 5)), DMA((13, 5)), DMA((2,)),
    ]
    return pl.pallas_call(
        fused_kernel,
        out_shape=(
            sh((T, D), BF), sh((T, D), F32), sh(iw.shape, F32), sh(ow.shape, F32), sh(ew.shape, F32),
            sh(cw.shape, F32), sh((8, 128), F32), sh((D // HD, T, T), BF),
        ),
        in_specs=[anyspec, anyspec, vspec, vspec, anyspec, anyspec, anyspec, anyspec, anyspec],
        out_specs=(anyspec,) * 8,
        scratch_shapes=scratch,
        compiler_params=pltpu.CompilerParams(
            collective_id=0, has_side_effects=True, vmem_limit_bytes=67043328
        ),
    )(tokens, cot, time_embed, segments, iw, ow, ew, cw, small)


epsilon = 1e-05
masked_score = -1e30


def matmul(left, right):
    return jnp.dot(left, right, preferred_element_type=jnp.float32)


def product_tn(left, right):
    return lax.dot_general(
        left, right, (((0,), (0,)), ((), ())), preferred_element_type=jnp.float32
    )


def product_nt(left, right):
    return lax.dot_general(
        left, right, (((1,), (1,)), ((), ())), preferred_element_type=jnp.float32
    )


def normalize(values):
    mean = jnp.mean(values, axis=-1, keepdims=True)
    centred = values - mean
    scale = lax.rsqrt(jnp.mean(centred * centred, axis=-1, keepdims=True) + epsilon)
    return (centred * scale, scale)


def norm_back(grad, normed, scale, gain):
    scaled = grad * gain
    return scale * (
        scaled
        - jnp.mean(scaled, axis=-1, keepdims=True)
        - normed * jnp.mean(scaled * normed, axis=-1, keepdims=True)
    )


def gelu_value(values):
    return 0.5 * values * (1.0 + lax.erf(values * math.sqrt(0.5)))


def gelu_slope(values):
    return 0.5 * (1.0 + lax.erf(values * math.sqrt(0.5))) + values * jnp.exp(
        -0.5 * values * values
    ) / math.sqrt(2.0 * math.pi)


def attend_forward(item):
    query, key, value, segment_row = item
    length, depth = query.shape
    block = min(512, length)
    blocks = length // block
    scale = depth ** (-0.5)

    def one_block(part):
        query_block, segment_block = part
        scores = product_nt(query_block, key) * scale
        scores = jnp.where(segment_block[:, None] == segment_row[None, :], scores, masked_score)
        top = jnp.max(scores, axis=-1, keepdims=True)
        expo = jnp.exp(scores - top)
        total = jnp.sum(expo, axis=-1, keepdims=True)
        probs_low = (expo / total).astype(jnp.bfloat16)
        return (matmul(probs_low, value).astype(jnp.bfloat16), (top + jnp.log(total))[:, 0])

    outputs, logsum = lax.map(
        one_block, (query.reshape(blocks, block, depth), segment_row.reshape(blocks, block))
    )
    return (outputs.reshape(length, depth), logsum.reshape(length))


def attend_backward(item):
    query, key, value, segment_row, logsum, out_grad = item
    length, depth = query.shape
    block = min(512, length)
    blocks = length // block
    scale = depth ** (-0.5)

    def one_block(carry, part):
        key_grad, value_grad = carry
        query_block, segment_block, logsum_block, grad_block = part
        scores = product_nt(query_block, key) * scale
        scores = jnp.where(segment_block[:, None] == segment_row[None, :], scores, masked_score)
        probs = jnp.exp(scores - logsum_block[:, None])
        probs_low = probs.astype(jnp.bfloat16)
        prob_grad = product_nt(grad_block, value)
        row_total = jnp.sum(probs * prob_grad, axis=-1, keepdims=True)
        score_grad = (probs * (prob_grad - row_total)).astype(jnp.bfloat16)
        query_grad = matmul(score_grad, key) * scale
        key_grad = key_grad + product_tn(score_grad, query_block) * scale
        value_grad = value_grad + product_tn(probs_low, grad_block)
        return ((key_grad, value_grad), query_grad.astype(jnp.bfloat16))

    zeros = jnp.zeros((length, depth), jnp.float32)
    parts = (
        query.reshape(blocks, block, depth),
        segment_row.reshape(blocks, block),
        logsum.reshape(blocks, block),
        out_grad.reshape(blocks, block, depth),
    )
    (key_grad, value_grad), query_grad = lax.scan(one_block, (zeros, zeros), parts)
    return (
        query_grad.reshape(length, depth),
        key_grad.astype(jnp.bfloat16),
        value_grad.astype(jnp.bfloat16),
    )


def plain_body(
    tokens,
    time_embed,
    segments,
    input_weight,
    query_bias,
    value_bias,
    output_weight,
    output_bias,
    first_gain,
    first_shift,
    expand_weight,
    expand_bias,
    contract_weight,
    contract_bias,
    second_gain,
    second_shift,
    cotangent,
):
    pairs = lax.axis_size("seq")
    seqs, half, width = tokens.shape
    length = half * pairs
    rows = seqs * half
    group = width // pairs
    heads_here = group // HD
    start = (tokens.astype(jnp.float32) + time_embed[:, None, :]).reshape(rows, width)
    start_low = start.astype(jnp.bfloat16)
    attention_set = (
        lax.all_gather(input_weight, "dp", axis=0, tiled=True),
        lax.all_gather(output_weight, "dp", axis=0, tiled=True),
        lax.all_gather(query_bias, "dp", axis=0, tiled=True),
        lax.all_gather(value_bias, "dp", axis=0, tiled=True),
        lax.all_gather(output_bias, "dp", axis=0, tiled=True),
        lax.all_gather(first_gain, "dp", axis=0, tiled=True),
        lax.all_gather(first_shift, "dp", axis=0, tiled=True),
    )
    (
        full_input,
        full_output,
        full_query_bias,
        full_value_bias,
        full_output_bias,
        full_first_gain,
        full_first_shift,
    ) = attention_set
    bias_row = jnp.concatenate(
        [
            full_query_bias.astype(jnp.float32),
            jnp.zeros((width,), jnp.float32),
            full_value_bias.astype(jnp.float32),
        ]
    )
    projected_low = (matmul(start_low, full_input) + bias_row).astype(jnp.bfloat16)
    regrouped = lax.all_to_all(
        projected_low.reshape(seqs, half, 3, pairs, group),
        "seq",
        split_axis=3,
        concat_axis=1,
        tiled=True,
    )
    split = regrouped.reshape(seqs, length, 3, heads_here, HD).transpose(2, 0, 3, 1, 4)
    split = split.reshape(3, seqs * heads_here, length, HD)
    query_heads, key_heads, value_heads = (split[0], split[1], split[2])
    segment_heads = jnp.repeat(segments, heads_here, axis=0)
    heads_out, logsum = lax.map(
        attend_forward, (query_heads, key_heads, value_heads, segment_heads)
    )
    heads_tokens = (
        heads_out.reshape(seqs, heads_here, length, HD)
        .transpose(0, 2, 1, 3)
        .reshape(seqs, length, 1, group)
    )
    heads_low = lax.all_to_all(
        heads_tokens, "seq", split_axis=1, concat_axis=2, tiled=True
    ).reshape(rows, width)
    attention = matmul(heads_low, full_output) + full_output_bias.astype(jnp.float32)
    normed_one, scale_one = normalize(start + attention)
    gain_one = full_first_gain.astype(jnp.float32)
    first = normed_one * gain_one + full_first_shift.astype(jnp.float32)
    first_low = first.astype(jnp.bfloat16)
    network_set = (
        lax.all_gather(expand_weight, "dp", axis=0, tiled=True),
        lax.all_gather(contract_weight, "dp", axis=0, tiled=True),
        lax.all_gather(expand_bias, "dp", axis=0, tiled=True),
        lax.all_gather(contract_bias, "dp", axis=0, tiled=True),
        lax.all_gather(second_gain, "dp", axis=0, tiled=True),
        lax.all_gather(second_shift, "dp", axis=0, tiled=True),
    )
    (
        full_expand,
        full_contract,
        full_expand_bias,
        full_contract_bias,
        full_second_gain,
        full_second_shift,
    ) = network_set
    expand = matmul(first_low, full_expand) + full_expand_bias.astype(jnp.float32)
    hidden = gelu_value(expand).astype(jnp.bfloat16)
    second_sum = first + matmul(hidden, full_contract) + full_contract_bias.astype(jnp.float32)
    normed_two, scale_two = normalize(second_sum)
    gain_two = full_second_gain.astype(jnp.float32)
    layer_output = (normed_two * gain_two + full_second_shift.astype(jnp.float32)).astype(
        jnp.bfloat16
    )
    network_set = (
        lax.all_gather(expand_weight, "dp", axis=0, tiled=True),
        lax.all_gather(contract_weight, "dp", axis=0, tiled=True),
        lax.all_gather(expand_bias, "dp", axis=0, tiled=True),
        lax.all_gather(contract_bias, "dp", axis=0, tiled=True),
        lax.all_gather(second_gain, "dp", axis=0, tiled=True),
        lax.all_gather(second_shift, "dp", axis=0, tiled=True),
    )
    full_expand, full_contract = (network_set[0], network_set[1])
    out_grad = cotangent.astype(jnp.float32).reshape(rows, width)
    grad_second_gain = jnp.sum(out_grad * normed_two, axis=0)
    grad_second_shift = jnp.sum(out_grad, axis=0)
    second_grad = norm_back(out_grad, normed_two, scale_two, gain_two)
    branch_grad = second_grad.astype(jnp.bfloat16)
    grad_contract_bias = jnp.sum(branch_grad.astype(jnp.float32), axis=0)
    grad_contract_weight = product_tn(hidden, branch_grad)
    expand_grad = (product_nt(branch_grad, full_contract) * gelu_slope(expand)).astype(jnp.bfloat16)
    grad_expand_bias = jnp.sum(expand_grad.astype(jnp.float32), axis=0)
    grad_expand_weight = product_tn(first_low, expand_grad)
    first_grad = second_grad + product_nt(expand_grad, full_expand)
    grad_first_gain = jnp.sum(first_grad * normed_one, axis=0)
    grad_first_shift = jnp.sum(first_grad, axis=0)
    start_grad = norm_back(first_grad, normed_one, scale_one, gain_one)
    attention_set = (
        lax.all_gather(input_weight, "dp", axis=0, tiled=True),
        lax.all_gather(output_weight, "dp", axis=0, tiled=True),
        lax.all_gather(query_bias, "dp", axis=0, tiled=True),
        lax.all_gather(value_bias, "dp", axis=0, tiled=True),
        lax.all_gather(output_bias, "dp", axis=0, tiled=True),
        lax.all_gather(first_gain, "dp", axis=0, tiled=True),
        lax.all_gather(first_shift, "dp", axis=0, tiled=True),
    )
    full_input, full_output = (attention_set[0], attention_set[1])
    attention_grad = start_grad.astype(jnp.bfloat16)
    grad_output_bias = jnp.sum(attention_grad.astype(jnp.float32), axis=0)
    grad_output_weight = product_tn(heads_low, attention_grad)
    heads_grad = product_nt(attention_grad, full_output).astype(jnp.bfloat16)
    grad_heads = lax.all_to_all(
        heads_grad.reshape(seqs, half, pairs, group), "seq", split_axis=2, concat_axis=1, tiled=True
    )
    grad_heads = (
        grad_heads.reshape(seqs, length, heads_here, HD)
        .transpose(0, 2, 1, 3)
        .reshape(seqs * heads_here, length, HD)
    )
    query_grad, key_grad, value_grad = lax.map(
        attend_backward, (query_heads, key_heads, value_heads, segment_heads, logsum, grad_heads)
    )
    stacked = jnp.stack([query_grad, key_grad, value_grad]).reshape(3, seqs, heads_here, length, HD)
    stacked = stacked.transpose(1, 3, 0, 2, 4).reshape(seqs, length, 3, 1, group)
    projected_grad = lax.all_to_all(
        stacked, "seq", split_axis=1, concat_axis=3, tiled=True
    ).reshape(rows, 3 * width)
    grad_query_bias = jnp.sum(projected_grad[:, :width].astype(jnp.float32), axis=0)
    grad_value_bias = jnp.sum(projected_grad[:, 2 * width :].astype(jnp.float32), axis=0)
    grad_input_weight = product_tn(start_low, projected_grad)
    input_grad = (start_grad + product_nt(projected_grad, full_input)).reshape(seqs, half, width)
    grads = (
        grad_input_weight,
        grad_query_bias,
        grad_value_bias,
        grad_output_weight,
        grad_output_bias,
        grad_first_gain,
        grad_first_shift,
        grad_expand_weight,
        grad_expand_bias,
        grad_contract_weight,
        grad_contract_bias,
        grad_second_gain,
        grad_second_shift,
    )
    owned = (
        lax.psum_scatter(grads[0], "dp", scatter_dimension=0, tiled=True),
        lax.psum_scatter(grads[1], "dp", scatter_dimension=0, tiled=True),
        lax.psum_scatter(grads[2], "dp", scatter_dimension=0, tiled=True),
        lax.psum_scatter(grads[3], "dp", scatter_dimension=0, tiled=True),
        lax.psum_scatter(grads[4], "dp", scatter_dimension=0, tiled=True),
        lax.psum_scatter(grads[5], "dp", scatter_dimension=0, tiled=True),
        lax.psum_scatter(grads[6], "dp", scatter_dimension=0, tiled=True),
        lax.psum_scatter(grads[7], "dp", scatter_dimension=0, tiled=True),
        lax.psum_scatter(grads[8], "dp", scatter_dimension=0, tiled=True),
        lax.psum_scatter(grads[9], "dp", scatter_dimension=0, tiled=True),
        lax.psum_scatter(grads[10], "dp", scatter_dimension=0, tiled=True),
        lax.psum_scatter(grads[11], "dp", scatter_dimension=0, tiled=True),
        lax.psum_scatter(grads[12], "dp", scatter_dimension=0, tiled=True),
    )
    summed = (
        lax.psum(owned[0].astype(jnp.bfloat16), "seq").astype(jnp.float32),
        lax.psum(owned[1].astype(jnp.bfloat16), "seq").astype(jnp.float32),
        lax.psum(owned[2].astype(jnp.bfloat16), "seq").astype(jnp.float32),
        lax.psum(owned[3].astype(jnp.bfloat16), "seq").astype(jnp.float32),
        lax.psum(owned[4].astype(jnp.bfloat16), "seq").astype(jnp.float32),
        lax.psum(owned[5].astype(jnp.bfloat16), "seq").astype(jnp.float32),
        lax.psum(owned[6].astype(jnp.bfloat16), "seq").astype(jnp.float32),
        lax.psum(owned[7].astype(jnp.bfloat16), "seq").astype(jnp.float32),
        lax.psum(owned[8].astype(jnp.bfloat16), "seq").astype(jnp.float32),
        lax.psum(owned[9].astype(jnp.bfloat16), "seq").astype(jnp.float32),
        lax.psum(owned[10].astype(jnp.bfloat16), "seq").astype(jnp.float32),
        lax.psum(owned[11].astype(jnp.bfloat16), "seq").astype(jnp.float32),
        lax.psum(owned[12].astype(jnp.bfloat16), "seq").astype(jnp.float32),
    )
    return (layer_output.reshape(seqs, half, width), input_grad) + tuple(summed)


def fused_body(
    tokens, time_embed, segments, input_weight, query_bias, value_bias, output_weight, output_bias, first_gain,
    first_shift, expand_weight, expand_bias, contract_weight, contract_bias, second_gain, second_shift, cotangent,
):
    vectors = [
        query_bias, value_bias, output_bias, first_gain, first_shift, contract_bias, second_gain, second_shift,
    ]
    own = query_bias.shape[0]
    small = jnp.pad(jnp.stack(vectors), ((0, 8), (0, 64 - own)))
    wide = jnp.pad(expand_bias.reshape(4, own), ((0, 12), (0, 64 - own)))
    small = jnp.concatenate([small, wide], axis=1)
    layer_output, input_grad, g_in, g_out, g_exp, g_con, vec = fused_layer(
        tokens[0], time_embed, segments, input_weight, output_weight, expand_weight, contract_weight, small,
        cotangent[0],
    )[:7]
    row = [vec[k, :own] for k in range(8)]
    g_eb = vec[0:4, 64 : 64 + own].reshape(4 * own)
    return (
        layer_output[None], input_grad[None], g_in, row[0], row[1], g_out, row[2], row[3], row[4],
        g_exp, g_eb, g_con, row[5], row[6], row[7],
    )


def body(*args):
    if lax.axis_size("dp") == 16 and lax.axis_size("seq") == 2:
        return fused_body(*args)
    return plain_body(*args)


def solution(mesh):
    return jax.shard_map(
        body,
        mesh=mesh,
        in_specs=(
            P("dp", "seq", None),
            P("dp", None),
            P("dp", None),
            P("dp", None),
            P("dp"),
            P("dp"),
            P("dp", None),
            P("dp"),
            P("dp"),
            P("dp"),
            P("dp", None),
            P("dp"),
            P("dp", None),
            P("dp"),
            P("dp"),
            P("dp"),
            P("dp", "seq", None),
        ),
        out_specs=(
            P("dp", "seq", None),
            P("dp", "seq", None),
            P("dp", None),
            P("dp"),
            P("dp"),
            P("dp", None),
            P("dp"),
            P("dp"),
            P("dp"),
            P("dp", None),
            P("dp"),
            P("dp", None),
            P("dp"),
            P("dp"),
            P("dp"),
        ),
        check_vma=False,
    )
```

```python
import functools
import math

import jax
import jax.numpy as jnp
from jax import lax
from jax.experimental import pallas as pl
from jax.experimental.pallas import tpu as pltpu
from jax.sharding import PartitionSpec as P

HD = 64
DOCS = 4
BF = jnp.bfloat16
F32 = jnp.float32
MESH = pl.DeviceIdType.MESH
VM = pltpu.VMEM
DMA = pltpu.SemaphoreType.DMA


def nn(a, b):
    return jnp.dot(a, b, preferred_element_type=F32)


def nt(a, b):
    return lax.dot_general(a, b, (((1,), (1,)), ((), ())), preferred_element_type=F32)


def tn(a, b):
    return lax.dot_general(a, b, (((0,), (0,)), ((), ())), preferred_element_type=F32)


def fused_kernel(
    tokens, cot, te, seg, win_s, wout_s, wexp_s, wcon_s, small_s,
    lo_o, ig_o, gin_o, gout_o, gexp_o, gcon_o, gvec_o, spill,
    wide, wcon, tok, tokr, cotn, cotr, vec, fullv, fulle, fullp, proj, xl, n1, sg,
    sc1, heads, fl, hidden, slope, pslot, bg,
    gin, gcon, con_r, gv, ge, vout, vsum, vr, fin, fout, fexp, fcon,
    swap_sem, sw3, ls, gs, gr, vs, ps, rs, rr, pd,
):
    T, D = tok.shape
    FF = wcon.shape[0]
    IN, OUT, EXP = 0, 3 * D, 4 * D
    bias, lonew, lor = sg, tok, tokr
    me = lax.axis_index("dp")
    c = lax.axis_index("seq")
    x = lax.rem(me, 2)
    y = lax.rem(me // 2, 2)
    xy = lax.rem(me, 4)
    z = me // 4
    flip_x = me + 1 - 2 * x
    flip_y = me + 2 - 4 * y
    near = (1 - c) * flip_x + c * flip_y
    far = (1 - c) * flip_y + c * flip_x
    other = 1 - c
    zs = [lax.rem(z + k, 4) * 4 + xy for k in (1, 2, 3)]

    def send(src, dst, s, r, dp, seq):
        return pltpu.make_async_remote_copy(
            src_ref=src, dst_ref=dst, send_sem=s, recv_sem=r,
            device_id={"dp": dp, "seq": seq}, device_id_type=MESH,
        )

    barrier = pltpu.get_barrier_semaphore()
    for dp, seq in [(me, other), (near, c), (far, c)] + [(q, c) for q in zs]:
        pl.semaphore_signal(
            barrier, inc=1, device_id={"dp": dp, "seq": seq}, device_id_type=MESH
        )
    pl.semaphore_wait(barrier, 6)

    def al(v, m):
        return pl.multiple_of(v, m)

    class Piece:
        def __init__(self, n, buf, rows, col, half, shards):
            self.n, self.buf, self.rows, self.col, self.half, self.shards = n, buf, rows, col, half, shards

        def cols(self, core):
            return pl.ds(al(self.col + core * self.half, 128), self.half)

        def block(self, o):
            return self.buf.at[pl.ds(al(o * self.rows, 16), self.rows), self.cols(c)]

        def region(self, k, core=c):
            return self.buf.at[pl.ds(0, k * self.rows), self.cols(core)]

        def arrival(self, stage, k):
            return gr.at[stage * 4 + k] if self.n == 0 and stage < 3 else gr.at[12 + self.n * 4 + stage]

        def push(self, src, dst, stage, k, dp):
            send(src, dst, gs.at[self.n], self.arrival(stage, k), dp, c).start()

        def got(self, stage, k, blocks):
            m = self.region(blocks)
            send(m, m, gs.at[self.n], self.arrival(stage, k), me, other).wait_recv()

        def own(self):
            base = pl.ds(al(me * self.rows, 16), self.rows)
            for i, (ref, first, width) in enumerate(self.shards):
                yield (
                    ref.at[:, pl.ds(al(first + c * width, 128), width)],
                    self.buf.at[base, pl.ds(al(self.col + c * self.half + i * width, 128), width)],
                )

        def s1(self):
            for k in range(3):
                for a, b in self.own():
                    self.push(a, b, 0, k + 1, zs[k])
            for a, b in self.own():
                pltpu.make_async_copy(a, b, ls.at[self.n]).start()

        def s2o(self):
            for a, b in self.own():
                self.push(a, b, 1, 0, near)
                self.push(a, b, 2, 0, far)

        def s2(self, k=None):
            if k is None:
                self.got(0, 0, 3)
            else:
                self.got(0, k, 1)

            def one(i, _):
                b = self.block(lax.rem(z + 4 - i, 4) * 4 + xy)
                self.push(b, b, 1, i, near)
                self.push(b, b, 2, i, far)
                return 0

            if k is None:
                lax.fori_loop(1, 4, one, 0)
            else:
                one(k, 0)

        def s3(self, k=None):
            if k is None:
                self.got(1, 0, 4)
            else:
                self.got(1, k, 1)

            def one(i, _):
                b = self.block(lax.rem(z + 4 - i, 4) * 4 + near_xy)
                self.push(b, b, 2, i, far)
                return 0

            if k is None:
                lax.fori_loop(0, 4, one, 0)
            else:
                one(k, 0)

        def s4(self, k=None):
            if k is None:
                self.got(2, 0, 8)
            else:
                self.got(2, k, 2)
            if not k:
                m = self.block(me)
                pltpu.make_async_copy(m, m, ls.at[self.n]).wait()
            if k is None:
                p = self.region(16)
            else:
                p = self.buf.at[pl.ds(al(lax.rem(z + 4 - k, 4) * 4 * self.rows, 16), 4 * self.rows), self.cols(c)]
            send(p, p, gs.at[self.n], self.arrival(3, 0), me, other).start()

        def done(self):
            m = self.region(16, other)
            send(m, m, gs.at[self.n], self.arrival(3, 0), me, other).wait_recv()

        def drain(self):
            m = wide.at[pl.ds(0, 496), pl.ds(0, self.rows * self.half // 16)]
            send(m, m, gs.at[self.n], self.arrival(3, 0), me, other).wait_send()

    near_xy = xy + (1 - c) * (1 - 2 * x) + c * (2 - 4 * y)
    pieces = [
        Piece(g, wide, 48, g * 768, 384, [(win_s, k * D + g * 256, 128) for k in range(3)]) for g in range(3)
    ]
    pieces += [Piece(3, wide, 48, OUT, 384, [(wout_s, 0, 384)])]
    pieces += [Piece(4 + k, wide, 48, EXP + k * 768, 384, [(wexp_s, k * 768, 384)]) for k in range(4)]
    pieces += [Piece(8 + k, wcon, 192, k * 256, 128, [(wcon_s, k * 256, 128)]) for k in range(3)]
    loose = {}

    def run(ops):
        for op in ops:
            name, _, rest = op.partition(":")
            if op in loose:
                loose[op]()
            elif "." in rest:
                p, k = rest.split(".")
                getattr(pieces[int(p)], name)(int(k))
            else:
                getattr(pieces[int(rest)], name)()


    def small(stage, k, recv):
        d = send(vec.at[pl.ds(0, k)], vec.at[pl.ds(0, k)], vs.at[stage], vs.at[3 + stage], me, other)
        d.wait_recv() if recv else d.wait_send()

    swap_tok = send(tokens, tokr, swap_sem.at[0, 0], swap_sem.at[0, 1], me, other)
    swap_cot = send(cot, cotr, swap_sem.at[1, 0], swap_sem.at[1, 1], me, other)
    own_tok = pltpu.make_async_copy(tokens, tok, ls.at[11])
    own_cot = pltpu.make_async_copy(cot, cotn, ls.at[12])
    own_vec = pltpu.make_async_copy(small_s, vec.at[me], ls.at[13])

    own_tok.start()
    own_vec.start()
    for q in zs:
        send(small_s, vec.at[me], vs.at[0], vs.at[3], q, c).start()
    loose["swap"] = swap_tok.start

    def swap_cotangent():
        swap_cot.start()
        own_cot.start()

    loose["swc"] = swap_cotangent

    row = seg[...].astype(F32)
    first_row = jnp.zeros((1, 1), F32)
    for d in range(DOCS):
        size = jnp.sum(jnp.where(row == d, 1.0, 0.0), axis=1, keepdims=True)
        before = jnp.sum(jnp.where(row < d, 1.0, 0.0), axis=1, keepdims=True)
        first_row = first_row + jnp.where(size == T, before, 0.0)
    keep_row = lax.broadcasted_iota(jnp.int32, (1, T), 1).astype(F32) >= first_row
    mine = seg[:, pl.ds(al(c * T, 128), T)].astype(F32)
    theirs = seg[:, pl.ds(al(other * T, 128), T)].astype(F32)
    seg_row = jnp.where(keep_row, mine, theirs)
    seg_col = jnp.broadcast_to(seg_row, (128, T)).T[:, :1]
    keep_col = lax.broadcasted_iota(jnp.int32, (T, 1), 0).astype(F32) >= first_row
    keep_col = jnp.where(keep_col, 1.0, 0.0)
    sc1[...] = jnp.concatenate([keep_col, seg_col], axis=1)

    def fill_mask():
        def mask_rows(i, _):
            r = pl.ds(al(i * 128, 128), 128)
            bias[r, :] = jnp.where(sc1[r, 1:2] == seg_row, 0.0, -1e30)
            return 0

        lax.fori_loop(0, T // 128, mask_rows, 0)

    def fill_start():
        own_tok.wait()
        swap_tok.wait_recv()

        def start_rows(i, _):
            r = pl.ds(al(i * 128, 128), 128)
            t = jnp.where(sc1[r, 0:1] > 0.5, tok[r, :].astype(F32), tokr[r, :].astype(F32)) + te[...]
            n1[r, :] = t
            xl[r, :] = t.astype(BF)
            return 0

        lax.fori_loop(0, T // 128, start_rows, 0)

    def small_near():
        own_vec.wait()
        small(0, 3, True)

        def one(k, _):
            b = vec.at[k * 4 + xy]
            send(b, b, vs.at[1], vs.at[4], near, c).start()
            return 0

        lax.fori_loop(0, 4, one, 0)

    def small_far():
        small(1, 4, True)

        def one(k, _):
            b = vec.at[(k // 2) * 4 + (1 - c) * 2 * y + c * x + lax.rem(k, 2) * (1 + c)]
            send(b, b, vs.at[2], vs.at[5], far, c).start()
            return 0

        lax.fori_loop(0, 8, one, 0)

    def fill_vectors():
        small(2, 8, True)
        for o in range(16):
            fullv[:, o * 48 : (o + 1) * 48] = vec[o][:, :48].astype(F32)
            for k in range(4):
                fulle[:, o * 192 + k * 48 : o * 192 + (k + 1) * 48] = vec[o][k : k + 1, 64:112].astype(F32)
        fullp[...] = jnp.concatenate([jnp.zeros_like(fullp[0:1, :]), jnp.ones_like(fullp[0:1, :])], axis=0)
        for h in range(D // 128):
            fullp[0:1, h * 384 : h * 384 + 128] = fullv[0:1, h * 128 : (h + 1) * 128]
            fullp[0:1, h * 384 + 256 : h * 384 + 384] = fullv[1:2, h * 128 : (h + 1) * 128]
            fullp[1:2, h * 384 : h * 384 + 128] = jnp.full((1, 128), HD**-0.5, F32)

    loose.update({"mask": fill_mask, "start": fill_start, "vec": fill_vectors, "vn": small_near, "vf": small_far})
    run(['s1:0', 's2o:0', 's1:1', 'swap', 's1:2', 's2o:2', 's1:3', 's1:4', 's2o:4', 's2o:3', 's3:0.0', 's2o:1', 's2:0.1', 's2:0.2', 's1:6', 's2:0.3', 'vn', 's1:5', 's3:0.1', 's1:8', 's2o:8', 's2o:5', 's4:0.0', 's3:0.2', 's3:0.3', 'vf', 's4:0.1', 's2:1', 's4:0.2', 's2:2', 's1:7', 's4:0.3', 'start', 'mask', 's3:1', 'vec'])

    def project(g):
        cs = pl.ds(al(g * 768, 768), 768)
        proj[:, cs] = ((nn(xl[...], wide[:, cs]) + fullp[0:1, cs]) * fullp[1:2, cs]).astype(BF)

    lane = lax.broadcasted_iota(jnp.int32, (1, 128), 1)
    halves = (lane < HD, lane >= HD)
    pairs = D // 128

    def keep(h, a):
        return pltpu.make_async_copy(pslot.at[a], spill.at[h * 2 + a], ps.at[a])

    tasks = [
        ['s3:2', 's2:4', 's1:10', 's4:1'],
        [],
        ['s2:5', 's4:2'],
        ['s1:9', 'swc'],
        ['s2:7'],
        ['s4:4'],
    ]
    between = [['s2o:6', 's2:3'], ['s3:3', 's2:6', 's3:4'], ['s3:6', 's3:5', 's2o:7', 's2:8', 's4:3']]

    def attend(h, _):
        for g in range(3):

            @pl.when(h == 2 * g)
            def _():
                pieces[g].done()

        @pl.when(lax.rem(h, 2) == 0)
        def _():
            project(h // 2)

        for g in range(3):
            if between[g]:

                @pl.when(h == 2 * g)
                def _():
                    run(between[g])

        cs = al(h * 384, 128)
        q2 = proj[:, pl.ds(cs, 128)]
        k2 = proj[:, pl.ds(cs + 128, 128)]
        v2 = proj[:, pl.ds(cs + 256, 128)]
        outs = []
        for a in range(2):
            s = nt(jnp.where(halves[a], q2, jnp.zeros_like(q2)), k2) + bias[...]
            e = jnp.exp(s - jnp.max(s, axis=-1, keepdims=True))
            p = (e * (1.0 / jnp.sum(e, axis=-1, keepdims=True))).astype(BF)

            @pl.when(h > 0)
            def _():
                keep(h - 1, a).wait()

            pslot[a] = p
            keep(h, a).start()
            outs.append(nn(p, v2))
        heads[:, pl.ds(al(h * 128, 128), 128)] = jnp.where(halves[0], outs[0], outs[1]).astype(BF)
        for k in range(pairs):

            @pl.when(h == k)
            def _():
                run(tasks[k])

        return 0

    lax.fori_loop(0, pairs, attend, 0)
    pieces[3].done()

    def load(h, a):
        return pltpu.make_async_copy(spill.at[h * 2 + a], pslot.at[a], pd.at[a])

    for a in range(2):
        keep(pairs - 1, a).wait()
        load(0, a).start()

    def normalize(v):
        centred = v - jnp.mean(v, axis=-1, keepdims=True)
        scale = lax.rsqrt(jnp.mean(centred * centred, axis=-1, keepdims=True) + 1e-5)
        return centred * scale, scale

    def first_rows(i, _):
        r = pl.ds(al(i * 256, 256), 256)
        v = n1[r, :] + (nn(heads[r, :], wide[:, OUT:EXP]) + fullv[2:3, :])
        n, s = normalize(v)
        n1[r, :] = n
        sc1[r, 1:2] = s
        fl[r, :] = (n * fullv[3:4, :] + fullv[4:5, :]).astype(BF)
        return 0

    lax.fori_loop(0, T // 256, first_rows, 0)
    run(['s4:6', 's2o:10', 's3:7', 's3:8', 's4:5', 's2o:9'])
    after = [
        [],
        [],
        ['s4:7', 's2:9', 's2:10', 's4:8'],
        ['s3:9'],
    ]
    then = [['s3:10', 's4:9', 's4:10'], [], []]

    def expand(i, _):
        for k in range(4):

            @pl.when(i == k)
            def _():
                pieces[4 + k].done()

        cs = pl.ds(al(i * 768, 768), 768)
        u = nn(fl[...], wide[:, pl.ds(al(EXP + i * 768, 768), 768)]) + fulle[:, cs]
        cdf = 0.5 * (1.0 + lax.erf(u * math.sqrt(0.5)))
        hidden[:, cs] = (u * cdf).astype(BF)
        slope[:, cs] = (cdf + u * jnp.exp(-0.5 * u * u) * (1.0 / math.sqrt(2.0 * math.pi))).astype(BF)
        for k in range(4):

            @pl.when(i == k)
            def _():
                run(after[k])

        return 0

    lax.fori_loop(0, FF // 768, expand, 0)

    def contract(i, _):
        for k in range(3):

            @pl.when(i == k)
            def _():
                pieces[8 + k].done()

        cs = pl.ds(al(i * 256, 256), 256)
        sg[:, cs] = nn(hidden[...], wcon[:, cs]) + fullv[5:6, cs]
        for k in range(3):
            if then[k]:

                @pl.when(i == k)
                def _():
                    run(then[k])

        return 0

    lax.fori_loop(0, D // 256, contract, 0)
    own_cot.wait()
    swap_cot.wait_recv()

    gv[...] = jnp.zeros_like(gv)

    def second_rows(i, _):
        r = pl.ds(al(i * 256, 256), 256)
        v = n1[r, :] * fullv[3:4, :] + fullv[4:5, :] + sg[r, :]
        n, s = normalize(v)
        lonew[r, :] = (n * fullv[6:7, :] + fullv[7:8, :]).astype(BF)
        og = jnp.where(sc1[r, 0:1] > 0.5, cotn[r, :].astype(F32), cotr[r, :].astype(F32))
        gv[6:7, :] += jnp.sum(og * n, axis=0, keepdims=True)
        gv[7:8, :] += jnp.sum(og, axis=0, keepdims=True)
        w = og * fullv[6:7, :]
        g = s * (w - jnp.mean(w, axis=-1, keepdims=True) - n * jnp.mean(w * n, axis=-1, keepdims=True))
        sg[r, :] = g
        low = g.astype(BF)
        bg[r, :] = low
        gv[5:6, :] += jnp.sum(low.astype(F32), axis=0, keepdims=True)
        return 0

    lax.fori_loop(0, T // 256, second_rows, 0)
    swap_lo = send(lonew, lor, swap_sem.at[2, 0], swap_sem.at[2, 1], me, other)
    swap_lo.start()

    S = 384
    my_k = (1 - c) * x + c * y
    far_base = (1 - c) * (2 - 2 * y) + c * (1 - x)
    own_base = (1 - c) * 2 * y + c * x
    step_k = 1 + c

    def total(*refs):
        t = refs[0][...].astype(F32)
        for ref in refs[1:]:
            t = t + ref[...].astype(F32)
        return t

    class Red:
        def __init__(self, n, g, col, rows, recv, rcol, fsum, plane=None, width=384, parts=()):
            self.n, self.g, self.col, self.rows, self.recv, self.rcol, self.fsum = n, g, col, rows, recv, rcol, fsum
            self.plane, self.width, self.parts = plane, width, parts

        def cols(self, core):
            return pl.ds(al(self.col + core * S, 128), self.width)

        def part(self, base, i, k=1, second=False):
            if self.plane is None:
                cs = pl.ds(self.rcol + (self.width if second else 0), self.width)
            else:
                cs = pl.ds(0, S)
                base = base + self.rcol
            return self.recv.at[pl.ds(al(base + i * self.rows, 16), k * self.rows), cs]

        def mine(self, o):
            base = 0 if self.plane is None else self.plane * 4
            return self.g.at[pl.ds(al((base + o) * self.rows, 16), self.rows), self.cols(c)]

        def planes(self):
            return 4 if self.plane is None else 1

        def rp(self, o, k=1):
            return self.part(0, o, k)

        def ra(self, i, k=1):
            return self.part(0 if self.plane is None else 768, i, k, True)

        def rb(self, i, k=1):
            return self.part(384 if self.plane is None else 1152, i, k, True)

        def rz(self, i, k=1):
            if self.plane is None:
                return self.part(576, i, k, True)
            return self.recv.at[pl.ds(al(5376 + i * self.rows, 16), k * self.rows), pl.ds(0, S)]

        def sem(self, stage):
            n = 0 if self.plane is not None and stage == 3 else self.n
            return rs.at[self.n], rr.at[n * 5 + stage]

        def got(self, stage, ref):
            s, r = self.sem(stage)
            send(ref, ref, s, r, me, other).wait_recv()

        def P(self):
            base = 0 if self.plane is None else self.plane * 4 * self.rows
            n = 4 * self.planes() * self.rows
            src = self.g.at[pl.ds(al(base, 16), n), self.cols(other)]
            s, r = self.sem(0)
            send(src, self.rp(0, 4 * self.planes()), s, r, me, other).start()

        def A(self):
            self.got(0, self.rp(0, 4 * self.planes()))
            s, r = self.sem(1)

            def one(i, _):
                o = (i // 2) * 4 + far_base + lax.rem(i, 2) * step_k
                b = self.mine(o)
                b[...] = total(b, self.rp(o)).astype(BF)
                send(b, self.ra(i), s, r, far, c).start()
                return 0

            lax.fori_loop(0, 2 * self.planes(), one, 0)

        def B(self):
            self.got(1, self.ra(0, 2 * self.planes()))
            s, r = self.sem(2)

            def one(i, _):
                o = i * 4 + near_xy
                b = self.mine(o)
                b[...] = total(b, self.rp(o), self.ra(i * 2 + 1 - my_k)).astype(BF)
                send(b, self.rb(i), s, r, near, c).start()
                return 0

            lax.fori_loop(0, self.planes(), one, 0)

        def Z(self):
            self.got(2, self.rb(0, self.planes()))
            s, r = self.sem(3)
            if self.plane is None:
                for k in range(3):
                    p = lax.rem(z + k + 1, 4)
                    b = self.mine(p * 4 + xy)
                    b[...] = total(b, self.rp(p * 4 + xy), self.ra(p * 2 + my_k), self.rb(p)).astype(BF)
                    send(b, self.rz(k), s, r, zs[k], c).start()
            elif self.n > 0:
                b = self.mine(xy)
                b[...] = total(b, self.rp(xy), self.ra(my_k), self.rb(0)).astype(BF)
                send(b, self.rz(self.n - 1), s, r, zs[self.n - 1], c).start()

        def F(self):
            self.got(3, self.rz(0, 3))
            o, p = (z * 4 + xy, z) if self.plane is None else (xy, 0)
            t = total(self.mine(o), self.rp(o), self.ra(p * 2 + my_k), self.rb(p), self.rz(0), self.rz(1), self.rz(2))
            s, r = self.sem(4)
            if self.parts:
                for i, k in enumerate(self.parts):
                    b = self.fsum.at[:, pl.ds(al(k + c * 128, 128), 128)]
                    b[...] = t[:, i * 128 : (i + 1) * 128]
                    send(b, b, s, r, me, other).start()
            else:
                b = self.fsum.at[:, pl.ds(al((self.n - 4 if 4 <= self.n < 8 else 0) * 768 + c * S, 128), S)]
                b[...] = t
                send(b, b, s, r, me, other).start()

        def end(self):
            if self.plane is None:
                m = wide.at[pl.ds(0, 528), pl.ds(0, 3 * self.width)]
            else:
                m = wide.at[pl.ds(0, 576 if self.n == 0 else 512), pl.ds(0, 1152)]
            send(m, m, rs.at[self.n], rr.at[self.n], me, other).wait_send()
            if self.plane is None or self.n == 0:
                self.got(4, self.fsum.at[:, pl.ds(0, self.width)])

    con = {j: Red(j, gcon, 0, 192, con_r, j * 1344, fcon, plane=lax.rem(z + j, 4)) for j in range(4)}
    exp = [Red(4 + k, wide, EXP + k * 768, 48, hidden, k * 768, fexp) for k in range(4)]
    out = Red(8, wide, OUT, 48, cotn, 0, fout)
    ins = [
        Red(9 + k, gin, k * 768, 48, slope, k * 768, fin, parts=[q * D + k * 256 for q in range(3)]) for k in range(2)
    ]
    ins.append(Red(11, gin, 1536, 48, slope, 1536, fin, width=256, parts=[512, D + 512]))
    ins.append(Red(12, gin, 1792, 48, slope, 2048, fin, width=128, parts=[2 * D + 512]))
    sums = {f"C{k}": con[k] for k in range(4)}
    sums.update({f"E{k}": exp[k] for k in range(4)})
    sums.update({f"I{k}": ins[k] for k in range(4)})
    sums["O"] = out

    def reduce(ops):
        for op in ops:
            name, _, rest = op.partition(":")
            if op in loose:
                loose[op]()
            else:
                getattr(sums[rest], name)()

    def steps(i, lists):
        for k, ops in enumerate(lists):
            if ops:

                @pl.when(i == k)
                def _():
                    reduce(ops)

    def send_back():
        def out_rows(i, _):
            r = pl.ds(al(i * 128, 128), 128)
            lonew[r, :] = jnp.where(sc1[r, 0:1] > 0.5, lonew[r, :].astype(F32), lor[r, :].astype(F32)).astype(BF)
            return 0

        swap_lo.wait()
        lax.fori_loop(0, T // 128, out_rows, 0)
        lo_done.start()

    lo_done = pltpu.make_async_copy(lonew, lo_o, ls.at[14])
    loose["lo"] = send_back

    def vsend(stage, src, dst, dp, seq):
        return send(src, dst, rs.at[13 + stage], rr.at[65 + stage], dp, seq)

    def v_partner():
        vout[...] = jnp.zeros_like(vout)
        for o in range(16):
            vout[o, :, 0:48] = gv[0:8, o * 48 : (o + 1) * 48]
            for k in range(4):
                vout[o, k : k + 1, 64:112] = ge[:, o * 192 + k * 48 : o * 192 + (k + 1) * 48]
        vsend(0, vout, vr.at[pl.ds(0, 16)], me, other).start()

    def v_flip_y():
        vsend(0, vout, vr.at[pl.ds(0, 16)], me, other).wait_recv()
        vsum[...] = vout[...] + vr[pl.ds(0, 16)]
        for i in range(8):
            vsend(1, vsum.at[(i // 2) * 4 + 2 - 2 * y + i % 2], vr.at[16 + i], flip_y, c).start()

    def v_flip_x():
        vsend(1, vr.at[pl.ds(16, 8)], vr.at[pl.ds(16, 8)], me, other).wait_recv()
        for i in range(8):
            o = (i // 2) * 4 + 2 * y + i % 2
            vsum[o] = vsum[o] + vr[16 + i]
        for i in range(4):
            vsend(2, vsum.at[i * 4 + 2 * y + 1 - x], vr.at[24 + i], flip_x, c).start()

    def v_planes():
        vsend(2, vr.at[pl.ds(24, 4)], vr.at[pl.ds(24, 4)], me, other).wait_recv()
        for i in range(4):
            vsum[i * 4 + xy] = vsum[i * 4 + xy] + vr[24 + i]
        for k in range(3):
            vsend(3, vsum.at[lax.rem(z + k + 1, 4) * 4 + xy], vr.at[28 + k], zs[k], c).start()

    def v_total():
        vsend(3, vr.at[pl.ds(28, 3)], vr.at[pl.ds(28, 3)], me, other).wait_recv()
        vr[31] = vsum[z * 4 + xy] + vr[28] + vr[29] + vr[30]
        v_done.start()

    v_done = pltpu.make_async_copy(vr.at[31], gvec_o, ls.at[16])
    loose.update({"vP": v_partner, "vA": v_flip_y, "vB": v_flip_x, "vZ": v_planes, "vF": v_total})

    ig_mine, ig_theirs = bg, fl
    swap_ig = [
        send(ig_mine.at[pl.ds(256 * k, 256)], ig_theirs.at[pl.ds(256 * k, 256)], sw3.at[0, k], sw3.at[1, k], me, other)
        for k in range(3)
    ]
    for k in range(3):
        loose[f"swg{k}"] = swap_ig[k].start
    ig_done = pltpu.make_async_copy(sg, ig_o, ls.at[15])

    def take_rows():
        for d in swap_ig:
            d.wait_recv()

        def grad_rows(i, _):
            r = pl.ds(al(i * 128, 128), 128)
            sg[r, :] = jnp.where(sc1[r, 0:1] > 0.5, sg[r, :], ig_theirs[r, :].astype(F32))
            return 0

        lax.fori_loop(0, T // 128, grad_rows, 0)
        ig_done.start()

    loose["sel"] = take_rows

    def grad_con(i, _):
        p = al(lax.rem(z + i + 1, 4) * 768, 768)
        gcon[pl.ds(p, 768), :] = tn(hidden[:, pl.ds(p, 768)], bg[...]).astype(BF)
        steps(i, [['P:C1'], ['P:C2'], ['P:C3', 'A:C1'], ['P:C0']])
        return 0

    lax.fori_loop(0, 4, grad_con, 0)

    def expand_back(i, _):
        cs = pl.ds(al(i * 768, 768), 768)
        g = (nt(bg[...], wcon[cs, :]) * slope[:, cs].astype(F32)).astype(BF)
        slope[:, cs] = g
        ge[:, cs] = jnp.sum(g.astype(F32), axis=0, keepdims=True)
        steps(i, [['A:C3', 'A:C2'], [], [], []])
        return 0

    lax.fori_loop(0, FF // 768, expand_back, 0)

    def first_back(i, _):
        r = pl.ds(al(i * 256, 256), 256)
        g = sg[r, :] + nt(slope[r, :], wide[:, EXP:])
        n = n1[r, :]
        gv[3:4, :] += jnp.sum(g * n, axis=0, keepdims=True)
        gv[4:5, :] += jnp.sum(g, axis=0, keepdims=True)
        w = g * fullv[3:4, :]
        g = sc1[r, 1:2] * (w - jnp.mean(w, axis=-1, keepdims=True) - n * jnp.mean(w * n, axis=-1, keepdims=True))
        sg[r, :] = g
        low = g.astype(BF)
        bg[r, :] = low
        gv[2:3, :] += jnp.sum(low.astype(F32), axis=0, keepdims=True)
        steps(i, [['B:C1'], ['A:C0'], []])
        return 0

    lax.fori_loop(0, T // 256, first_back, 0)
    for p in pieces[4:8]:
        p.drain()

    def grad_exp(i, _):
        cs = pl.ds(al(i * 768, 768), 768)
        wide[:, pl.ds(al(EXP + i * 768, 768), 768)] = tn(fl[...], slope[:, cs]).astype(BF)
        steps(i, [['P:E0', 'B:C3'], ['P:E1', 'B:C2'], ['Z:C1', 'B:C0'], ['P:E3', 'Z:C3', 'A:E0']])
        return 0

    lax.fori_loop(0, 4, grad_exp, 0)
    hg = cotr
    hg[...] = nt(bg[...], wide[:, OUT:EXP]).astype(BF)
    reduce([])
    pieces[3].drain()
    wide[:, OUT:EXP] = tn(heads[...], bg[...]).astype(BF)
    reduce(['P:O', 'A:E1', 'Z:C2', 'P:E2'])

    tasks = [['A:E3'], ['A:O'], ['P:I0', 'B:E3', 'B:E0', 'Z:C0'], ['F:C0', 'B:E1'], ['Z:E0', 'A:I1'], ['Z:E1', 'vP', 'B:E2']]
    after = [[], ['P:I1', 'Z:E3', 'A:E2', 'lo', 'B:O'], []]

    def attend_back(h, _):
        cs = al(h * 384, 128)
        hs = pl.ds(al(h * 128, 128), 128)
        q2 = proj[:, pl.ds(cs, 128)]
        k2 = proj[:, pl.ds(cs + 128, 128)]
        v2 = proj[:, pl.ds(cs + 256, 128)]
        g2 = hg[:, hs]
        prod = g2.astype(F32) * heads[:, hs].astype(F32)
        qt = q2.astype(F32).T.astype(BF)
        gt = g2.astype(F32).T.astype(BF)
        dq, dk, dv = [], [], []
        for a in range(2):
            load(h, a).wait()
            rowdot = jnp.sum(jnp.where(halves[a], prod, 0.0), axis=-1, keepdims=True)
            p = pslot[a]
            dp = nt(jnp.where(halves[a], g2, jnp.zeros_like(g2)), v2)
            ds = (p.astype(F32) * (dp - rowdot)).astype(BF)
            dq.append(nn(ds, k2))
            dk.append(nn(qt[a * HD : (a + 1) * HD], ds))
            dv.append(nn(gt[a * HD : (a + 1) * HD], p))

            @pl.when(h + 1 < pairs)
            def _():
                load(h + 1, a).start()

        dq = (jnp.where(halves[0], dq[0], dq[1]) * HD**-0.5).astype(BF)
        dk = jnp.concatenate(dk, axis=0).T.astype(BF)
        dv = jnp.concatenate(dv, axis=0).T.astype(BF)
        proj[:, pl.ds(cs, 128)] = dq
        proj[:, pl.ds(cs + 128, 128)] = dk
        proj[:, pl.ds(cs + 256, 128)] = dv
        gv[0:1, hs] = jnp.sum(dq.astype(F32), axis=0, keepdims=True)
        gv[1:2, hs] = jnp.sum(dv.astype(F32), axis=0, keepdims=True)

        steps(h, tasks)

        @pl.when(lax.rem(h, 2) == 1)
        def _():
            cols = pl.ds(al((h // 2) * 768, 768), 768)
            gin[:, cols] = tn(xl[...], proj[:, cols]).astype(BF)

        steps((h - 1) // 2 + 8 * (1 - lax.rem(h, 2)), after)
        return 0

    lax.fori_loop(0, pairs, attend_back, 0)

    def input_rows(i, _):
        r = pl.ds(al(i * 256, 256), 256)
        g = sg[r, :] + nt(proj[r, :], wide[:, IN:OUT])
        sg[r, :] = g
        ig_mine[r, :] = g.astype(BF)
        steps(i, [['Z:O', 'A:I0', 'P:I2'], [], ['Z:E2', 'B:I1', 'P:I3', 'swg0', 'A:I3', 'swg1', 'F:E0', 'F:E3', 'F:O', 'B:I0', 'Z:I1', 'A:I2', 'vA', 'swg2', 'F:E2', 'Z:I0', 'B:I3', 'B:I2', 'Z:I3', 'vB', 'sel', 'Z:I2', 'F:I0', 'vZ', 'F:I3', 'F:E1', 'F:I1', 'F:I2', 'vF']])
        return 0

    lax.fori_loop(0, T // 256, input_rows, 0)
    outs = [lo_done, ig_done, v_done]
    for k, (v, o) in enumerate([(fcon, gcon_o), (fexp, gexp_o), (fout, gout_o), (fin, gin_o)]):
        for p in [[con[0]], exp, [out], ins][k]:
            p.end()
        outs.append(pltpu.make_async_copy(v, o, ls.at[17 + k]))
        outs[-1].start()
    for k in (1, 2, 3):
        con[k].end()
    swap_tok.wait_send()
    swap_cot.wait_send()
    for d in swap_ig:
        d.wait_send()
    for p in pieces[0:3] + pieces[8:]:
        p.drain()
    for stage, k in ((0, 3), (1, 4), (2, 8)):
        small(stage, k, False)
        m = vr.at[pl.ds(0, (8, 4, 3)[stage])]
        vsend(stage + 1, m, m, me, other).wait_send()
    vsend(0, vout, vr.at[pl.ds(0, 16)], me, other).wait_send()
    for o in outs:
        o.wait()


def fused_layer(tokens, time_embed, segments, iw, ow, ew, cw, small, cot):
    T, D = tokens.shape
    FF = ew.shape[1]
    sh = jax.ShapeDtypeStruct
    anyspec = pl.BlockSpec(memory_space=pl.ANY)
    vspec = pl.BlockSpec(memory_space=VM)
    scratch = [
        VM((D, 4 * D + FF), BF), VM((FF, D), BF),
        VM((T, D), BF), VM((T, D), BF), VM((T, D), BF), VM((T, D), BF),
        VM((16, 16, 128), BF), VM((16, D), F32), VM((1, FF), F32), VM((2, 3 * D), F32),
        VM((T, 3 * D), BF), VM((T, D), BF), VM((T, D), F32), VM((T, T), F32),
        VM((T, 2), F32), VM((T, D), BF), VM((T, D), BF), VM((T, FF), BF), VM((T, FF), BF),
        VM((2, T, T), BF), VM((T, D), BF),
        VM((D, 3 * D), BF), VM((FF, D), BF), VM((5952, 384), BF), VM((8, D), F32), VM((1, FF), F32),
        VM((16, 8, 128), F32), VM((16, 8, 128), F32), VM((32, 8, 128), F32),
        VM(iw.shape, F32), VM(ow.shape, F32), VM(ew.shape, F32), VM(cw.shape, F32),
        DMA((3, 2)), DMA((2, 3)), DMA((21,)), DMA((11,)), DMA((56,)), DMA((6,)), DMA((2,)), DMA((17,)), DMA((69,)), DMA((2,)),
    ]
    return pl.pallas_call(
        fused_kernel,
        out_shape=(
            sh((T, D), BF), sh((T, D), F32), sh(iw.shape, F32), sh(ow.shape, F32), sh(ew.shape, F32),
            sh(cw.shape, F32), sh((8, 128), F32), sh((D // HD, T, T), BF),
        ),
        in_specs=[anyspec, anyspec, vspec, vspec, anyspec, anyspec, anyspec, anyspec, anyspec],
        out_specs=(anyspec,) * 8,
        scratch_shapes=scratch,
        compiler_params=pltpu.CompilerParams(
            collective_id=0, has_side_effects=True, vmem_limit_bytes=67043328
        ),
    )(tokens, cot, time_embed, segments, iw, ow, ew, cw, small)


epsilon = 1e-05
masked_score = -1e30


def matmul(left, right):
    return jnp.dot(left, right, preferred_element_type=jnp.float32)


def product_tn(left, right):
    return lax.dot_general(
        left, right, (((0,), (0,)), ((), ())), preferred_element_type=jnp.float32
    )


def product_nt(left, right):
    return lax.dot_general(
        left, right, (((1,), (1,)), ((), ())), preferred_element_type=jnp.float32
    )


def normalize(values):
    mean = jnp.mean(values, axis=-1, keepdims=True)
    centred = values - mean
    scale = lax.rsqrt(jnp.mean(centred * centred, axis=-1, keepdims=True) + epsilon)
    return (centred * scale, scale)


def norm_back(grad, normed, scale, gain):
    scaled = grad * gain
    return scale * (
        scaled
        - jnp.mean(scaled, axis=-1, keepdims=True)
        - normed * jnp.mean(scaled * normed, axis=-1, keepdims=True)
    )


def gelu_value(values):
    return 0.5 * values * (1.0 + lax.erf(values * math.sqrt(0.5)))


def gelu_slope(values):
    return 0.5 * (1.0 + lax.erf(values * math.sqrt(0.5))) + values * jnp.exp(
        -0.5 * values * values
    ) / math.sqrt(2.0 * math.pi)


def attend_forward(item):
    query, key, value, segment_row = item
    length, depth = query.shape
    block = min(512, length)
    blocks = length // block
    scale = depth ** (-0.5)

    def one_block(part):
        query_block, segment_block = part
        scores = product_nt(query_block, key) * scale
        scores = jnp.where(segment_block[:, None] == segment_row[None, :], scores, masked_score)
        top = jnp.max(scores, axis=-1, keepdims=True)
        expo = jnp.exp(scores - top)
        total = jnp.sum(expo, axis=-1, keepdims=True)
        probs_low = (expo / total).astype(jnp.bfloat16)
        return (matmul(probs_low, value).astype(jnp.bfloat16), (top + jnp.log(total))[:, 0])

    outputs, logsum = lax.map(
        one_block, (query.reshape(blocks, block, depth), segment_row.reshape(blocks, block))
    )
    return (outputs.reshape(length, depth), logsum.reshape(length))


def attend_backward(item):
    query, key, value, segment_row, logsum, out_grad = item
    length, depth = query.shape
    block = min(512, length)
    blocks = length // block
    scale = depth ** (-0.5)

    def one_block(carry, part):
        key_grad, value_grad = carry
        query_block, segment_block, logsum_block, grad_block = part
        scores = product_nt(query_block, key) * scale
        scores = jnp.where(segment_block[:, None] == segment_row[None, :], scores, masked_score)
        probs = jnp.exp(scores - logsum_block[:, None])
        probs_low = probs.astype(jnp.bfloat16)
        prob_grad = product_nt(grad_block, value)
        row_total = jnp.sum(probs * prob_grad, axis=-1, keepdims=True)
        score_grad = (probs * (prob_grad - row_total)).astype(jnp.bfloat16)
        query_grad = matmul(score_grad, key) * scale
        key_grad = key_grad + product_tn(score_grad, query_block) * scale
        value_grad = value_grad + product_tn(probs_low, grad_block)
        return ((key_grad, value_grad), query_grad.astype(jnp.bfloat16))

    zeros = jnp.zeros((length, depth), jnp.float32)
    parts = (
        query.reshape(blocks, block, depth),
        segment_row.reshape(blocks, block),
        logsum.reshape(blocks, block),
        out_grad.reshape(blocks, block, depth),
    )
    (key_grad, value_grad), query_grad = lax.scan(one_block, (zeros, zeros), parts)
    return (
        query_grad.reshape(length, depth),
        key_grad.astype(jnp.bfloat16),
        value_grad.astype(jnp.bfloat16),
    )


def plain_body(
    tokens,
    time_embed,
    segments,
    input_weight,
    query_bias,
    value_bias,
    output_weight,
    output_bias,
    first_gain,
    first_shift,
    expand_weight,
    expand_bias,
    contract_weight,
    contract_bias,
    second_gain,
    second_shift,
    cotangent,
):
    pairs = lax.axis_size("seq")
    seqs, half, width = tokens.shape
    length = half * pairs
    rows = seqs * half
    group = width // pairs
    heads_here = group // HD
    start = (tokens.astype(jnp.float32) + time_embed[:, None, :]).reshape(rows, width)
    start_low = start.astype(jnp.bfloat16)
    attention_set = (
        lax.all_gather(input_weight, "dp", axis=0, tiled=True),
        lax.all_gather(output_weight, "dp", axis=0, tiled=True),
        lax.all_gather(query_bias, "dp", axis=0, tiled=True),
        lax.all_gather(value_bias, "dp", axis=0, tiled=True),
        lax.all_gather(output_bias, "dp", axis=0, tiled=True),
        lax.all_gather(first_gain, "dp", axis=0, tiled=True),
        lax.all_gather(first_shift, "dp", axis=0, tiled=True),
    )
    (
        full_input,
        full_output,
        full_query_bias,
        full_value_bias,
        full_output_bias,
        full_first_gain,
        full_first_shift,
    ) = attention_set
    bias_row = jnp.concatenate(
        [
            full_query_bias.astype(jnp.float32),
            jnp.zeros((width,), jnp.float32),
            full_value_bias.astype(jnp.float32),
        ]
    )
    projected_low = (matmul(start_low, full_input) + bias_row).astype(jnp.bfloat16)
    regrouped = lax.all_to_all(
        projected_low.reshape(seqs, half, 3, pairs, group),
        "seq",
        split_axis=3,
        concat_axis=1,
        tiled=True,
    )
    split = regrouped.reshape(seqs, length, 3, heads_here, HD).transpose(2, 0, 3, 1, 4)
    split = split.reshape(3, seqs * heads_here, length, HD)
    query_heads, key_heads, value_heads = (split[0], split[1], split[2])
    segment_heads = jnp.repeat(segments, heads_here, axis=0)
    heads_out, logsum = lax.map(
        attend_forward, (query_heads, key_heads, value_heads, segment_heads)
    )
    heads_tokens = (
        heads_out.reshape(seqs, heads_here, length, HD)
        .transpose(0, 2, 1, 3)
        .reshape(seqs, length, 1, group)
    )
    heads_low = lax.all_to_all(
        heads_tokens, "seq", split_axis=1, concat_axis=2, tiled=True
    ).reshape(rows, width)
    attention = matmul(heads_low, full_output) + full_output_bias.astype(jnp.float32)
    normed_one, scale_one = normalize(start + attention)
    gain_one = full_first_gain.astype(jnp.float32)
    first = normed_one * gain_one + full_first_shift.astype(jnp.float32)
    first_low = first.astype(jnp.bfloat16)
    network_set = (
        lax.all_gather(expand_weight, "dp", axis=0, tiled=True),
        lax.all_gather(contract_weight, "dp", axis=0, tiled=True),
        lax.all_gather(expand_bias, "dp", axis=0, tiled=True),
        lax.all_gather(contract_bias, "dp", axis=0, tiled=True),
        lax.all_gather(second_gain, "dp", axis=0, tiled=True),
        lax.all_gather(second_shift, "dp", axis=0, tiled=True),
    )
    (
        full_expand,
        full_contract,
        full_expand_bias,
        full_contract_bias,
        full_second_gain,
        full_second_shift,
    ) = network_set
    expand = matmul(first_low, full_expand) + full_expand_bias.astype(jnp.float32)
    hidden = gelu_value(expand).astype(jnp.bfloat16)
    second_sum = first + matmul(hidden, full_contract) + full_contract_bias.astype(jnp.float32)
    normed_two, scale_two = normalize(second_sum)
    gain_two = full_second_gain.astype(jnp.float32)
    layer_output = (normed_two * gain_two + full_second_shift.astype(jnp.float32)).astype(
        jnp.bfloat16
    )
    network_set = (
        lax.all_gather(expand_weight, "dp", axis=0, tiled=True),
        lax.all_gather(contract_weight, "dp", axis=0, tiled=True),
        lax.all_gather(expand_bias, "dp", axis=0, tiled=True),
        lax.all_gather(contract_bias, "dp", axis=0, tiled=True),
        lax.all_gather(second_gain, "dp", axis=0, tiled=True),
        lax.all_gather(second_shift, "dp", axis=0, tiled=True),
    )
    full_expand, full_contract = (network_set[0], network_set[1])
    out_grad = cotangent.astype(jnp.float32).reshape(rows, width)
    grad_second_gain = jnp.sum(out_grad * normed_two, axis=0)
    grad_second_shift = jnp.sum(out_grad, axis=0)
    second_grad = norm_back(out_grad, normed_two, scale_two, gain_two)
    branch_grad = second_grad.astype(jnp.bfloat16)
    grad_contract_bias = jnp.sum(branch_grad.astype(jnp.float32), axis=0)
    grad_contract_weight = product_tn(hidden, branch_grad)
    expand_grad = (product_nt(branch_grad, full_contract) * gelu_slope(expand)).astype(jnp.bfloat16)
    grad_expand_bias = jnp.sum(expand_grad.astype(jnp.float32), axis=0)
    grad_expand_weight = product_tn(first_low, expand_grad)
    first_grad = second_grad + product_nt(expand_grad, full_expand)
    grad_first_gain = jnp.sum(first_grad * normed_one, axis=0)
    grad_first_shift = jnp.sum(first_grad, axis=0)
    start_grad = norm_back(first_grad, normed_one, scale_one, gain_one)
    attention_set = (
        lax.all_gather(input_weight, "dp", axis=0, tiled=True),
        lax.all_gather(output_weight, "dp", axis=0, tiled=True),
        lax.all_gather(query_bias, "dp", axis=0, tiled=True),
        lax.all_gather(value_bias, "dp", axis=0, tiled=True),
        lax.all_gather(output_bias, "dp", axis=0, tiled=True),
        lax.all_gather(first_gain, "dp", axis=0, tiled=True),
        lax.all_gather(first_shift, "dp", axis=0, tiled=True),
    )
    full_input, full_output = (attention_set[0], attention_set[1])
    attention_grad = start_grad.astype(jnp.bfloat16)
    grad_output_bias = jnp.sum(attention_grad.astype(jnp.float32), axis=0)
    grad_output_weight = product_tn(heads_low, attention_grad)
    heads_grad = product_nt(attention_grad, full_output).astype(jnp.bfloat16)
    grad_heads = lax.all_to_all(
        heads_grad.reshape(seqs, half, pairs, group), "seq", split_axis=2, concat_axis=1, tiled=True
    )
    grad_heads = (
        grad_heads.reshape(seqs, length, heads_here, HD)
        .transpose(0, 2, 1, 3)
        .reshape(seqs * heads_here, length, HD)
    )
    query_grad, key_grad, value_grad = lax.map(
        attend_backward, (query_heads, key_heads, value_heads, segment_heads, logsum, grad_heads)
    )
    stacked = jnp.stack([query_grad, key_grad, value_grad]).reshape(3, seqs, heads_here, length, HD)
    stacked = stacked.transpose(1, 3, 0, 2, 4).reshape(seqs, length, 3, 1, group)
    projected_grad = lax.all_to_all(
        stacked, "seq", split_axis=1, concat_axis=3, tiled=True
    ).reshape(rows, 3 * width)
    grad_query_bias = jnp.sum(projected_grad[:, :width].astype(jnp.float32), axis=0)
    grad_value_bias = jnp.sum(projected_grad[:, 2 * width :].astype(jnp.float32), axis=0)
    grad_input_weight = product_tn(start_low, projected_grad)
    input_grad = (start_grad + product_nt(projected_grad, full_input)).reshape(seqs, half, width)
    grads = (
        grad_input_weight,
        grad_query_bias,
        grad_value_bias,
        grad_output_weight,
        grad_output_bias,
        grad_first_gain,
        grad_first_shift,
        grad_expand_weight,
        grad_expand_bias,
        grad_contract_weight,
        grad_contract_bias,
        grad_second_gain,
        grad_second_shift,
    )
    owned = (
        lax.psum_scatter(grads[0], "dp", scatter_dimension=0, tiled=True),
        lax.psum_scatter(grads[1], "dp", scatter_dimension=0, tiled=True),
        lax.psum_scatter(grads[2], "dp", scatter_dimension=0, tiled=True),
        lax.psum_scatter(grads[3], "dp", scatter_dimension=0, tiled=True),
        lax.psum_scatter(grads[4], "dp", scatter_dimension=0, tiled=True),
        lax.psum_scatter(grads[5], "dp", scatter_dimension=0, tiled=True),
        lax.psum_scatter(grads[6], "dp", scatter_dimension=0, tiled=True),
        lax.psum_scatter(grads[7], "dp", scatter_dimension=0, tiled=True),
        lax.psum_scatter(grads[8], "dp", scatter_dimension=0, tiled=True),
        lax.psum_scatter(grads[9], "dp", scatter_dimension=0, tiled=True),
        lax.psum_scatter(grads[10], "dp", scatter_dimension=0, tiled=True),
        lax.psum_scatter(grads[11], "dp", scatter_dimension=0, tiled=True),
        lax.psum_scatter(grads[12], "dp", scatter_dimension=0, tiled=True),
    )
    summed = (
        lax.psum(owned[0].astype(jnp.bfloat16), "seq").astype(jnp.float32),
        lax.psum(owned[1].astype(jnp.bfloat16), "seq").astype(jnp.float32),
        lax.psum(owned[2].astype(jnp.bfloat16), "seq").astype(jnp.float32),
        lax.psum(owned[3].astype(jnp.bfloat16), "seq").astype(jnp.float32),
        lax.psum(owned[4].astype(jnp.bfloat16), "seq").astype(jnp.float32),
        lax.psum(owned[5].astype(jnp.bfloat16), "seq").astype(jnp.float32),
        lax.psum(owned[6].astype(jnp.bfloat16), "seq").astype(jnp.float32),
        lax.psum(owned[7].astype(jnp.bfloat16), "seq").astype(jnp.float32),
        lax.psum(owned[8].astype(jnp.bfloat16), "seq").astype(jnp.float32),
        lax.psum(owned[9].astype(jnp.bfloat16), "seq").astype(jnp.float32),
        lax.psum(owned[10].astype(jnp.bfloat16), "seq").astype(jnp.float32),
        lax.psum(owned[11].astype(jnp.bfloat16), "seq").astype(jnp.float32),
        lax.psum(owned[12].astype(jnp.bfloat16), "seq").astype(jnp.float32),
    )
    return (layer_output.reshape(seqs, half, width), input_grad) + tuple(summed)


def finish_kernel(lo, ig, gi, go, ge, gc, vec, lo_o, ig_o, gi_o, go_o, ge_o, gc_o, *rest):
    small, bufs, sems = rest[:9], rest[9:15], rest[15]
    pairs = list(zip((ig, lo, ge, gi, gc, go), (bufs[1], bufs[0], bufs[4], bufs[2], bufs[5], bufs[3])))
    results = (ig_o, lo_o, ge_o, gi_o, gc_o, go_o)
    loads = [pltpu.make_async_copy(a, b, sems.at[0, k]) for k, (a, b) in enumerate(pairs)]
    stores = [pltpu.make_async_copy(b, r, sems.at[1, k]) for k, ((_, b), r) in enumerate(zip(pairs, results))]
    for d in loads:
        d.start()
    own = small[0].shape[1]
    for k in range(8):
        small[k][...] = vec[k : k + 1, :own]
    for k in range(4):
        small[8][:, k * own : (k + 1) * own] = vec[k : k + 1, 64 : 64 + own]
    for a, b in zip(loads, stores):
        a.wait()
        b.start()
    for b in stores:
        b.wait()


def finish(lo, ig, gi, go, ge, gc, vec, own):
    sh = jax.ShapeDtypeStruct
    anyspec = pl.BlockSpec(memory_space=pl.ANY)
    vspec = pl.BlockSpec(memory_space=VM)
    big = (lo, ig, gi, go, ge, gc)
    return pl.pallas_call(
        finish_kernel,
        out_shape=[sh(v.shape, v.dtype) for v in big] + [sh((1, own), F32)] * 8 + [sh((1, 4 * own), F32)],
        in_specs=[anyspec] * 6 + [vspec],
        out_specs=[anyspec] * 6 + [vspec] * 9,
        scratch_shapes=[VM(v.shape, v.dtype) for v in big] + [DMA((2, 6))],
    )(*big, vec)


def fused_body(
    tokens, time_embed, segments, input_weight, query_bias, value_bias, output_weight, output_bias, first_gain,
    first_shift, expand_weight, expand_bias, contract_weight, contract_bias, second_gain, second_shift, cotangent,
):
    vectors = [
        query_bias, value_bias, output_bias, first_gain, first_shift, contract_bias, second_gain, second_shift,
    ]
    own = query_bias.shape[0]
    small = jnp.pad(jnp.stack(vectors), ((0, 8), (0, 64 - own)))
    wide = jnp.pad(expand_bias.reshape(4, own), ((0, 12), (0, 64 - own)))
    small = jnp.concatenate([small, wide], axis=1)
    parts = fused_layer(
        tokens[0], time_embed, segments, input_weight, output_weight, expand_weight, contract_weight, small,
        cotangent[0],
    )[:7]
    layer_output, input_grad, g_in, g_out, g_exp, g_con, *row = finish(*parts, own)
    row = [v.reshape(v.shape[1]) for v in row]
    return (
        layer_output[None], input_grad[None], g_in, row[0], row[1], g_out, row[2], row[3], row[4],
        g_exp, row[8], g_con, row[5], row[6], row[7],
    )


def body(*args):
    if lax.axis_size("dp") == 16 and lax.axis_size("seq") == 2:
        return fused_body(*args)
    return plain_body(*args)


def solution(mesh):
    return jax.shard_map(
        body,
        mesh=mesh,
        in_specs=(
            P("dp", "seq", None),
            P("dp", None),
            P("dp", None),
            P("dp", None),
            P("dp"),
            P("dp"),
            P("dp", None),
            P("dp"),
            P("dp"),
            P("dp"),
            P("dp", None),
            P("dp"),
            P("dp", None),
            P("dp"),
            P("dp"),
            P("dp"),
            P("dp", "seq", None),
        ),
        out_specs=(
            P("dp", "seq", None),
            P("dp", "seq", None),
            P("dp", None),
            P("dp"),
            P("dp"),
            P("dp", None),
            P("dp"),
            P("dp"),
            P("dp"),
            P("dp", None),
            P("dp"),
            P("dp", None),
            P("dp"),
            P("dp"),
            P("dp"),
        ),
        check_vma=False,
    )
```

```python
import functools
import math

import jax
import jax.numpy as jnp
from jax import lax
from jax.experimental import pallas as pl
from jax.experimental.pallas import tpu as pltpu
from jax.sharding import PartitionSpec as P

HD = 64
DOCS = 4
BF = jnp.bfloat16
F32 = jnp.float32
MESH = pl.DeviceIdType.MESH
VM = pltpu.VMEM
DMA = pltpu.SemaphoreType.DMA


def nn(a, b):
    return jnp.dot(a, b, preferred_element_type=F32)


def nt(a, b):
    return lax.dot_general(a, b, (((1,), (1,)), ((), ())), preferred_element_type=F32)


def tn(a, b):
    return lax.dot_general(a, b, (((0,), (0,)), ((), ())), preferred_element_type=F32)


def fused_kernel(
    tokens, cot, te, seg, win_s, wout_s, wexp_s, wcon_s, v0, v1, v2, v3, v4, v5, v6, v7, v8,
    lo_o, ig_o, gin_o, gout_o, gexp_o, gcon_o, gvec_o, spill,
    wide, wcon, tok, tokr, cotn, cotr, vec, pack, fullv, fulle, fullp, proj, xl, n1, sg,
    sc1, heads, fl, hidden, slope, pslot, bg,
    gin, gcon, con_r, gv, ge, vout, vsum, vr, fin, fout, fexp, fcon,
    swap_sem, sw3, ls, gs, gr, vs, ps, rs, rr, pd,
):
    vectors = (v0, v1, v2, v3, v4, v5, v6, v7, v8)
    T, D = tok.shape
    FF = wcon.shape[0]
    IN, OUT, EXP = 0, 3 * D, 4 * D
    bias, lonew, lor = sg, tok, tokr
    me = lax.axis_index("dp")
    c = lax.axis_index("seq")
    x = lax.rem(me, 2)
    y = lax.rem(me // 2, 2)
    xy = lax.rem(me, 4)
    z = me // 4
    flip_x = me + 1 - 2 * x
    flip_y = me + 2 - 4 * y
    near = (1 - c) * flip_x + c * flip_y
    far = (1 - c) * flip_y + c * flip_x
    other = 1 - c
    zs = [lax.rem(z + k, 4) * 4 + xy for k in (1, 2, 3)]

    def send(src, dst, s, r, dp, seq):
        return pltpu.make_async_remote_copy(
            src_ref=src, dst_ref=dst, send_sem=s, recv_sem=r,
            device_id={"dp": dp, "seq": seq}, device_id_type=MESH,
        )

    barrier = pltpu.get_barrier_semaphore()
    for dp, seq in [(me, other), (near, c), (far, c)] + [(q, c) for q in zs]:
        pl.semaphore_signal(
            barrier, inc=1, device_id={"dp": dp, "seq": seq}, device_id_type=MESH
        )

    def al(v, m):
        return pl.multiple_of(v, m)

    class Piece:
        def __init__(self, n, buf, rows, col, half, shards, whole=None):
            self.n, self.buf, self.rows, self.col, self.half, self.shards = n, buf, rows, col, half, shards
            self.whole = whole
            self.low = 1 if whole is None else 2

        def cols(self, core):
            return pl.ds(al(self.col + core * self.half, 128), self.half)

        def block(self, o):
            return self.buf.at[pl.ds(al(o * self.rows, 16), self.rows), self.cols(c)]

        def region(self, k, core=c):
            return self.buf.at[pl.ds(0, k * self.rows), self.cols(core)]

        def arrival(self, stage, k):
            if stage > 3:
                return gr.at[56 + self.whole * 3 + stage - 4]
            return gr.at[stage * 4 + k] if self.n == 0 and stage < 3 else gr.at[12 + self.n * 4 + stage]

        def push(self, src, dst, stage, k, dp):
            send(src, dst, gs.at[self.n], self.arrival(stage, k), dp, c).start()

        def got(self, stage, k, blocks):
            m = self.region(blocks)
            send(m, m, gs.at[self.n], self.arrival(stage, k), me, other).wait_recv()

        def own(self):
            base = pl.ds(al(me * self.rows, 16), self.rows)
            for i, (ref, first, width) in enumerate(self.shards):
                yield (
                    ref.at[:, pl.ds(al(first + c * width, 128), width)],
                    self.buf.at[base, pl.ds(al(self.col + c * self.half + i * width, 128), width)],
                )

        def s1(self):
            for k in range(self.low - 1, 3):
                for a, b in self.own():
                    self.push(a, b, 0, k + 1, zs[k])
            for a, b in self.own():
                pltpu.make_async_copy(a, b, ls.at[self.n]).start()

        def s2o(self):
            for a, b in self.own():
                self.push(a, b, 1 if self.whole is None else 4, 0, near)
                self.push(a, b, 2 if self.whole is None else 5, 0, far)

        def s2n(self):
            self.got(4, 0, 1)
            b = self.block(z * 4 + near_xy)
            self.push(b, b, 5, 0, far)

        def s5(self):
            self.got(5, 0, 2)
            m = self.block(me)
            pltpu.make_async_copy(m, m, ls.at[self.n]).wait()
            p = self.buf.at[pl.ds(al(z * 4 * self.rows, 16), 4 * self.rows), self.cols(c)]
            self.push(p, p, 6, 0, zs[0])

        def s2(self, k=None):
            if k is None:
                self.got(0, 0, 4 - self.low)
            else:
                self.got(0, k, 1)

            def one(i, _):
                b = self.block(lax.rem(z + 4 - i, 4) * 4 + xy)
                self.push(b, b, 1, i, near)
                self.push(b, b, 2, i, far)
                return 0

            if k is None:
                lax.fori_loop(self.low, 4, one, 0)
            else:
                one(k, 0)

        def s3(self, k=None):
            if k is None:
                self.got(1, 0, 4 if self.whole is None else 2)
            else:
                self.got(1, k, 1)

            def one(i, _):
                b = self.block(lax.rem(z + 4 - i, 4) * 4 + near_xy)
                self.push(b, b, 2, i, far)
                return 0

            if k is None:
                lax.fori_loop(0 if self.whole is None else 2, 4, one, 0)
            else:
                one(k, 0)

        def s4(self, k=None):
            if k is None:
                self.got(2, 0, 8 if self.whole is None else 4)
            else:
                self.got(2, k, 2)
            if self.whole is not None:
                self.got(6, 0, 4)
            elif not k:
                m = self.block(me)
                pltpu.make_async_copy(m, m, ls.at[self.n]).wait()
            if k is None:
                p = self.region(16)
            else:
                p = self.buf.at[pl.ds(al(lax.rem(z + 4 - k, 4) * 4 * self.rows, 16), 4 * self.rows), self.cols(c)]
            send(p, p, gs.at[self.n], self.arrival(3, 0), me, other).start()

        def done(self):
            m = self.region(16, other)
            send(m, m, gs.at[self.n], self.arrival(3, 0), me, other).wait_recv()

        def drain(self):
            m = wide.at[pl.ds(0, 496), pl.ds(0, self.rows * self.half // 16)]
            send(m, m, gs.at[self.n], self.arrival(3, 0), me, other).wait_send()

    near_xy = xy + (1 - c) * (1 - 2 * x) + c * (2 - 4 * y)
    whole = {8: 0, 9: 1, 10: 2}
    pieces = []
    for n in range(11):
        if n < 3:
            spec = (wide, 48, n * 768, 384, [(win_s, k * D + n * 256, 128) for k in range(3)])
        elif n == 3:
            spec = (wide, 48, OUT, 384, [(wout_s, 0, 384)])
        elif n < 8:
            spec = (wide, 48, EXP + (n - 4) * 768, 384, [(wexp_s, (n - 4) * 768, 384)])
        else:
            spec = (wcon, 192, (n - 8) * 256, 128, [(wcon_s, (n - 8) * 256, 128)])
        pieces.append(Piece(n, *spec, whole=whole.get(n)))

    loose = {}

    def run(ops):
        for op in ops:
            name, _, rest = op.partition(":")
            if op in loose:
                loose[op]()
            elif "." in rest:
                p, k = rest.split(".")
                getattr(pieces[int(p)], name)(int(k))
            else:
                getattr(pieces[int(rest)], name)()


    def small(stage, k, recv):
        d = send(vec.at[pl.ds(0, k)], vec.at[pl.ds(0, k)], vs.at[stage], vs.at[3 + stage], me, other)
        d.wait_recv() if recv else d.wait_send()

    swap_tok = send(tokens, tokr, swap_sem.at[0, 0], swap_sem.at[0, 1], me, other)
    swap_cot = send(cot, cotr, swap_sem.at[1, 0], swap_sem.at[1, 1], me, other)
    own_tok = pltpu.make_async_copy(tokens, tok, ls.at[11])
    own_cot = pltpu.make_async_copy(cot, cotn, ls.at[12])

    own_tok.start()
    pack[...] = jnp.zeros_like(pack)
    for k in range(8):
        pack[k : k + 1, 0:48] = vectors[k][...].astype(F32)
    for k in range(4):
        pack[k : k + 1, 64:112] = vectors[8][:, k * 48 : (k + 1) * 48].astype(F32)
    vec[me] = pack[...].astype(BF)

    row = seg[...].astype(F32)
    first_row = jnp.zeros((1, 1), F32)
    for d in range(DOCS):
        size = jnp.sum(jnp.where(row == d, 1.0, 0.0), axis=1, keepdims=True)
        before = jnp.sum(jnp.where(row < d, 1.0, 0.0), axis=1, keepdims=True)
        first_row = first_row + jnp.where(size == T, before, 0.0)
    keep_row = lax.broadcasted_iota(jnp.int32, (1, T), 1).astype(F32) >= first_row
    mine = seg[:, pl.ds(al(c * T, 128), T)].astype(F32)
    theirs = seg[:, pl.ds(al(other * T, 128), T)].astype(F32)
    seg_row = jnp.where(keep_row, mine, theirs)
    seg_col = jnp.broadcast_to(seg_row, (128, T)).T[:, :1]
    keep_col = lax.broadcasted_iota(jnp.int32, (T, 1), 0).astype(F32) >= first_row
    keep_col = jnp.where(keep_col, 1.0, 0.0)
    sc1[...] = jnp.concatenate([keep_col, seg_col], axis=1)

    def mask_rows(i, _):
        r = pl.ds(al(i * 128, 128), 128)
        bias[r, :] = jnp.where(sc1[r, 1:2] == seg_row, 0.0, -1e30)
        return 0

    lax.fori_loop(0, T // 128, mask_rows, 0)
    pl.semaphore_wait(barrier, 6)
    for q in zs:
        send(vec.at[me], vec.at[me], vs.at[0], vs.at[3], q, c).start()
    loose["swap"] = swap_tok.start

    def swap_cotangent():
        swap_cot.start()
        own_cot.start()

    loose["swc"] = swap_cotangent

    def fill_start():
        own_tok.wait()
        swap_tok.wait_recv()

        def start_rows(i, _):
            r = pl.ds(al(i * 128, 128), 128)
            t = jnp.where(sc1[r, 0:1] > 0.5, tok[r, :].astype(F32), tokr[r, :].astype(F32)) + te[...]
            n1[r, :] = t
            xl[r, :] = t.astype(BF)
            return 0

        lax.fori_loop(0, T // 128, start_rows, 0)

    def small_near():
        small(0, 3, True)

        def one(k, _):
            b = vec.at[k * 4 + xy]
            send(b, b, vs.at[1], vs.at[4], near, c).start()
            return 0

        lax.fori_loop(0, 4, one, 0)

    def small_far():
        small(1, 4, True)

        def one(k, _):
            b = vec.at[(k // 2) * 4 + (1 - c) * 2 * y + c * x + lax.rem(k, 2) * (1 + c)]
            send(b, b, vs.at[2], vs.at[5], far, c).start()
            return 0

        lax.fori_loop(0, 8, one, 0)

    def fill_vectors():
        small(2, 8, True)
        for o in range(16):
            fullv[:, o * 48 : (o + 1) * 48] = vec[o][:, :48].astype(F32)
            for k in range(4):
                fulle[:, o * 192 + k * 48 : o * 192 + (k + 1) * 48] = vec[o][k : k + 1, 64:112].astype(F32)
        fullp[...] = jnp.concatenate([jnp.zeros_like(fullp[0:1, :]), jnp.ones_like(fullp[0:1, :])], axis=0)
        for h in range(D // 128):
            fullp[0:1, h * 384 : h * 384 + 128] = fullv[0:1, h * 128 : (h + 1) * 128]
            fullp[0:1, h * 384 + 256 : h * 384 + 384] = fullv[1:2, h * 128 : (h + 1) * 128]
            fullp[1:2, h * 384 : h * 384 + 128] = jnp.full((1, 128), HD**-0.5, F32)

    loose.update({"start": fill_start, "vec": fill_vectors, "vn": small_near, "vf": small_far})
    run(['s1:0', 's1:1', 's2o:9', 's1:2', 's2o:8', 'swap', 's2o:0', 's2o:10', 's2n:9', 's2o:2', 'start', 's1:3', 's2n:8', 's3:0.0', 's1:4', 's2o:1', 's2:0.1', 's2:0.2', 's2o:4', 's1:7', 's4:0.0', 's2o:7', 's2:0.3', 'vn', 'swc', 's3:0.1', 's2n:10', 's1:5', 's1:6', 's3:0.2', 's2:1', 's3:0.3', 'vf', 's4:0.1', 's2o:6', 's2o:3', 's2:2', 's4:0.2', 's3:1', 's4:0.3', 's2:3', 'vec'])

    def project(g):
        cs = pl.ds(al(g * 768, 768), 768)
        proj[:, cs] = ((nn(xl[...], wide[:, cs]) + fullp[0:1, cs]) * fullp[1:2, cs]).astype(BF)

    lane = lax.broadcasted_iota(jnp.int32, (1, 128), 1)
    halves = (lane < HD, lane >= HD)
    pairs = D // 128

    def keep(h, a):
        return pltpu.make_async_copy(pslot.at[a], spill.at[h * 2 + a], ps.at[a])

    tasks = [
        ['s4:1', 's3:3', 's2:7'],
        ['s1:9', 's2:5', 's4:2'],
        [],
        ['s5:9', 's3:5', 's3:6', 's3:7', 's2:8'],
        [],
        ['s4:5', 's3:8', 's3:9', 's2:10'],
    ]
    between = [['s2o:5', 's3:2', 's1:8', 's2:4'], ['s1:10', 's3:4', 's2:6'], ['s4:3', 's5:8', 's4:4', 's2:9', 's5:10']]

    def attend(h, _):
        for g in range(3):

            @pl.when(h == 2 * g)
            def _():
                pieces[g].done()

        @pl.when(lax.rem(h, 2) == 0)
        def _():
            project(h // 2)

        for g in range(3):
            if between[g]:

                @pl.when(h == 2 * g)
                def _():
                    run(between[g])

        cs = al(h * 384, 128)
        q2 = proj[:, pl.ds(cs, 128)]
        k2 = proj[:, pl.ds(cs + 128, 128)]
        v2 = proj[:, pl.ds(cs + 256, 128)]
        outs = []
        for a in range(2):
            s = nt(jnp.where(halves[a], q2, jnp.zeros_like(q2)), k2) + bias[...]
            e = jnp.exp(s - jnp.max(s, axis=-1, keepdims=True))
            p = (e * (1.0 / jnp.sum(e, axis=-1, keepdims=True))).astype(BF)

            @pl.when(h > 0)
            def _():
                keep(h - 1, a).wait()

            pslot[a] = p
            keep(h, a).start()
            outs.append(nn(p, v2))
        heads[:, pl.ds(al(h * 128, 128), 128)] = jnp.where(halves[0], outs[0], outs[1]).astype(BF)
        for k in range(pairs):

            @pl.when(h == k)
            def _():
                run(tasks[k])

        return 0

    lax.fori_loop(0, pairs, attend, 0)
    pieces[3].done()

    def load(h, a):
        return pltpu.make_async_copy(spill.at[h * 2 + a], pslot.at[a], pd.at[a])

    for a in range(2):
        keep(pairs - 1, a).wait()
        load(0, a).start()

    def normalize(v):
        centred = v - jnp.mean(v, axis=-1, keepdims=True)
        scale = lax.rsqrt(jnp.mean(centred * centred, axis=-1, keepdims=True) + 1e-5)
        return centred * scale, scale

    def first_rows(i, _):
        r = pl.ds(al(i * 256, 256), 256)
        v = n1[r, :] + (nn(heads[r, :], wide[:, OUT:EXP]) + fullv[2:3, :])
        n, s = normalize(v)
        n1[r, :] = n
        sc1[r, 1:2] = s
        fl[r, :] = (n * fullv[3:4, :] + fullv[4:5, :]).astype(BF)
        return 0

    lax.fori_loop(0, T // 256, first_rows, 0)
    run(['s4:7', 's4:6'])
    after = [
        [],
        ['s3:10', 's4:8'],
        ['s4:9'],
        ['s4:10'],
    ]
    then = [[], [], []]

    def expand(i, _):
        for k in range(4):

            @pl.when(i == k)
            def _():
                pieces[4 + k].done()

        cs = pl.ds(al(i * 768, 768), 768)
        u = nn(fl[...], wide[:, pl.ds(al(EXP + i * 768, 768), 768)]) + fulle[:, cs]
        cdf = 0.5 * (1.0 + lax.erf(u * math.sqrt(0.5)))
        hidden[:, cs] = (u * cdf).astype(BF)
        slope[:, cs] = (cdf + u * jnp.exp(-0.5 * u * u) * (1.0 / math.sqrt(2.0 * math.pi))).astype(BF)
        for k in range(4):

            @pl.when(i == k)
            def _():
                run(after[k])

        return 0

    lax.fori_loop(0, FF // 768, expand, 0)

    def contract(i, _):
        for k in range(3):

            @pl.when(i == k)
            def _():
                pieces[8 + k].done()

        cs = pl.ds(al(i * 256, 256), 256)
        sg[:, cs] = nn(hidden[...], wcon[:, cs]) + fullv[5:6, cs]
        for k in range(3):
            if then[k]:

                @pl.when(i == k)
                def _():
                    run(then[k])

        return 0

    lax.fori_loop(0, D // 256, contract, 0)
    own_cot.wait()
    swap_cot.wait_recv()

    gv[...] = jnp.zeros_like(gv)

    def second_rows(i, _):
        r = pl.ds(al(i * 256, 256), 256)
        v = n1[r, :] * fullv[3:4, :] + fullv[4:5, :] + sg[r, :]
        n, s = normalize(v)
        lonew[r, :] = (n * fullv[6:7, :] + fullv[7:8, :]).astype(BF)
        og = jnp.where(sc1[r, 0:1] > 0.5, cotn[r, :].astype(F32), cotr[r, :].astype(F32))
        gv[6:7, :] += jnp.sum(og * n, axis=0, keepdims=True)
        gv[7:8, :] += jnp.sum(og, axis=0, keepdims=True)
        w = og * fullv[6:7, :]
        g = s * (w - jnp.mean(w, axis=-1, keepdims=True) - n * jnp.mean(w * n, axis=-1, keepdims=True))
        sg[r, :] = g
        low = g.astype(BF)
        bg[r, :] = low
        gv[5:6, :] += jnp.sum(low.astype(F32), axis=0, keepdims=True)
        return 0

    lax.fori_loop(0, T // 256, second_rows, 0)
    swap_lo = send(lonew, lor, swap_sem.at[2, 0], swap_sem.at[2, 1], me, other)
    swap_lo.start()

    S = 384
    my_k = (1 - c) * x + c * y
    far_base = (1 - c) * (2 - 2 * y) + c * (1 - x)
    own_base = (1 - c) * 2 * y + c * x
    step_k = 1 + c

    def total(*refs):
        t = refs[0][...].astype(F32)
        for ref in refs[1:]:
            t = t + ref[...].astype(F32)
        return t

    class Red:
        def __init__(self, n, g, col, rows, recv, rcol, fsum, plane=None, width=384, parts=()):
            self.n, self.g, self.col, self.rows, self.recv, self.rcol, self.fsum = n, g, col, rows, recv, rcol, fsum
            self.plane, self.width, self.parts = plane, width, parts

        def cols(self, core):
            return pl.ds(al(self.col + core * S, 128), self.width)

        def part(self, base, i, k=1, second=False):
            if self.plane is None:
                cs = pl.ds(self.rcol + (self.width if second else 0), self.width)
            else:
                cs = pl.ds(0, S)
                base = base + self.rcol
            return self.recv.at[pl.ds(al(base + i * self.rows, 16), k * self.rows), cs]

        def mine(self, o):
            base = 0 if self.plane is None else self.plane * 4
            return self.g.at[pl.ds(al((base + o) * self.rows, 16), self.rows), self.cols(c)]

        def planes(self):
            return 4 if self.plane is None else 1

        def rp(self, o, k=1):
            return self.part(0, o, k)

        def ra(self, i, k=1):
            return self.part(0 if self.plane is None else 768, i, k, True)

        def rb(self, i, k=1):
            return self.part(384 if self.plane is None else 1152, i, k, True)

        def rz(self, i, k=1):
            if self.plane is None:
                return self.part(576, i, k, True)
            return self.recv.at[pl.ds(al(5376 + i * self.rows, 16), k * self.rows), pl.ds(0, S)]

        def sem(self, stage):
            n = 0 if self.plane is not None and stage == 3 else self.n
            return rs.at[self.n], rr.at[n * 5 + stage]

        def got(self, stage, ref):
            s, r = self.sem(stage)
            send(ref, ref, s, r, me, other).wait_recv()

        def P(self):
            base = 0 if self.plane is None else self.plane * 4 * self.rows
            n = 4 * self.planes() * self.rows
            src = self.g.at[pl.ds(al(base, 16), n), self.cols(other)]
            s, r = self.sem(0)
            send(src, self.rp(0, 4 * self.planes()), s, r, me, other).start()

        def A(self):
            self.got(0, self.rp(0, 4 * self.planes()))
            s, r = self.sem(1)

            def one(i, _):
                o = (i // 2) * 4 + far_base + lax.rem(i, 2) * step_k
                b = self.mine(o)
                b[...] = total(b, self.rp(o)).astype(BF)
                send(b, self.ra(i), s, r, far, c).start()
                return 0

            lax.fori_loop(0, 2 * self.planes(), one, 0)

        def B(self):
            self.got(1, self.ra(0, 2 * self.planes()))
            s, r = self.sem(2)

            def one(i, _):
                o = i * 4 + near_xy
                b = self.mine(o)
                b[...] = total(b, self.rp(o), self.ra(i * 2 + 1 - my_k)).astype(BF)
                send(b, self.rb(i), s, r, near, c).start()
                return 0

            lax.fori_loop(0, self.planes(), one, 0)

        def Z(self):
            self.got(2, self.rb(0, self.planes()))
            s, r = self.sem(3)
            if self.plane is None:
                for k in range(3):
                    p = lax.rem(z + k + 1, 4)
                    b = self.mine(p * 4 + xy)
                    b[...] = total(b, self.rp(p * 4 + xy), self.ra(p * 2 + my_k), self.rb(p)).astype(BF)
                    send(b, self.rz(k), s, r, zs[k], c).start()
            elif self.n > 0:
                b = self.mine(xy)
                b[...] = total(b, self.rp(xy), self.ra(my_k), self.rb(0)).astype(BF)
                send(b, self.rz(self.n - 1), s, r, zs[self.n - 1], c).start()

        def F(self):
            self.got(3, self.rz(0, 3))
            o, p = (z * 4 + xy, z) if self.plane is None else (xy, 0)
            t = total(self.mine(o), self.rp(o), self.ra(p * 2 + my_k), self.rb(p), self.rz(0), self.rz(1), self.rz(2))
            s, r = self.sem(4)
            if self.parts:
                for i, k in enumerate(self.parts):
                    b = self.fsum.at[:, pl.ds(al(k + c * 128, 128), 128)]
                    b[...] = t[:, i * 128 : (i + 1) * 128]
                    send(b, b, s, r, me, other).start()
            else:
                b = self.fsum.at[:, pl.ds(al((self.n - 4 if 4 <= self.n < 8 else 0) * 768 + c * S, 128), S)]
                b[...] = t
                send(b, b, s, r, me, other).start()

        def end(self):
            if self.plane is None:
                m = wide.at[pl.ds(0, 528), pl.ds(0, 3 * self.width)]
            else:
                m = wide.at[pl.ds(0, 576 if self.n == 0 else 512), pl.ds(0, 1152)]
            send(m, m, rs.at[self.n], rr.at[self.n], me, other).wait_send()
            if self.plane is None or self.n == 0:
                self.got(4, self.fsum.at[:, pl.ds(0, self.width)])

    con = {j: Red(j, gcon, 0, 192, con_r, j * 1344, fcon, plane=lax.rem(z + j, 4)) for j in range(4)}
    exp = [Red(4 + k, wide, EXP + k * 768, 48, hidden, k * 768, fexp) for k in range(4)]
    out = Red(8, wide, OUT, 48, cotn, 0, fout)
    ins = [
        Red(9 + k, gin, k * 768, 48, slope, k * 768, fin, parts=[q * D + k * 256 for q in range(3)]) for k in range(2)
    ]
    ins.append(Red(11, gin, 1536, 48, slope, 1536, fin, width=256, parts=[512, D + 512]))
    ins.append(Red(12, gin, 1792, 48, slope, 2048, fin, width=128, parts=[2 * D + 512]))
    sums = {f"C{k}": con[k] for k in range(4)}
    sums.update({f"E{k}": exp[k] for k in range(4)})
    sums.update({f"I{k}": ins[k] for k in range(4)})
    sums["O"] = out

    def reduce(ops):
        for op in ops:
            name, _, rest = op.partition(":")
            if op in loose:
                loose[op]()
            else:
                getattr(sums[rest], name)()

    def steps(i, lists):
        for k, ops in enumerate(lists):
            if ops:

                @pl.when(i == k)
                def _():
                    reduce(ops)

    def send_back():
        def out_rows(i, _):
            r = pl.ds(al(i * 128, 128), 128)
            lonew[r, :] = jnp.where(sc1[r, 0:1] > 0.5, lonew[r, :].astype(F32), lor[r, :].astype(F32)).astype(BF)
            return 0

        swap_lo.wait()
        lax.fori_loop(0, T // 128, out_rows, 0)
        lo_done.start()

    lo_done = pltpu.make_async_copy(lonew, lo_o, ls.at[14])
    loose["lo"] = send_back

    def vsend(stage, src, dst, dp, seq):
        return send(src, dst, rs.at[13 + stage], rr.at[65 + stage], dp, seq)

    def v_partner():
        vout[...] = jnp.zeros_like(vout)
        for o in range(16):
            vout[o, :, 0:48] = gv[0:8, o * 48 : (o + 1) * 48]
            for k in range(4):
                vout[o, k : k + 1, 64:112] = ge[:, o * 192 + k * 48 : o * 192 + (k + 1) * 48]
        vsend(0, vout, vr.at[pl.ds(0, 16)], me, other).start()

    def v_flip_y():
        vsend(0, vout, vr.at[pl.ds(0, 16)], me, other).wait_recv()
        vsum[...] = vout[...] + vr[pl.ds(0, 16)]
        for i in range(8):
            vsend(1, vsum.at[(i // 2) * 4 + 2 - 2 * y + i % 2], vr.at[16 + i], flip_y, c).start()

    def v_flip_x():
        vsend(1, vr.at[pl.ds(16, 8)], vr.at[pl.ds(16, 8)], me, other).wait_recv()
        for i in range(8):
            o = (i // 2) * 4 + 2 * y + i % 2
            vsum[o] = vsum[o] + vr[16 + i]
        for i in range(4):
            vsend(2, vsum.at[i * 4 + 2 * y + 1 - x], vr.at[24 + i], flip_x, c).start()

    def v_planes():
        vsend(2, vr.at[pl.ds(24, 4)], vr.at[pl.ds(24, 4)], me, other).wait_recv()
        for i in range(4):
            vsum[i * 4 + xy] = vsum[i * 4 + xy] + vr[24 + i]
        for k in range(3):
            vsend(3, vsum.at[lax.rem(z + k + 1, 4) * 4 + xy], vr.at[28 + k], zs[k], c).start()

    def v_total():
        vsend(3, vr.at[pl.ds(28, 3)], vr.at[pl.ds(28, 3)], me, other).wait_recv()
        vr[31] = vsum[z * 4 + xy] + vr[28] + vr[29] + vr[30]
        v_done.start()

    v_done = pltpu.make_async_copy(vr.at[31], gvec_o, ls.at[16])
    loose.update({"vP": v_partner, "vA": v_flip_y, "vB": v_flip_x, "vZ": v_planes, "vF": v_total})

    ig_mine, ig_theirs = bg, fl
    swap_ig = [
        send(ig_mine.at[pl.ds(256 * k, 256)], ig_theirs.at[pl.ds(256 * k, 256)], sw3.at[0, k], sw3.at[1, k], me, other)
        for k in range(3)
    ]
    for k in range(3):
        loose[f"swg{k}"] = swap_ig[k].start
    ig_done = pltpu.make_async_copy(sg, ig_o, ls.at[15])

    def take_rows():
        for d in swap_ig:
            d.wait_recv()

        def grad_rows(i, _):
            r = pl.ds(al(i * 128, 128), 128)
            sg[r, :] = jnp.where(sc1[r, 0:1] > 0.5, sg[r, :], ig_theirs[r, :].astype(F32))
            return 0

        lax.fori_loop(0, T // 128, grad_rows, 0)
        ig_done.start()

    loose["sel"] = take_rows

    def grad_con(i, _):
        p = al(lax.rem(z + i + 1, 4) * 768, 768)
        gcon[pl.ds(p, 768), :] = tn(hidden[:, pl.ds(p, 768)], bg[...]).astype(BF)
        steps(i, [['P:C1'], ['P:C2'], ['P:C3', 'A:C1'], ['P:C0']])
        return 0

    lax.fori_loop(0, 4, grad_con, 0)

    def expand_back(i, _):
        cs = pl.ds(al(i * 768, 768), 768)
        g = (nt(bg[...], wcon[cs, :]) * slope[:, cs].astype(F32)).astype(BF)
        slope[:, cs] = g
        ge[:, cs] = jnp.sum(g.astype(F32), axis=0, keepdims=True)
        steps(i, [['A:C3', 'A:C2'], [], [], []])
        return 0

    lax.fori_loop(0, FF // 768, expand_back, 0)

    def first_back(i, _):
        r = pl.ds(al(i * 256, 256), 256)
        g = sg[r, :] + nt(slope[r, :], wide[:, EXP:])
        n = n1[r, :]
        gv[3:4, :] += jnp.sum(g * n, axis=0, keepdims=True)
        gv[4:5, :] += jnp.sum(g, axis=0, keepdims=True)
        w = g * fullv[3:4, :]
        g = sc1[r, 1:2] * (w - jnp.mean(w, axis=-1, keepdims=True) - n * jnp.mean(w * n, axis=-1, keepdims=True))
        sg[r, :] = g
        low = g.astype(BF)
        bg[r, :] = low
        gv[2:3, :] += jnp.sum(low.astype(F32), axis=0, keepdims=True)
        steps(i, [['B:C1'], ['A:C0'], []])
        return 0

    lax.fori_loop(0, T // 256, first_back, 0)
    for p in pieces[4:8]:
        p.drain()

    def grad_exp(i, _):
        cs = pl.ds(al(i * 768, 768), 768)
        wide[:, pl.ds(al(EXP + i * 768, 768), 768)] = tn(fl[...], slope[:, cs]).astype(BF)
        steps(i, [['P:E0', 'B:C3'], ['P:E1', 'B:C2'], ['Z:C1', 'B:C0'], ['P:E3', 'Z:C3', 'A:E0']])
        return 0

    lax.fori_loop(0, 4, grad_exp, 0)
    hg = cotr
    hg[...] = nt(bg[...], wide[:, OUT:EXP]).astype(BF)
    reduce([])
    pieces[3].drain()
    wide[:, OUT:EXP] = tn(heads[...], bg[...]).astype(BF)
    reduce(['P:O', 'A:E1', 'Z:C2', 'P:E2'])

    tasks = [['A:E3'], ['A:O'], ['P:I0', 'B:E3', 'B:E0', 'Z:C0'], ['F:C0', 'B:E1'], ['Z:E0', 'A:I1'], ['Z:E1', 'vP', 'B:E2']]
    after = [[], ['P:I1', 'Z:E3', 'A:E2', 'lo', 'B:O'], []]

    def attend_back(h, _):
        cs = al(h * 384, 128)
        hs = pl.ds(al(h * 128, 128), 128)
        q2 = proj[:, pl.ds(cs, 128)]
        k2 = proj[:, pl.ds(cs + 128, 128)]
        v2 = proj[:, pl.ds(cs + 256, 128)]
        g2 = hg[:, hs]
        prod = g2.astype(F32) * heads[:, hs].astype(F32)
        qt = q2.astype(F32).T.astype(BF)
        gt = g2.astype(F32).T.astype(BF)
        dq, dk, dv = [], [], []
        for a in range(2):
            load(h, a).wait()
            rowdot = jnp.sum(jnp.where(halves[a], prod, 0.0), axis=-1, keepdims=True)
            p = pslot[a]
            dp = nt(jnp.where(halves[a], g2, jnp.zeros_like(g2)), v2)
            ds = (p.astype(F32) * (dp - rowdot)).astype(BF)
            dq.append(nn(ds, k2))
            dk.append(nn(qt[a * HD : (a + 1) * HD], ds))
            dv.append(nn(gt[a * HD : (a + 1) * HD], p))

            @pl.when(h + 1 < pairs)
            def _():
                load(h + 1, a).start()

        dq = (jnp.where(halves[0], dq[0], dq[1]) * HD**-0.5).astype(BF)
        dk = jnp.concatenate(dk, axis=0).T.astype(BF)
        dv = jnp.concatenate(dv, axis=0).T.astype(BF)
        proj[:, pl.ds(cs, 128)] = dq
        proj[:, pl.ds(cs + 128, 128)] = dk
        proj[:, pl.ds(cs + 256, 128)] = dv
        gv[0:1, hs] = jnp.sum(dq.astype(F32), axis=0, keepdims=True)
        gv[1:2, hs] = jnp.sum(dv.astype(F32), axis=0, keepdims=True)

        steps(h, tasks)

        @pl.when(lax.rem(h, 2) == 1)
        def _():
            cols = pl.ds(al((h // 2) * 768, 768), 768)
            gin[:, cols] = tn(xl[...], proj[:, cols]).astype(BF)

        steps((h - 1) // 2 + 8 * (1 - lax.rem(h, 2)), after)
        return 0

    lax.fori_loop(0, pairs, attend_back, 0)

    def input_rows(i, _):
        r = pl.ds(al(i * 256, 256), 256)
        g = sg[r, :] + nt(proj[r, :], wide[:, IN:OUT])
        sg[r, :] = g
        ig_mine[r, :] = g.astype(BF)
        steps(i, [['Z:O', 'A:I0', 'P:I2'], [], ['Z:E2', 'B:I1', 'P:I3', 'swg0', 'A:I3', 'swg1', 'F:E0', 'F:E3', 'F:O', 'B:I0', 'Z:I1', 'A:I2', 'vA', 'swg2', 'F:E2', 'Z:I0', 'B:I3', 'B:I2', 'Z:I3', 'vB', 'sel', 'Z:I2', 'F:I0', 'vZ', 'F:I3', 'F:E1', 'F:I1', 'F:I2', 'vF']])
        return 0

    lax.fori_loop(0, T // 256, input_rows, 0)
    outs = [lo_done, ig_done, v_done]
    for k, (v, o) in enumerate([(fcon, gcon_o), (fexp, gexp_o), (fout, gout_o), (fin, gin_o)]):
        for p in [[con[0]], exp, [out], ins][k]:
            p.end()
        outs.append(pltpu.make_async_copy(v, o, ls.at[17 + k]))
        outs[-1].start()
    for k in (1, 2, 3):
        con[k].end()
    swap_tok.wait_send()
    swap_cot.wait_send()
    for d in swap_ig:
        d.wait_send()
    for p in pieces[0:3] + pieces[8:]:
        p.drain()
    for stage, k in ((0, 3), (1, 4), (2, 8)):
        small(stage, k, False)
        m = vr.at[pl.ds(0, (8, 4, 3)[stage])]
        vsend(stage + 1, m, m, me, other).wait_send()
    vsend(0, vout, vr.at[pl.ds(0, 16)], me, other).wait_send()
    for o in outs:
        o.wait()


def fused_layer(tokens, time_embed, segments, iw, ow, ew, cw, vectors, cot):
    T, D = tokens.shape
    FF = ew.shape[1]
    sh = jax.ShapeDtypeStruct
    anyspec = pl.BlockSpec(memory_space=pl.ANY)
    vspec = pl.BlockSpec(memory_space=VM)
    scratch = [
        VM((D, 4 * D + FF), BF), VM((FF, D), BF),
        VM((T, D), BF), VM((T, D), BF), VM((T, D), BF), VM((T, D), BF),
        VM((16, 16, 128), BF), VM((16, 128), F32), VM((16, D), F32), VM((1, FF), F32), VM((2, 3 * D), F32),
        VM((T, 3 * D), BF), VM((T, D), BF), VM((T, D), F32), VM((T, T), F32),
        VM((T, 2), F32), VM((T, D), BF), VM((T, D), BF), VM((T, FF), BF), VM((T, FF), BF),
        VM((2, T, T), BF), VM((T, D), BF),
        VM((D, 3 * D), BF), VM((FF, D), BF), VM((5952, 384), BF), VM((8, D), F32), VM((1, FF), F32),
        VM((16, 8, 128), F32), VM((16, 8, 128), F32), VM((32, 8, 128), F32),
        VM(iw.shape, F32), VM(ow.shape, F32), VM(ew.shape, F32), VM(cw.shape, F32),
        DMA((3, 2)), DMA((2, 3)), DMA((21,)), DMA((11,)), DMA((65,)), DMA((6,)), DMA((2,)), DMA((17,)), DMA((69,)), DMA((2,)),
    ]
    return pl.pallas_call(
        fused_kernel,
        out_shape=(
            sh((T, D), BF), sh((T, D), F32), sh(iw.shape, F32), sh(ow.shape, F32), sh(ew.shape, F32),
            sh(cw.shape, F32), sh((8, 128), F32), sh((D // HD, T, T), BF),
        ),
        in_specs=[anyspec, anyspec, vspec, vspec, anyspec, anyspec, anyspec, anyspec] + [vspec] * 9,
        out_specs=(anyspec,) * 8,
        scratch_shapes=scratch,
        compiler_params=pltpu.CompilerParams(
            collective_id=0, has_side_effects=True, vmem_limit_bytes=67043328
        ),
    )(tokens, cot, time_embed, segments, iw, ow, ew, cw, *vectors)


epsilon = 1e-05
masked_score = -1e30


def matmul(left, right):
    return jnp.dot(left, right, preferred_element_type=jnp.float32)


def product_tn(left, right):
    return lax.dot_general(
        left, right, (((0,), (0,)), ((), ())), preferred_element_type=jnp.float32
    )


def product_nt(left, right):
    return lax.dot_general(
        left, right, (((1,), (1,)), ((), ())), preferred_element_type=jnp.float32
    )


def normalize(values):
    mean = jnp.mean(values, axis=-1, keepdims=True)
    centred = values - mean
    scale = lax.rsqrt(jnp.mean(centred * centred, axis=-1, keepdims=True) + epsilon)
    return (centred * scale, scale)


def norm_back(grad, normed, scale, gain):
    scaled = grad * gain
    return scale * (
        scaled
        - jnp.mean(scaled, axis=-1, keepdims=True)
        - normed * jnp.mean(scaled * normed, axis=-1, keepdims=True)
    )


def gelu_value(values):
    return 0.5 * values * (1.0 + lax.erf(values * math.sqrt(0.5)))


def gelu_slope(values):
    return 0.5 * (1.0 + lax.erf(values * math.sqrt(0.5))) + values * jnp.exp(
        -0.5 * values * values
    ) / math.sqrt(2.0 * math.pi)


def attend_forward(item):
    query, key, value, segment_row = item
    length, depth = query.shape
    block = min(512, length)
    blocks = length // block
    scale = depth ** (-0.5)

    def one_block(part):
        query_block, segment_block = part
        scores = product_nt(query_block, key) * scale
        scores = jnp.where(segment_block[:, None] == segment_row[None, :], scores, masked_score)
        top = jnp.max(scores, axis=-1, keepdims=True)
        expo = jnp.exp(scores - top)
        total = jnp.sum(expo, axis=-1, keepdims=True)
        probs_low = (expo / total).astype(jnp.bfloat16)
        return (matmul(probs_low, value).astype(jnp.bfloat16), (top + jnp.log(total))[:, 0])

    outputs, logsum = lax.map(
        one_block, (query.reshape(blocks, block, depth), segment_row.reshape(blocks, block))
    )
    return (outputs.reshape(length, depth), logsum.reshape(length))


def attend_backward(item):
    query, key, value, segment_row, logsum, out_grad = item
    length, depth = query.shape
    block = min(512, length)
    blocks = length // block
    scale = depth ** (-0.5)

    def one_block(carry, part):
        key_grad, value_grad = carry
        query_block, segment_block, logsum_block, grad_block = part
        scores = product_nt(query_block, key) * scale
        scores = jnp.where(segment_block[:, None] == segment_row[None, :], scores, masked_score)
        probs = jnp.exp(scores - logsum_block[:, None])
        probs_low = probs.astype(jnp.bfloat16)
        prob_grad = product_nt(grad_block, value)
        row_total = jnp.sum(probs * prob_grad, axis=-1, keepdims=True)
        score_grad = (probs * (prob_grad - row_total)).astype(jnp.bfloat16)
        query_grad = matmul(score_grad, key) * scale
        key_grad = key_grad + product_tn(score_grad, query_block) * scale
        value_grad = value_grad + product_tn(probs_low, grad_block)
        return ((key_grad, value_grad), query_grad.astype(jnp.bfloat16))

    zeros = jnp.zeros((length, depth), jnp.float32)
    parts = (
        query.reshape(blocks, block, depth),
        segment_row.reshape(blocks, block),
        logsum.reshape(blocks, block),
        out_grad.reshape(blocks, block, depth),
    )
    (key_grad, value_grad), query_grad = lax.scan(one_block, (zeros, zeros), parts)
    return (
        query_grad.reshape(length, depth),
        key_grad.astype(jnp.bfloat16),
        value_grad.astype(jnp.bfloat16),
    )


def plain_body(
    tokens,
    time_embed,
    segments,
    input_weight,
    query_bias,
    value_bias,
    output_weight,
    output_bias,
    first_gain,
    first_shift,
    expand_weight,
    expand_bias,
    contract_weight,
    contract_bias,
    second_gain,
    second_shift,
    cotangent,
):
    pairs = lax.axis_size("seq")
    seqs, half, width = tokens.shape
    length = half * pairs
    rows = seqs * half
    group = width // pairs
    heads_here = group // HD
    start = (tokens.astype(jnp.float32) + time_embed[:, None, :]).reshape(rows, width)
    start_low = start.astype(jnp.bfloat16)
    attention_set = (
        lax.all_gather(input_weight, "dp", axis=0, tiled=True),
        lax.all_gather(output_weight, "dp", axis=0, tiled=True),
        lax.all_gather(query_bias, "dp", axis=0, tiled=True),
        lax.all_gather(value_bias, "dp", axis=0, tiled=True),
        lax.all_gather(output_bias, "dp", axis=0, tiled=True),
        lax.all_gather(first_gain, "dp", axis=0, tiled=True),
        lax.all_gather(first_shift, "dp", axis=0, tiled=True),
    )
    (
        full_input,
        full_output,
        full_query_bias,
        full_value_bias,
        full_output_bias,
        full_first_gain,
        full_first_shift,
    ) = attention_set
    bias_row = jnp.concatenate(
        [
            full_query_bias.astype(jnp.float32),
            jnp.zeros((width,), jnp.float32),
            full_value_bias.astype(jnp.float32),
        ]
    )
    projected_low = (matmul(start_low, full_input) + bias_row).astype(jnp.bfloat16)
    regrouped = lax.all_to_all(
        projected_low.reshape(seqs, half, 3, pairs, group),
        "seq",
        split_axis=3,
        concat_axis=1,
        tiled=True,
    )
    split = regrouped.reshape(seqs, length, 3, heads_here, HD).transpose(2, 0, 3, 1, 4)
    split = split.reshape(3, seqs * heads_here, length, HD)
    query_heads, key_heads, value_heads = (split[0], split[1], split[2])
    segment_heads = jnp.repeat(segments, heads_here, axis=0)
    heads_out, logsum = lax.map(
        attend_forward, (query_heads, key_heads, value_heads, segment_heads)
    )
    heads_tokens = (
        heads_out.reshape(seqs, heads_here, length, HD)
        .transpose(0, 2, 1, 3)
        .reshape(seqs, length, 1, group)
    )
    heads_low = lax.all_to_all(
        heads_tokens, "seq", split_axis=1, concat_axis=2, tiled=True
    ).reshape(rows, width)
    attention = matmul(heads_low, full_output) + full_output_bias.astype(jnp.float32)
    normed_one, scale_one = normalize(start + attention)
    gain_one = full_first_gain.astype(jnp.float32)
    first = normed_one * gain_one + full_first_shift.astype(jnp.float32)
    first_low = first.astype(jnp.bfloat16)
    network_set = (
        lax.all_gather(expand_weight, "dp", axis=0, tiled=True),
        lax.all_gather(contract_weight, "dp", axis=0, tiled=True),
        lax.all_gather(expand_bias, "dp", axis=0, tiled=True),
        lax.all_gather(contract_bias, "dp", axis=0, tiled=True),
        lax.all_gather(second_gain, "dp", axis=0, tiled=True),
        lax.all_gather(second_shift, "dp", axis=0, tiled=True),
    )
    (
        full_expand,
        full_contract,
        full_expand_bias,
        full_contract_bias,
        full_second_gain,
        full_second_shift,
    ) = network_set
    expand = matmul(first_low, full_expand) + full_expand_bias.astype(jnp.float32)
    hidden = gelu_value(expand).astype(jnp.bfloat16)
    second_sum = first + matmul(hidden, full_contract) + full_contract_bias.astype(jnp.float32)
    normed_two, scale_two = normalize(second_sum)
    gain_two = full_second_gain.astype(jnp.float32)
    layer_output = (normed_two * gain_two + full_second_shift.astype(jnp.float32)).astype(
        jnp.bfloat16
    )
    network_set = (
        lax.all_gather(expand_weight, "dp", axis=0, tiled=True),
        lax.all_gather(contract_weight, "dp", axis=0, tiled=True),
        lax.all_gather(expand_bias, "dp", axis=0, tiled=True),
        lax.all_gather(contract_bias, "dp", axis=0, tiled=True),
        lax.all_gather(second_gain, "dp", axis=0, tiled=True),
        lax.all_gather(second_shift, "dp", axis=0, tiled=True),
    )
    full_expand, full_contract = (network_set[0], network_set[1])
    out_grad = cotangent.astype(jnp.float32).reshape(rows, width)
    grad_second_gain = jnp.sum(out_grad * normed_two, axis=0)
    grad_second_shift = jnp.sum(out_grad, axis=0)
    second_grad = norm_back(out_grad, normed_two, scale_two, gain_two)
    branch_grad = second_grad.astype(jnp.bfloat16)
    grad_contract_bias = jnp.sum(branch_grad.astype(jnp.float32), axis=0)
    grad_contract_weight = product_tn(hidden, branch_grad)
    expand_grad = (product_nt(branch_grad, full_contract) * gelu_slope(expand)).astype(jnp.bfloat16)
    grad_expand_bias = jnp.sum(expand_grad.astype(jnp.float32), axis=0)
    grad_expand_weight = product_tn(first_low, expand_grad)
    first_grad = second_grad + product_nt(expand_grad, full_expand)
    grad_first_gain = jnp.sum(first_grad * normed_one, axis=0)
    grad_first_shift = jnp.sum(first_grad, axis=0)
    start_grad = norm_back(first_grad, normed_one, scale_one, gain_one)
    attention_set = (
        lax.all_gather(input_weight, "dp", axis=0, tiled=True),
        lax.all_gather(output_weight, "dp", axis=0, tiled=True),
        lax.all_gather(query_bias, "dp", axis=0, tiled=True),
        lax.all_gather(value_bias, "dp", axis=0, tiled=True),
        lax.all_gather(output_bias, "dp", axis=0, tiled=True),
        lax.all_gather(first_gain, "dp", axis=0, tiled=True),
        lax.all_gather(first_shift, "dp", axis=0, tiled=True),
    )
    full_input, full_output = (attention_set[0], attention_set[1])
    attention_grad = start_grad.astype(jnp.bfloat16)
    grad_output_bias = jnp.sum(attention_grad.astype(jnp.float32), axis=0)
    grad_output_weight = product_tn(heads_low, attention_grad)
    heads_grad = product_nt(attention_grad, full_output).astype(jnp.bfloat16)
    grad_heads = lax.all_to_all(
        heads_grad.reshape(seqs, half, pairs, group), "seq", split_axis=2, concat_axis=1, tiled=True
    )
    grad_heads = (
        grad_heads.reshape(seqs, length, heads_here, HD)
        .transpose(0, 2, 1, 3)
        .reshape(seqs * heads_here, length, HD)
    )
    query_grad, key_grad, value_grad = lax.map(
        attend_backward, (query_heads, key_heads, value_heads, segment_heads, logsum, grad_heads)
    )
    stacked = jnp.stack([query_grad, key_grad, value_grad]).reshape(3, seqs, heads_here, length, HD)
    stacked = stacked.transpose(1, 3, 0, 2, 4).reshape(seqs, length, 3, 1, group)
    projected_grad = lax.all_to_all(
        stacked, "seq", split_axis=1, concat_axis=3, tiled=True
    ).reshape(rows, 3 * width)
    grad_query_bias = jnp.sum(projected_grad[:, :width].astype(jnp.float32), axis=0)
    grad_value_bias = jnp.sum(projected_grad[:, 2 * width :].astype(jnp.float32), axis=0)
    grad_input_weight = product_tn(start_low, projected_grad)
    input_grad = (start_grad + product_nt(projected_grad, full_input)).reshape(seqs, half, width)
    grads = (
        grad_input_weight,
        grad_query_bias,
        grad_value_bias,
        grad_output_weight,
        grad_output_bias,
        grad_first_gain,
        grad_first_shift,
        grad_expand_weight,
        grad_expand_bias,
        grad_contract_weight,
        grad_contract_bias,
        grad_second_gain,
        grad_second_shift,
    )
    owned = (
        lax.psum_scatter(grads[0], "dp", scatter_dimension=0, tiled=True),
        lax.psum_scatter(grads[1], "dp", scatter_dimension=0, tiled=True),
        lax.psum_scatter(grads[2], "dp", scatter_dimension=0, tiled=True),
        lax.psum_scatter(grads[3], "dp", scatter_dimension=0, tiled=True),
        lax.psum_scatter(grads[4], "dp", scatter_dimension=0, tiled=True),
        lax.psum_scatter(grads[5], "dp", scatter_dimension=0, tiled=True),
        lax.psum_scatter(grads[6], "dp", scatter_dimension=0, tiled=True),
        lax.psum_scatter(grads[7], "dp", scatter_dimension=0, tiled=True),
        lax.psum_scatter(grads[8], "dp", scatter_dimension=0, tiled=True),
        lax.psum_scatter(grads[9], "dp", scatter_dimension=0, tiled=True),
        lax.psum_scatter(grads[10], "dp", scatter_dimension=0, tiled=True),
        lax.psum_scatter(grads[11], "dp", scatter_dimension=0, tiled=True),
        lax.psum_scatter(grads[12], "dp", scatter_dimension=0, tiled=True),
    )
    summed = (
        lax.psum(owned[0].astype(jnp.bfloat16), "seq").astype(jnp.float32),
        lax.psum(owned[1].astype(jnp.bfloat16), "seq").astype(jnp.float32),
        lax.psum(owned[2].astype(jnp.bfloat16), "seq").astype(jnp.float32),
        lax.psum(owned[3].astype(jnp.bfloat16), "seq").astype(jnp.float32),
        lax.psum(owned[4].astype(jnp.bfloat16), "seq").astype(jnp.float32),
        lax.psum(owned[5].astype(jnp.bfloat16), "seq").astype(jnp.float32),
        lax.psum(owned[6].astype(jnp.bfloat16), "seq").astype(jnp.float32),
        lax.psum(owned[7].astype(jnp.bfloat16), "seq").astype(jnp.float32),
        lax.psum(owned[8].astype(jnp.bfloat16), "seq").astype(jnp.float32),
        lax.psum(owned[9].astype(jnp.bfloat16), "seq").astype(jnp.float32),
        lax.psum(owned[10].astype(jnp.bfloat16), "seq").astype(jnp.float32),
        lax.psum(owned[11].astype(jnp.bfloat16), "seq").astype(jnp.float32),
        lax.psum(owned[12].astype(jnp.bfloat16), "seq").astype(jnp.float32),
    )
    return (layer_output.reshape(seqs, half, width), input_grad) + tuple(summed)


def finish_kernel(lo, ig, gi, go, ge, gc, vec, lo_o, ig_o, gi_o, go_o, ge_o, gc_o, *rest):
    small, bufs, sems = rest[:9], rest[9:15], rest[15]
    pairs = list(zip((ig, lo, ge, gi, gc, go), (bufs[1], bufs[0], bufs[4], bufs[2], bufs[5], bufs[3])))
    results = (ig_o, lo_o, ge_o, gi_o, gc_o, go_o)
    loads = [pltpu.make_async_copy(a, b, sems.at[0, k]) for k, (a, b) in enumerate(pairs)]
    stores = [pltpu.make_async_copy(b, r, sems.at[1, k]) for k, ((_, b), r) in enumerate(zip(pairs, results))]
    for d in loads:
        d.start()
    own = small[0].shape[1]
    for k in range(8):
        small[k][...] = vec[k : k + 1, :own]
    for k in range(4):
        small[8][:, k * own : (k + 1) * own] = vec[k : k + 1, 64 : 64 + own]
    for a, b in zip(loads, stores):
        a.wait()
        b.start()
    for b in stores:
        b.wait()


def finish(lo, ig, gi, go, ge, gc, vec, own):
    sh = jax.ShapeDtypeStruct
    anyspec = pl.BlockSpec(memory_space=pl.ANY)
    vspec = pl.BlockSpec(memory_space=VM)
    big = (lo, ig, gi, go, ge, gc)
    return pl.pallas_call(
        finish_kernel,
        out_shape=[sh(v.shape, v.dtype) for v in big] + [sh((1, own), F32)] * 8 + [sh((1, 4 * own), F32)],
        in_specs=[anyspec] * 6 + [vspec],
        out_specs=[anyspec] * 6 + [vspec] * 9,
        scratch_shapes=[VM(v.shape, v.dtype) for v in big] + [DMA((2, 6))],
    )(*big, vec)


def fused_body(
    tokens, time_embed, segments, input_weight, query_bias, value_bias, output_weight, output_bias, first_gain,
    first_shift, expand_weight, expand_bias, contract_weight, contract_bias, second_gain, second_shift, cotangent,
):
    vectors = [
        query_bias, value_bias, output_bias, first_gain, first_shift, contract_bias, second_gain, second_shift,
        expand_bias,
    ]
    own = query_bias.shape[0]
    vectors = [v.reshape(1, v.shape[0]) for v in vectors]
    parts = fused_layer(
        tokens[0], time_embed, segments, input_weight, output_weight, expand_weight, contract_weight, vectors,
        cotangent[0],
    )[:7]
    layer_output, input_grad, g_in, g_out, g_exp, g_con, *row = finish(*parts, own)
    row = [v.reshape(v.shape[1]) for v in row]
    return (
        layer_output[None], input_grad[None], g_in, row[0], row[1], g_out, row[2], row[3], row[4],
        g_exp, row[8], g_con, row[5], row[6], row[7],
    )


def body(*args):
    if lax.axis_size("dp") == 16 and lax.axis_size("seq") == 2:
        return fused_body(*args)
    return plain_body(*args)


def solution(mesh):
    return jax.shard_map(
        body,
        mesh=mesh,
        in_specs=(
            P("dp", "seq", None),
            P("dp", None),
            P("dp", None),
            P("dp", None),
            P("dp"),
            P("dp"),
            P("dp", None),
            P("dp"),
            P("dp"),
            P("dp"),
            P("dp", None),
            P("dp"),
            P("dp", None),
            P("dp"),
            P("dp"),
            P("dp"),
            P("dp", "seq", None),
        ),
        out_specs=(
            P("dp", "seq", None),
            P("dp", "seq", None),
            P("dp", None),
            P("dp"),
            P("dp"),
            P("dp", None),
            P("dp"),
            P("dp"),
            P("dp"),
            P("dp", None),
            P("dp"),
            P("dp", None),
            P("dp"),
            P("dp"),
            P("dp"),
        ),
        check_vma=False,
    )
```

```python
import functools
import math

import jax
import jax.numpy as jnp
from jax import lax
from jax.experimental import pallas as pl
from jax.experimental.pallas import tpu as pltpu
from jax.sharding import PartitionSpec as P

HD = 64
DOCS = 4
BF = jnp.bfloat16
F32 = jnp.float32
MESH = pl.DeviceIdType.MESH
VM = pltpu.VMEM
DMA = pltpu.SemaphoreType.DMA


def nn(a, b):
    return jnp.dot(a, b, preferred_element_type=F32)


def nt(a, b):
    return lax.dot_general(a, b, (((1,), (1,)), ((), ())), preferred_element_type=F32)


def tn(a, b):
    return lax.dot_general(a, b, (((0,), (0,)), ((), ())), preferred_element_type=F32)


def fused_kernel(
    tokens, cot, te, seg, win_s, wout_s, wexp_s, wcon_s, v0, v1, v2, v3, v4, v5, v6, v7, v8,
    lo_o, ig_o, gin_o, gout_o, gexp_o, gcon_o, gvec_o, spill,
    wide, wcon, tok, tokr, cotn, cotr, vec, pack, fullv, fulle, fullp, proj, xl, n1, sg,
    sc1, heads, fl, hidden, slope, pslot, bg,
    gin, gcon, con_r, ry, gv, ge, vout, vsum, vr, fin, fout, fexp, fcon,
    swap_sem, sw3, ls, gs, gr, vs, ps, rs, rr, pd,
):
    vectors = (v0, v1, v2, v3, v4, v5, v6, v7, v8)
    T, D = tok.shape
    FF = wcon.shape[0]
    IN, OUT, EXP = 0, 3 * D, 4 * D
    bias, lonew, lor = sg, tok, tokr
    me = lax.axis_index("dp")
    c = lax.axis_index("seq")
    x = lax.rem(me, 2)
    y = lax.rem(me // 2, 2)
    xy = lax.rem(me, 4)
    z = me // 4
    flip_x = me + 1 - 2 * x
    flip_y = me + 2 - 4 * y
    near = (1 - c) * flip_x + c * flip_y
    far = (1 - c) * flip_y + c * flip_x
    other = 1 - c
    zs = [lax.rem(z + k, 4) * 4 + xy for k in (1, 2, 3)]

    def send(src, dst, s, r, dp, seq):
        return pltpu.make_async_remote_copy(
            src_ref=src, dst_ref=dst, send_sem=s, recv_sem=r,
            device_id={"dp": dp, "seq": seq}, device_id_type=MESH,
        )

    barrier = pltpu.get_barrier_semaphore()
    for dp, seq in [(me, other), (near, c), (far, c)] + [(q, c) for q in zs]:
        pl.semaphore_signal(
            barrier, inc=1, device_id={"dp": dp, "seq": seq}, device_id_type=MESH
        )

    def al(v, m):
        return pl.multiple_of(v, m)

    class Piece:
        def __init__(self, n, buf, rows, col, half, shards, whole=None):
            self.n, self.buf, self.rows, self.col, self.half, self.shards = n, buf, rows, col, half, shards
            self.whole = whole
            self.low = 1 if whole is None else 2

        def cols(self, core):
            return pl.ds(al(self.col + core * self.half, 128), self.half)

        def block(self, o):
            return self.buf.at[pl.ds(al(o * self.rows, 16), self.rows), self.cols(c)]

        def region(self, k, core=c):
            return self.buf.at[pl.ds(0, k * self.rows), self.cols(core)]

        def arrival(self, stage, k):
            if stage > 3:
                return gr.at[56 + self.whole * 3 + stage - 4]
            return gr.at[stage * 4 + k] if self.n == 0 and stage < 3 else gr.at[12 + self.n * 4 + stage]

        def push(self, src, dst, stage, k, dp):
            send(src, dst, gs.at[self.n], self.arrival(stage, k), dp, c).start()

        def got(self, stage, k, blocks):
            m = self.region(blocks)
            send(m, m, gs.at[self.n], self.arrival(stage, k), me, other).wait_recv()

        def own(self):
            base = pl.ds(al(me * self.rows, 16), self.rows)
            for i, (ref, first, width) in enumerate(self.shards):
                yield (
                    ref.at[:, pl.ds(al(first + c * width, 128), width)],
                    self.buf.at[base, pl.ds(al(self.col + c * self.half + i * width, 128), width)],
                )

        def s1(self):
            for k in range(self.low - 1, 3):
                for a, b in self.own():
                    self.push(a, b, 0, k + 1, zs[k])
            for a, b in self.own():
                pltpu.make_async_copy(a, b, ls.at[self.n]).start()

        def s2o(self):
            for a, b in self.own():
                self.push(a, b, 1 if self.whole is None else 4, 0, near)
                self.push(a, b, 2 if self.whole is None else 5, 0, far)

        def s2n(self):
            self.got(4, 0, 1)
            b = self.block(z * 4 + near_xy)
            self.push(b, b, 5, 0, far)

        def s5(self):
            self.got(5, 0, 2)
            m = self.block(me)
            pltpu.make_async_copy(m, m, ls.at[self.n]).wait()
            p = self.buf.at[pl.ds(al(z * 4 * self.rows, 16), 4 * self.rows), self.cols(c)]
            self.push(p, p, 6, 0, zs[0])

        def s2(self, k=None):
            if k is None:
                self.got(0, 0, 4 - self.low)
            else:
                self.got(0, k, 1)

            def one(i, _):
                b = self.block(lax.rem(z + 4 - i, 4) * 4 + xy)
                self.push(b, b, 1, i, near)
                self.push(b, b, 2, i, far)
                return 0

            if k is None:
                lax.fori_loop(self.low, 4, one, 0)
            else:
                one(k, 0)

        def s3(self, k=None):
            if k is None:
                self.got(1, 0, 4 if self.whole is None else 2)
            else:
                self.got(1, k, 1)

            def one(i, _):
                b = self.block(lax.rem(z + 4 - i, 4) * 4 + near_xy)
                self.push(b, b, 2, i, far)
                return 0

            if k is None:
                lax.fori_loop(0 if self.whole is None else 2, 4, one, 0)
            else:
                one(k, 0)

        def s4(self, k=None):
            if k is None:
                self.got(2, 0, 8 if self.whole is None else 4)
            else:
                self.got(2, k, 2)
            if self.whole is not None:
                self.got(6, 0, 4)
            elif not k:
                m = self.block(me)
                pltpu.make_async_copy(m, m, ls.at[self.n]).wait()
            if k is None:
                p = self.region(16)
            else:
                p = self.buf.at[pl.ds(al(lax.rem(z + 4 - k, 4) * 4 * self.rows, 16), 4 * self.rows), self.cols(c)]
            send(p, p, gs.at[self.n], self.arrival(3, 0), me, other).start()

        def done(self):
            m = self.region(16, other)
            send(m, m, gs.at[self.n], self.arrival(3, 0), me, other).wait_recv()

        def drain(self):
            m = wide.at[pl.ds(0, 496), pl.ds(0, self.rows * self.half // 16)]
            send(m, m, gs.at[self.n], self.arrival(3, 0), me, other).wait_send()

    near_xy = xy + (1 - c) * (1 - 2 * x) + c * (2 - 4 * y)
    whole = {8: 0, 9: 1, 10: 2}
    pieces = []
    for n in range(11):
        if n < 3:
            spec = (wide, 48, n * 768, 384, [(win_s, k * D + n * 256, 128) for k in range(3)])
        elif n == 3:
            spec = (wide, 48, OUT, 384, [(wout_s, 0, 384)])
        elif n < 8:
            spec = (wide, 48, EXP + (n - 4) * 768, 384, [(wexp_s, (n - 4) * 768, 384)])
        else:
            spec = (wcon, 192, (n - 8) * 256, 128, [(wcon_s, (n - 8) * 256, 128)])
        pieces.append(Piece(n, *spec, whole=whole.get(n)))

    loose = {}

    def run(ops):
        for op in ops:
            name, _, rest = op.partition(":")
            if op in loose:
                loose[op]()
            elif "." in rest:
                p, k = rest.split(".")
                getattr(pieces[int(p)], name)(int(k))
            else:
                getattr(pieces[int(rest)], name)()


    def small(stage, k, recv):
        d = send(vec.at[pl.ds(0, k)], vec.at[pl.ds(0, k)], vs.at[stage], vs.at[3 + stage], me, other)
        d.wait_recv() if recv else d.wait_send()

    swap_tok = send(tokens, tokr, swap_sem.at[0, 0], swap_sem.at[0, 1], me, other)
    swap_cot = send(cot, cotr, swap_sem.at[1, 0], swap_sem.at[1, 1], me, other)
    own_tok = pltpu.make_async_copy(tokens, tok, ls.at[11])
    own_cot = pltpu.make_async_copy(cot, cotn, ls.at[12])

    own_tok.start()
    pack[...] = jnp.zeros_like(pack)
    wide_bias = vectors[8][...].astype(F32).reshape(1, 192)
    for k in range(8):
        pack[k : k + 1, 0:48] = vectors[k][...].astype(F32)
    for k in range(4):
        pack[k : k + 1, 64:112] = wide_bias[:, k * 48 : (k + 1) * 48]
    vec[me] = pack[...].astype(BF)

    row = seg[...].astype(F32)
    first_row = jnp.zeros((1, 1), F32)
    for d in range(DOCS):
        size = jnp.sum(jnp.where(row == d, 1.0, 0.0), axis=1, keepdims=True)
        before = jnp.sum(jnp.where(row < d, 1.0, 0.0), axis=1, keepdims=True)
        first_row = first_row + jnp.where(size == T, before, 0.0)
    keep_row = lax.broadcasted_iota(jnp.int32, (1, T), 1).astype(F32) >= first_row
    mine = seg[:, pl.ds(al(c * T, 128), T)].astype(F32)
    theirs = seg[:, pl.ds(al(other * T, 128), T)].astype(F32)
    seg_row = jnp.where(keep_row, mine, theirs)
    seg_col = jnp.broadcast_to(seg_row, (128, T)).T[:, :1]
    keep_col = lax.broadcasted_iota(jnp.int32, (T, 1), 0).astype(F32) >= first_row
    keep_col = jnp.where(keep_col, 1.0, 0.0)
    sc1[...] = jnp.concatenate([keep_col, seg_col], axis=1)

    def mask_rows(i, _):
        r = pl.ds(al(i * 128, 128), 128)
        bias[r, :] = jnp.where(sc1[r, 1:2] == seg_row, 0.0, -1e30)
        return 0

    lax.fori_loop(0, T // 128, mask_rows, 0)
    pl.semaphore_wait(barrier, 6)
    for q in zs:
        send(vec.at[me], vec.at[me], vs.at[0], vs.at[3], q, c).start()
    loose["swap"] = swap_tok.start

    def swap_cotangent():
        swap_cot.start()
        own_cot.start()

    loose["swc"] = swap_cotangent

    def fill_start():
        own_tok.wait()
        swap_tok.wait_recv()

        def start_rows(i, _):
            r = pl.ds(al(i * 128, 128), 128)
            t = jnp.where(sc1[r, 0:1] > 0.5, tok[r, :].astype(F32), tokr[r, :].astype(F32)) + te[...]
            n1[r, :] = t
            xl[r, :] = t.astype(BF)
            return 0

        lax.fori_loop(0, T // 128, start_rows, 0)

    def small_near():
        small(0, 3, True)

        def one(k, _):
            b = vec.at[k * 4 + xy]
            send(b, b, vs.at[1], vs.at[4], near, c).start()
            return 0

        lax.fori_loop(0, 4, one, 0)

    def small_far():
        small(1, 4, True)

        def one(k, _):
            b = vec.at[(k // 2) * 4 + (1 - c) * 2 * y + c * x + lax.rem(k, 2) * (1 + c)]
            send(b, b, vs.at[2], vs.at[5], far, c).start()
            return 0

        lax.fori_loop(0, 8, one, 0)

    def fill_vectors():
        small(2, 8, True)
        for o in range(16):
            fullv[:, o * 48 : (o + 1) * 48] = vec[o][:, :48].astype(F32)
            for k in range(4):
                fulle[:, o * 192 + k * 48 : o * 192 + (k + 1) * 48] = vec[o][k : k + 1, 64:112].astype(F32)
        fullp[...] = jnp.concatenate([jnp.zeros_like(fullp[0:1, :]), jnp.ones_like(fullp[0:1, :])], axis=0)
        for h in range(D // 128):
            fullp[0:1, h * 384 : h * 384 + 128] = fullv[0:1, h * 128 : (h + 1) * 128]
            fullp[0:1, h * 384 + 256 : h * 384 + 384] = fullv[1:2, h * 128 : (h + 1) * 128]
            fullp[1:2, h * 384 : h * 384 + 128] = jnp.full((1, 128), HD**-0.5, F32)

    loose.update({"start": fill_start, "vec": fill_vectors, "vn": small_near, "vf": small_far})
    run(['s1:0', 's1:1', 's2o:9', 's1:2', 's2o:8', 'swap', 's2o:0', 's2o:10', 's2n:9', 's2o:2', 'start', 's1:3', 's2n:8', 's3:0.0', 's1:4', 's2o:1', 's2:0.1', 's2:0.2', 's2o:4', 's1:7', 's4:0.0', 's2o:7', 's2:0.3', 'vn', 'swc', 's3:0.1', 's2n:10', 's1:5', 's1:6', 's3:0.2', 's2:1', 's3:0.3', 'vf', 's4:0.1', 's2o:6', 's2o:3', 's2:2', 's4:0.2', 's3:1', 's4:0.3', 's2:3', 'vec'])

    def project(g):
        cs = pl.ds(al(g * 768, 768), 768)
        proj[:, cs] = ((nn(xl[...], wide[:, cs]) + fullp[0:1, cs]) * fullp[1:2, cs]).astype(BF)

    lane = lax.broadcasted_iota(jnp.int32, (1, 128), 1)
    halves = (lane < HD, lane >= HD)
    pairs = D // 128

    def keep(h, a):
        return pltpu.make_async_copy(pslot.at[a], spill.at[h * 2 + a], ps.at[a])

    tasks = [
        ['s4:1', 's3:3', 's2:7'],
        ['s1:9', 's2:5', 's4:2'],
        [],
        ['s5:9', 's3:5', 's3:6', 's3:7', 's2:8'],
        [],
        ['s4:5', 's3:8', 's3:9', 's2:10'],
    ]
    between = [['s2o:5', 's3:2', 's1:8', 's2:4'], ['s1:10', 's3:4', 's2:6'], ['s4:3', 's5:8', 's4:4', 's2:9', 's5:10']]

    def attend(h, _):
        for g in range(3):

            @pl.when(h == 2 * g)
            def _():
                pieces[g].done()

        @pl.when(lax.rem(h, 2) == 0)
        def _():
            project(h // 2)

        for g in range(3):
            if between[g]:

                @pl.when(h == 2 * g)
                def _():
                    run(between[g])

        cs = al(h * 384, 128)
        q2 = proj[:, pl.ds(cs, 128)]
        k2 = proj[:, pl.ds(cs + 128, 128)]
        v2 = proj[:, pl.ds(cs + 256, 128)]
        outs = []
        for a in range(2):
            s = nt(jnp.where(halves[a], q2, jnp.zeros_like(q2)), k2) + bias[...]
            e = jnp.exp(s - jnp.max(s, axis=-1, keepdims=True))
            p = (e * (1.0 / jnp.sum(e, axis=-1, keepdims=True))).astype(BF)

            @pl.when(h > 0)
            def _():
                keep(h - 1, a).wait()

            pslot[a] = p
            keep(h, a).start()
            outs.append(nn(p, v2))
        heads[:, pl.ds(al(h * 128, 128), 128)] = jnp.where(halves[0], outs[0], outs[1]).astype(BF)
        for k in range(pairs):

            @pl.when(h == k)
            def _():
                run(tasks[k])

        return 0

    lax.fori_loop(0, pairs, attend, 0)
    pieces[3].done()

    def load(h, a):
        return pltpu.make_async_copy(spill.at[h * 2 + a], pslot.at[a], pd.at[a])

    for a in range(2):
        keep(pairs - 1, a).wait()
        load(0, a).start()

    def normalize(v):
        centred = v - jnp.mean(v, axis=-1, keepdims=True)
        scale = lax.rsqrt(jnp.mean(centred * centred, axis=-1, keepdims=True) + 1e-5)
        return centred * scale, scale

    def first_rows(i, _):
        r = pl.ds(al(i * 256, 256), 256)
        v = n1[r, :] + (nn(heads[r, :], wide[:, OUT:EXP]) + fullv[2:3, :])
        n, s = normalize(v)
        n1[r, :] = n
        sc1[r, 1:2] = s
        fl[r, :] = (n * fullv[3:4, :] + fullv[4:5, :]).astype(BF)
        return 0

    lax.fori_loop(0, T // 256, first_rows, 0)
    run(['s4:7', 's4:6'])
    after = [
        [],
        ['s3:10', 's4:8'],
        ['s4:9'],
        ['s4:10'],
    ]

    def expand(i, _):
        for k in range(4):

            @pl.when(i == k)
            def _():
                pieces[4 + k].done()

        cs = pl.ds(al(i * 768, 768), 768)
        u = nn(fl[...], wide[:, pl.ds(al(EXP + i * 768, 768), 768)]) + fulle[:, cs]
        cdf = 0.5 * (1.0 + lax.erf(u * math.sqrt(0.5)))
        hidden[:, cs] = (u * cdf).astype(BF)
        slope[:, cs] = (cdf + u * jnp.exp(-0.5 * u * u) * (1.0 / math.sqrt(2.0 * math.pi))).astype(BF)
        for k in range(4):

            @pl.when(i == k)
            def _():
                run(after[k])

        return 0

    lax.fori_loop(0, FF // 768, expand, 0)

    pieces[8].done()
    sg[:, :256] = nn(hidden[...], wcon[:, :256]) + fullv[5:6, :256]
    run([])
    pieces[9].done()
    run([])
    pieces[10].done()
    run([])
    own_cot.wait()
    swap_cot.wait_recv()

    gv[...] = jnp.zeros_like(gv)

    def second_rows(i, _):
        r = pl.ds(al(i * 256, 256), 256)
        v = jnp.concatenate([sg[r, :256], nn(hidden[r, :], wcon[:, 256:]) + fullv[5:6, 256:]], axis=1)
        v = v + (n1[r, :] * fullv[3:4, :] + fullv[4:5, :])
        n, s = normalize(v)
        lonew[r, :] = (n * fullv[6:7, :] + fullv[7:8, :]).astype(BF)
        og = jnp.where(sc1[r, 0:1] > 0.5, cotn[r, :].astype(F32), cotr[r, :].astype(F32))
        gv[6:7, :] += jnp.sum(og * n, axis=0, keepdims=True)
        gv[7:8, :] += jnp.sum(og, axis=0, keepdims=True)
        w = og * fullv[6:7, :]
        g = s * (w - jnp.mean(w, axis=-1, keepdims=True) - n * jnp.mean(w * n, axis=-1, keepdims=True))
        sg[r, :] = g
        low = g.astype(BF)
        bg[r, :] = low
        gv[5:6, :] += jnp.sum(low.astype(F32), axis=0, keepdims=True)
        return 0

    lax.fori_loop(0, T // 256, second_rows, 0)
    swap_lo = send(lonew, lor, swap_sem.at[2, 0], swap_sem.at[2, 1], me, other)
    swap_lo.start()

    S = 384
    my_k = (1 - c) * x + c * y
    far_base = (1 - c) * (2 - 2 * y) + c * (1 - x)
    own_base = (1 - c) * 2 * y + c * x
    step_k = 1 + c

    def total(*refs):
        t = refs[0][...].astype(F32)
        for ref in refs[1:]:
            t = t + ref[...].astype(F32)
        return t

    class Red:
        def __init__(self, n, g, col, rows, recv, rcol, fsum, plane=None, width=384, parts=(), whole=None):
            self.n, self.g, self.col, self.rows, self.recv, self.rcol, self.fsum = n, g, col, rows, recv, rcol, fsum
            self.plane, self.width, self.parts, self.whole = plane, width, parts, whole
            self.paired = False

        def cols(self, core):
            return pl.ds(al(self.col + core * S, 128), self.width)

        def part(self, base, i, k=1, second=False):
            if self.plane is None:
                cs = pl.ds(self.rcol + (self.width if second else 0), self.width)
            else:
                cs = pl.ds(0, S)
                base = base + self.rcol
            return self.recv.at[pl.ds(al(base + i * self.rows, 16), k * self.rows), cs]

        def mine(self, o):
            base = 0 if self.plane is None else self.plane * 4
            return self.g.at[pl.ds(al((base + o) * self.rows, 16), self.rows), self.cols(c)]

        def planes(self):
            return 4 if self.plane is None else 1

        def rp(self, o, k=1):
            return self.part(0, o, k)

        def ra(self, i, k=1):
            return self.part(0 if self.plane is None else 768, i, k, True)

        def rb(self, i, k=1):
            return self.part(384 if self.plane is None else 1152, i, k, True)

        def rz(self, i, k=1):
            if self.plane is None:
                return self.part(576, i, k, True)
            return self.recv.at[pl.ds(al(5376 + i * self.rows, 16), k * self.rows), pl.ds(0, S)]

        def sem(self, stage):
            if stage > 4:
                return rs.at[self.n], rr.at[74 + self.whole * 3 + stage - 5]
            n = 0 if self.plane is not None and stage == 3 else self.n
            return rs.at[self.n], rr.at[n * 5 + stage]

        def got(self, stage, ref):
            s, r = self.sem(stage)
            send(ref, ref, s, r, me, other).wait_recv()

        def P(self):
            base = 0 if self.plane is None else self.plane * 4 * self.rows
            n = 4 * self.planes() * self.rows
            src = self.g.at[pl.ds(al(base, 16), n), self.cols(other)]
            s, r = self.sem(0)
            send(src, self.rp(0, 4 * self.planes()), s, r, me, other).start()

        def pair(self):
            if not self.paired:
                self.paired = True
                self.got(0, self.rp(0, 4 * self.planes()))

        def early(self, o, k=1):
            return [] if self.whole is None else [ry.at[pl.ds(al(self.whole * 192 + o * 48, 16), k * 48)]]

        def Y(self):
            self.pair()
            s, r = self.sem(5)
            p = lax.rem(z + 1, 4) * 4
            b = self.g.at[pl.ds(al(p * 48, 16), 192), self.cols(c)]
            b[...] = total(b, self.rp(p, 4)).astype(BF)
            send(b, self.early(0, 4)[0], s, r, zs[0], c).start()

        def A(self):
            self.pair()
            s, r = self.sem(1)

            def one(i, _):
                p = i // 2 if self.whole is None else lax.rem(z + 2 + i // 2, 4)
                o = p * 4 + far_base + lax.rem(i, 2) * step_k
                b = self.mine(o)
                b[...] = total(b, self.rp(o)).astype(BF)
                send(b, self.ra(p * 2 + lax.rem(i, 2)), s, r, far, c).start()
                return 0

            lax.fori_loop(0, 4 if self.whole is not None else 2 * self.planes(), one, 0)

        def A0(self):
            self.got(5, self.early(0, 4)[0])
            s, r = self.sem(6)
            for k in range(2):
                o = far_base + k * step_k
                b = self.mine(z * 4 + o)
                b[...] = total(b, self.rp(z * 4 + o), *self.early(o)).astype(BF)
                send(b, self.ra(z * 2 + k), s, r, far, c).start()

        def B(self):
            n = 2 if self.whole is not None else self.planes()
            self.got(1, self.ra(0, 2 * n))
            s, r = self.sem(2)

            def one(i, _):
                p = i if self.whole is None else lax.rem(z + 2 + i, 4)
                o = p * 4 + near_xy
                b = self.mine(o)
                b[...] = total(b, self.rp(o), self.ra(p * 2 + 1 - my_k)).astype(BF)
                send(b, self.rb(p), s, r, near, c).start()
                return 0

            lax.fori_loop(0, n, one, 0)

        def B0(self):
            self.got(6, self.ra(0, 2))
            s, r = self.sem(7)
            b = self.mine(z * 4 + near_xy)
            t = total(b, self.rp(z * 4 + near_xy), self.ra(z * 2 + 1 - my_k), *self.early(near_xy))
            b[...] = t.astype(BF)
            send(b, self.rb(z), s, r, near, c).start()

        def Z(self):
            self.got(2, self.rb(0, self.planes() if self.whole is None else 2))
            s, r = self.sem(3)
            if self.plane is None:
                for k in range(0 if self.whole is None else 1, 3):
                    p = lax.rem(z + k + 1, 4)
                    b = self.mine(p * 4 + xy)
                    b[...] = total(b, self.rp(p * 4 + xy), self.ra(p * 2 + my_k), self.rb(p)).astype(BF)
                    send(b, self.rz(k), s, r, zs[k], c).start()
            elif self.n > 0:
                b = self.mine(xy)
                b[...] = total(b, self.rp(xy), self.ra(my_k), self.rb(0)).astype(BF)
                send(b, self.rz(self.n - 1), s, r, zs[self.n - 1], c).start()

        def F(self):
            first = 0 if self.whole is None else 1
            self.got(3, self.rz(0, 3 - first))
            if first:
                self.got(7, self.rb(0))
            o, p = (z * 4 + xy, z) if self.plane is None else (xy, 0)
            last = [self.rz(k) for k in range(first, 3)] + self.early(xy)
            t = total(self.mine(o), self.rp(o), self.ra(p * 2 + my_k), self.rb(p), *last)
            s, r = self.sem(4)
            if self.parts:
                for i, k in enumerate(self.parts):
                    b = self.fsum.at[:, pl.ds(al(k + c * 128, 128), 128)]
                    b[...] = t[:, i * 128 : (i + 1) * 128]
                    send(b, b, s, r, me, other).start()
            else:
                b = self.fsum.at[:, pl.ds(al((self.n - 4 if 4 <= self.n < 8 else 0) * 768 + c * S, 128), S)]
                b[...] = t
                send(b, b, s, r, me, other).start()

        def end(self):
            if self.plane is None:
                m = wide.at[pl.ds(0, 528), pl.ds(0, 3 * self.width)]
            else:
                m = wide.at[pl.ds(0, 576 if self.n == 0 else 512), pl.ds(0, 1152)]
            send(m, m, rs.at[self.n], rr.at[self.n], me, other).wait_send()
            if self.plane is None or self.n == 0:
                self.got(4, self.fsum.at[:, pl.ds(0, self.width)])

    early = {0: 0, 1: 1}
    con = {j: Red(j, gcon, 0, 192, con_r, j * 1344, fcon, plane=lax.rem(z + j, 4)) for j in range(4)}
    exp = [Red(4 + k, wide, EXP + k * 768, 48, hidden, k * 768, fexp, whole=early.get(k)) for k in range(4)]
    out = Red(8, wide, OUT, 48, cotn, 0, fout)
    ins = [
        Red(9 + k, gin, k * 768, 48, slope, k * 768, fin, parts=[q * D + k * 256 for q in range(3)]) for k in range(2)
    ]
    for k, first in enumerate((512, 2 * D + 512, D + 512)):
        ins.append(Red(11 + k, gin, 1536 + (0, 256, 128)[k], 48, slope, 1536 + 256 * k, fin, width=128, parts=[first]))
    sums = {f"C{k}": con[k] for k in range(4)}
    sums.update({f"E{k}": exp[k] for k in range(4)})
    sums.update({f"I{k}": ins[k] for k in range(5)})
    sums["O"] = out

    def reduce(ops):
        for op in ops:
            name, _, rest = op.partition(":")
            if op in loose:
                loose[op]()
            else:
                getattr(sums[rest], name)()

    def steps(i, lists):
        for k, ops in enumerate(lists):
            if ops:

                @pl.when(i == k)
                def _():
                    reduce(ops)

    def send_back():
        def out_rows(i, _):
            r = pl.ds(al(i * 128, 128), 128)
            lonew[r, :] = jnp.where(sc1[r, 0:1] > 0.5, lonew[r, :].astype(F32), lor[r, :].astype(F32)).astype(BF)
            return 0

        swap_lo.wait()
        lax.fori_loop(0, T // 128, out_rows, 0)
        lo_done.start()

    lo_done = pltpu.make_async_copy(lonew, lo_o, ls.at[14])
    loose["lo"] = send_back

    def vsend(stage, src, dst, dp, seq):
        return send(src, dst, rs.at[14 + stage], rr.at[70 + stage], dp, seq)

    def v_partner():
        vout[...] = jnp.zeros_like(vout)
        for o in range(16):
            vout[o, :, 0:48] = gv[0:8, o * 48 : (o + 1) * 48]
            for k in range(4):
                vout[o, k : k + 1, 64:112] = ge[:, o * 192 + k * 48 : o * 192 + (k + 1) * 48]
        vsend(0, vout, vr.at[pl.ds(0, 16)], me, other).start()

    def v_flip_y():
        vsend(0, vout, vr.at[pl.ds(0, 16)], me, other).wait_recv()
        vsum[...] = vout[...] + vr[pl.ds(0, 16)]
        for i in range(8):
            vsend(1, vsum.at[(i // 2) * 4 + 2 - 2 * y + i % 2], vr.at[16 + i], flip_y, c).start()

    def v_flip_x():
        vsend(1, vr.at[pl.ds(16, 8)], vr.at[pl.ds(16, 8)], me, other).wait_recv()
        for i in range(8):
            o = (i // 2) * 4 + 2 * y + i % 2
            vsum[o] = vsum[o] + vr[16 + i]
        for i in range(4):
            vsend(2, vsum.at[i * 4 + 2 * y + 1 - x], vr.at[24 + i], flip_x, c).start()

    def v_planes():
        vsend(2, vr.at[pl.ds(24, 4)], vr.at[pl.ds(24, 4)], me, other).wait_recv()
        for i in range(4):
            vsum[i * 4 + xy] = vsum[i * 4 + xy] + vr[24 + i]
        for k in range(3):
            vsend(3, vsum.at[lax.rem(z + k + 1, 4) * 4 + xy], vr.at[28 + k], zs[k], c).start()

    def v_total():
        vsend(3, vr.at[pl.ds(28, 3)], vr.at[pl.ds(28, 3)], me, other).wait_recv()
        vr[31] = vsum[z * 4 + xy] + vr[28] + vr[29] + vr[30]
        v_done.start()

    v_done = pltpu.make_async_copy(vr.at[31], gvec_o, ls.at[16])
    loose.update({"vP": v_partner, "vA": v_flip_y, "vB": v_flip_x, "vZ": v_planes, "vF": v_total})

    ig_mine, ig_theirs = bg, fl
    swap_ig = [
        send(ig_mine.at[pl.ds(256 * k, 256)], ig_theirs.at[pl.ds(256 * k, 256)], sw3.at[0, k], sw3.at[1, k], me, other)
        for k in range(3)
    ]
    for k in range(3):
        loose[f"swg{k}"] = swap_ig[k].start
    ig_done = pltpu.make_async_copy(sg, ig_o, ls.at[15])

    def take_rows():
        for d in swap_ig:
            d.wait_recv()

        def grad_rows(i, _):
            r = pl.ds(al(i * 128, 128), 128)
            sg[r, :] = jnp.where(sc1[r, 0:1] > 0.5, sg[r, :], ig_theirs[r, :].astype(F32))
            return 0

        lax.fori_loop(0, T // 128, grad_rows, 0)
        ig_done.start()

    loose["sel"] = take_rows

    def grad_con(i, _):
        p = al(lax.rem(z + i + 1, 4) * 768, 768)
        gcon[pl.ds(p, 768), :] = tn(hidden[:, pl.ds(p, 768)], bg[...]).astype(BF)
        steps(i, [['P:C1'], ['P:C2'], [], ['A:C1', 'P:C3']])
        return 0

    lax.fori_loop(0, 4, grad_con, 0)

    def expand_back(i, _):
        cs = pl.ds(al(i * 768, 768), 768)
        g = (nt(bg[...], wcon[cs, :]) * slope[:, cs].astype(F32)).astype(BF)
        slope[:, cs] = g
        ge[:, cs] = jnp.sum(g.astype(F32), axis=0, keepdims=True)
        steps(i, [[], ['A:C2'], [], ['A:C3', 'P:C0']])
        return 0

    lax.fori_loop(0, FF // 768, expand_back, 0)

    def first_back(i, _):
        r = pl.ds(al(i * 256, 256), 256)
        g = sg[r, :] + nt(slope[r, :], wide[:, EXP:])
        n = n1[r, :]
        gv[3:4, :] += jnp.sum(g * n, axis=0, keepdims=True)
        gv[4:5, :] += jnp.sum(g, axis=0, keepdims=True)
        w = g * fullv[3:4, :]
        g = sc1[r, 1:2] * (w - jnp.mean(w, axis=-1, keepdims=True) - n * jnp.mean(w * n, axis=-1, keepdims=True))
        sg[r, :] = g
        low = g.astype(BF)
        bg[r, :] = low
        gv[2:3, :] += jnp.sum(low.astype(F32), axis=0, keepdims=True)
        steps(i, [['B:C1'], [], ['A:C0']])
        return 0

    lax.fori_loop(0, T // 256, first_back, 0)
    for p in pieces[4:8]:
        p.drain()

    def grad_exp(i, _):
        cs = pl.ds(al(i * 768, 768), 768)
        wide[:, pl.ds(al(EXP + i * 768, 768), 768)] = tn(fl[...], slope[:, cs]).astype(BF)
        steps(i, [[], ['B:C2', 'P:E0'], ['P:E1', 'Z:C1', 'B:C3'], []])
        return 0

    lax.fori_loop(0, 4, grad_exp, 0)
    hg = cotr
    hg[...] = nt(bg[...], wide[:, OUT:EXP]).astype(BF)
    reduce(['A:E0', 'Y:E0'])
    pieces[3].drain()
    wide[:, OUT:EXP] = tn(heads[...], bg[...]).astype(BF)
    reduce(['P:O', 'Y:E1', 'B:C0', 'A:E1', 'P:E2'])

    tasks = [['Z:C3', 'A:O'], [], ['B:E0', 'Z:C2', 'Z:C0', 'B:O'], ['A:I0'], ['A:E3'], []]
    after = [['A:E2', 'P:E3', 'P:I0'], ['B:E1'], ['P:I2', 'F:C0', 'Z:O', 'B:I0', 'P:I3', 'Z:E1', 'P:I4', 'P:I1']]

    def attend_back(h, _):
        cs = al(h * 384, 128)
        hs = pl.ds(al(h * 128, 128), 128)
        q2 = proj[:, pl.ds(cs, 128)]
        k2 = proj[:, pl.ds(cs + 128, 128)]
        v2 = proj[:, pl.ds(cs + 256, 128)]
        g2 = hg[:, hs]
        prod = g2.astype(F32) * heads[:, hs].astype(F32)
        qt = q2.astype(F32).T.astype(BF)
        gt = g2.astype(F32).T.astype(BF)
        dq, dk, dv = [], [], []
        for a in range(2):
            load(h, a).wait()
            rowdot = jnp.sum(jnp.where(halves[a], prod, 0.0), axis=-1, keepdims=True)
            p = pslot[a]
            dp = nt(jnp.where(halves[a], g2, jnp.zeros_like(g2)), v2)
            ds = (p.astype(F32) * (dp - rowdot)).astype(BF)
            dq.append(nn(ds, k2))
            dk.append(nn(qt[a * HD : (a + 1) * HD], ds))
            dv.append(nn(gt[a * HD : (a + 1) * HD], p))

            @pl.when(h + 1 < pairs)
            def _():
                load(h + 1, a).start()

        dq = (jnp.where(halves[0], dq[0], dq[1]) * HD**-0.5).astype(BF)
        dk = jnp.concatenate(dk, axis=0).T.astype(BF)
        dv = jnp.concatenate(dv, axis=0).T.astype(BF)
        proj[:, pl.ds(cs, 128)] = dq
        proj[:, pl.ds(cs + 128, 128)] = dk
        proj[:, pl.ds(cs + 256, 128)] = dv
        gv[0:1, hs] = jnp.sum(dq.astype(F32), axis=0, keepdims=True)
        gv[1:2, hs] = jnp.sum(dv.astype(F32), axis=0, keepdims=True)

        steps(h, tasks)

        @pl.when(lax.rem(h, 2) == 1)
        def _():
            cols = pl.ds(al((h // 2) * 768, 768), 768)
            gin[:, cols] = tn(xl[...], proj[:, cols]).astype(BF)

        steps((h - 1) // 2 + 8 * (1 - lax.rem(h, 2)), after)
        return 0

    lax.fori_loop(0, pairs, attend_back, 0)

    def input_rows(i, _):
        r = pl.ds(al(i * 256, 256), 256)
        g = sg[r, :] + nt(proj[r, :], wide[:, IN:OUT])
        sg[r, :] = g
        ig_mine[r, :] = g.astype(BF)
        steps(i, [['vP', 'A:I2', 'Z:E0', 'A:I3', 'B:E3'], ['B:E2', 'A:I4', 'A:I1'], ['A0:E1', 'Z:I0', 'Z:E3', 'Z:E2', 'swg2', 'B:I2', 'B:I3', 'B:I4', 'B:I1', 'lo', 'swg0', 'swg1', 'F:I0', 'Z:I2', 'Z:I3', 'Z:I4', 'vA', 'Z:I1', 'sel', 'F:O', 'A0:E0', 'vB', 'B0:E1', 'B0:E0', 'F:E1', 'F:E2', 'vZ', 'F:I3', 'F:E0', 'F:I4', 'F:E3', 'F:I2', 'F:I1', 'vF']])
        return 0

    lax.fori_loop(0, T // 256, input_rows, 0)
    outs = [lo_done, ig_done, v_done]
    for k, (v, o) in enumerate([(fcon, gcon_o), (fexp, gexp_o), (fout, gout_o), (fin, gin_o)]):
        for p in [[con[0]], exp, [out], ins][k]:
            p.end()
        outs.append(pltpu.make_async_copy(v, o, ls.at[17 + k]))
        outs[-1].start()
    for k in (1, 2, 3):
        con[k].end()
    swap_tok.wait_send()
    swap_cot.wait_send()
    for d in swap_ig:
        d.wait_send()
    for p in pieces[0:3] + pieces[8:]:
        p.drain()
    for stage, k in ((0, 3), (1, 4), (2, 8)):
        small(stage, k, False)
        m = vr.at[pl.ds(0, (8, 4, 3)[stage])]
        vsend(stage + 1, m, m, me, other).wait_send()
    vsend(0, vout, vr.at[pl.ds(0, 16)], me, other).wait_send()
    for o in outs:
        o.wait()


def fused_layer(tokens, time_embed, segments, iw, ow, ew, cw, vectors, cot):
    T, D = tokens.shape
    FF = ew.shape[1]
    sh = jax.ShapeDtypeStruct
    anyspec = pl.BlockSpec(memory_space=pl.ANY)
    vspec = pl.BlockSpec(memory_space=VM)
    scratch = [
        VM((D, 4 * D + FF), BF), VM((FF, D), BF),
        VM((T, D), BF), VM((T, D), BF), VM((T, D), BF), VM((T, D), BF),
        VM((16, 16, 128), BF), VM((16, 128), F32), VM((16, D), F32), VM((1, FF), F32), VM((2, 3 * D), F32),
        VM((T, 3 * D), BF), VM((T, D), BF), VM((T, D), F32), VM((T, T), F32),
        VM((T, 2), F32), VM((T, D), BF), VM((T, D), BF), VM((T, FF), BF), VM((T, FF), BF),
        VM((2, T, T), BF), VM((T, D), BF),
        VM((D, 3 * D), BF), VM((FF, D), BF), VM((5952, 384), BF), VM((768, 384), BF), VM((8, D), F32), VM((1, FF), F32),
        VM((16, 8, 128), F32), VM((16, 8, 128), F32), VM((32, 8, 128), F32),
        VM(iw.shape, F32), VM(ow.shape, F32), VM(ew.shape, F32), VM(cw.shape, F32),
        DMA((3, 2)), DMA((2, 3)), DMA((21,)), DMA((11,)), DMA((65,)), DMA((6,)), DMA((2,)), DMA((18,)), DMA((80,)), DMA((2,)),
    ]
    return pl.pallas_call(
        fused_kernel,
        out_shape=(
            sh((T, D), BF), sh((T, D), F32), sh(iw.shape, F32), sh(ow.shape, F32), sh(ew.shape, F32),
            sh(cw.shape, F32), sh((8, 128), F32), sh((D // HD, T, T), BF),
        ),
        in_specs=[anyspec, anyspec, vspec, vspec, anyspec, anyspec, anyspec, anyspec] + [vspec] * 9,
        out_specs=(anyspec,) * 8,
        scratch_shapes=scratch,
        compiler_params=pltpu.CompilerParams(
            collective_id=0, has_side_effects=True, vmem_limit_bytes=67043328
        ),
    )(tokens, cot, time_embed, segments, iw, ow, ew, cw, *vectors)


epsilon = 1e-05
masked_score = -1e30


def matmul(left, right):
    return jnp.dot(left, right, preferred_element_type=jnp.float32)


def product_tn(left, right):
    return lax.dot_general(
        left, right, (((0,), (0,)), ((), ())), preferred_element_type=jnp.float32
    )


def product_nt(left, right):
    return lax.dot_general(
        left, right, (((1,), (1,)), ((), ())), preferred_element_type=jnp.float32
    )


def normalize(values):
    mean = jnp.mean(values, axis=-1, keepdims=True)
    centred = values - mean
    scale = lax.rsqrt(jnp.mean(centred * centred, axis=-1, keepdims=True) + epsilon)
    return (centred * scale, scale)


def norm_back(grad, normed, scale, gain):
    scaled = grad * gain
    return scale * (
        scaled
        - jnp.mean(scaled, axis=-1, keepdims=True)
        - normed * jnp.mean(scaled * normed, axis=-1, keepdims=True)
    )


def gelu_value(values):
    return 0.5 * values * (1.0 + lax.erf(values * math.sqrt(0.5)))


def gelu_slope(values):
    return 0.5 * (1.0 + lax.erf(values * math.sqrt(0.5))) + values * jnp.exp(
        -0.5 * values * values
    ) / math.sqrt(2.0 * math.pi)


def attend_forward(item):
    query, key, value, segment_row = item
    length, depth = query.shape
    block = min(512, length)
    blocks = length // block
    scale = depth ** (-0.5)

    def one_block(part):
        query_block, segment_block = part
        scores = product_nt(query_block, key) * scale
        scores = jnp.where(segment_block[:, None] == segment_row[None, :], scores, masked_score)
        top = jnp.max(scores, axis=-1, keepdims=True)
        expo = jnp.exp(scores - top)
        total = jnp.sum(expo, axis=-1, keepdims=True)
        probs_low = (expo / total).astype(jnp.bfloat16)
        return (matmul(probs_low, value).astype(jnp.bfloat16), (top + jnp.log(total))[:, 0])

    outputs, logsum = lax.map(
        one_block, (query.reshape(blocks, block, depth), segment_row.reshape(blocks, block))
    )
    return (outputs.reshape(length, depth), logsum.reshape(length))


def attend_backward(item):
    query, key, value, segment_row, logsum, out_grad = item
    length, depth = query.shape
    block = min(512, length)
    blocks = length // block
    scale = depth ** (-0.5)

    def one_block(carry, part):
        key_grad, value_grad = carry
        query_block, segment_block, logsum_block, grad_block = part
        scores = product_nt(query_block, key) * scale
        scores = jnp.where(segment_block[:, None] == segment_row[None, :], scores, masked_score)
        probs = jnp.exp(scores - logsum_block[:, None])
        probs_low = probs.astype(jnp.bfloat16)
        prob_grad = product_nt(grad_block, value)
        row_total = jnp.sum(probs * prob_grad, axis=-1, keepdims=True)
        score_grad = (probs * (prob_grad - row_total)).astype(jnp.bfloat16)
        query_grad = matmul(score_grad, key) * scale
        key_grad = key_grad + product_tn(score_grad, query_block) * scale
        value_grad = value_grad + product_tn(probs_low, grad_block)
        return ((key_grad, value_grad), query_grad.astype(jnp.bfloat16))

    zeros = jnp.zeros((length, depth), jnp.float32)
    parts = (
        query.reshape(blocks, block, depth),
        segment_row.reshape(blocks, block),
        logsum.reshape(blocks, block),
        out_grad.reshape(blocks, block, depth),
    )
    (key_grad, value_grad), query_grad = lax.scan(one_block, (zeros, zeros), parts)
    return (
        query_grad.reshape(length, depth),
        key_grad.astype(jnp.bfloat16),
        value_grad.astype(jnp.bfloat16),
    )


def plain_body(
    tokens,
    time_embed,
    segments,
    input_weight,
    query_bias,
    value_bias,
    output_weight,
    output_bias,
    first_gain,
    first_shift,
    expand_weight,
    expand_bias,
    contract_weight,
    contract_bias,
    second_gain,
    second_shift,
    cotangent,
):
    pairs = lax.axis_size("seq")
    seqs, half, width = tokens.shape
    length = half * pairs
    rows = seqs * half
    group = width // pairs
    heads_here = group // HD
    start = (tokens.astype(jnp.float32) + time_embed[:, None, :]).reshape(rows, width)
    start_low = start.astype(jnp.bfloat16)
    attention_set = (
        lax.all_gather(input_weight, "dp", axis=0, tiled=True),
        lax.all_gather(output_weight, "dp", axis=0, tiled=True),
        lax.all_gather(query_bias, "dp", axis=0, tiled=True),
        lax.all_gather(value_bias, "dp", axis=0, tiled=True),
        lax.all_gather(output_bias, "dp", axis=0, tiled=True),
        lax.all_gather(first_gain, "dp", axis=0, tiled=True),
        lax.all_gather(first_shift, "dp", axis=0, tiled=True),
    )
    (
        full_input,
        full_output,
        full_query_bias,
        full_value_bias,
        full_output_bias,
        full_first_gain,
        full_first_shift,
    ) = attention_set
    bias_row = jnp.concatenate(
        [
            full_query_bias.astype(jnp.float32),
            jnp.zeros((width,), jnp.float32),
            full_value_bias.astype(jnp.float32),
        ]
    )
    projected_low = (matmul(start_low, full_input) + bias_row).astype(jnp.bfloat16)
    regrouped = lax.all_to_all(
        projected_low.reshape(seqs, half, 3, pairs, group),
        "seq",
        split_axis=3,
        concat_axis=1,
        tiled=True,
    )
    split = regrouped.reshape(seqs, length, 3, heads_here, HD).transpose(2, 0, 3, 1, 4)
    split = split.reshape(3, seqs * heads_here, length, HD)
    query_heads, key_heads, value_heads = (split[0], split[1], split[2])
    segment_heads = jnp.repeat(segments, heads_here, axis=0)
    heads_out, logsum = lax.map(
        attend_forward, (query_heads, key_heads, value_heads, segment_heads)
    )
    heads_tokens = (
        heads_out.reshape(seqs, heads_here, length, HD)
        .transpose(0, 2, 1, 3)
        .reshape(seqs, length, 1, group)
    )
    heads_low = lax.all_to_all(
        heads_tokens, "seq", split_axis=1, concat_axis=2, tiled=True
    ).reshape(rows, width)
    attention = matmul(heads_low, full_output) + full_output_bias.astype(jnp.float32)
    normed_one, scale_one = normalize(start + attention)
    gain_one = full_first_gain.astype(jnp.float32)
    first = normed_one * gain_one + full_first_shift.astype(jnp.float32)
    first_low = first.astype(jnp.bfloat16)
    network_set = (
        lax.all_gather(expand_weight, "dp", axis=0, tiled=True),
        lax.all_gather(contract_weight, "dp", axis=0, tiled=True),
        lax.all_gather(expand_bias, "dp", axis=0, tiled=True),
        lax.all_gather(contract_bias, "dp", axis=0, tiled=True),
        lax.all_gather(second_gain, "dp", axis=0, tiled=True),
        lax.all_gather(second_shift, "dp", axis=0, tiled=True),
    )
    (
        full_expand,
        full_contract,
        full_expand_bias,
        full_contract_bias,
        full_second_gain,
        full_second_shift,
    ) = network_set
    expand = matmul(first_low, full_expand) + full_expand_bias.astype(jnp.float32)
    hidden = gelu_value(expand).astype(jnp.bfloat16)
    second_sum = first + matmul(hidden, full_contract) + full_contract_bias.astype(jnp.float32)
    normed_two, scale_two = normalize(second_sum)
    gain_two = full_second_gain.astype(jnp.float32)
    layer_output = (normed_two * gain_two + full_second_shift.astype(jnp.float32)).astype(
        jnp.bfloat16
    )
    network_set = (
        lax.all_gather(expand_weight, "dp", axis=0, tiled=True),
        lax.all_gather(contract_weight, "dp", axis=0, tiled=True),
        lax.all_gather(expand_bias, "dp", axis=0, tiled=True),
        lax.all_gather(contract_bias, "dp", axis=0, tiled=True),
        lax.all_gather(second_gain, "dp", axis=0, tiled=True),
        lax.all_gather(second_shift, "dp", axis=0, tiled=True),
    )
    full_expand, full_contract = (network_set[0], network_set[1])
    out_grad = cotangent.astype(jnp.float32).reshape(rows, width)
    grad_second_gain = jnp.sum(out_grad * normed_two, axis=0)
    grad_second_shift = jnp.sum(out_grad, axis=0)
    second_grad = norm_back(out_grad, normed_two, scale_two, gain_two)
    branch_grad = second_grad.astype(jnp.bfloat16)
    grad_contract_bias = jnp.sum(branch_grad.astype(jnp.float32), axis=0)
    grad_contract_weight = product_tn(hidden, branch_grad)
    expand_grad = (product_nt(branch_grad, full_contract) * gelu_slope(expand)).astype(jnp.bfloat16)
    grad_expand_bias = jnp.sum(expand_grad.astype(jnp.float32), axis=0)
    grad_expand_weight = product_tn(first_low, expand_grad)
    first_grad = second_grad + product_nt(expand_grad, full_expand)
    grad_first_gain = jnp.sum(first_grad * normed_one, axis=0)
    grad_first_shift = jnp.sum(first_grad, axis=0)
    start_grad = norm_back(first_grad, normed_one, scale_one, gain_one)
    attention_set = (
        lax.all_gather(input_weight, "dp", axis=0, tiled=True),
        lax.all_gather(output_weight, "dp", axis=0, tiled=True),
        lax.all_gather(query_bias, "dp", axis=0, tiled=True),
        lax.all_gather(value_bias, "dp", axis=0, tiled=True),
        lax.all_gather(output_bias, "dp", axis=0, tiled=True),
        lax.all_gather(first_gain, "dp", axis=0, tiled=True),
        lax.all_gather(first_shift, "dp", axis=0, tiled=True),
    )
    full_input, full_output = (attention_set[0], attention_set[1])
    attention_grad = start_grad.astype(jnp.bfloat16)
    grad_output_bias = jnp.sum(attention_grad.astype(jnp.float32), axis=0)
    grad_output_weight = product_tn(heads_low, attention_grad)
    heads_grad = product_nt(attention_grad, full_output).astype(jnp.bfloat16)
    grad_heads = lax.all_to_all(
        heads_grad.reshape(seqs, half, pairs, group), "seq", split_axis=2, concat_axis=1, tiled=True
    )
    grad_heads = (
        grad_heads.reshape(seqs, length, heads_here, HD)
        .transpose(0, 2, 1, 3)
        .reshape(seqs * heads_here, length, HD)
    )
    query_grad, key_grad, value_grad = lax.map(
        attend_backward, (query_heads, key_heads, value_heads, segment_heads, logsum, grad_heads)
    )
    stacked = jnp.stack([query_grad, key_grad, value_grad]).reshape(3, seqs, heads_here, length, HD)
    stacked = stacked.transpose(1, 3, 0, 2, 4).reshape(seqs, length, 3, 1, group)
    projected_grad = lax.all_to_all(
        stacked, "seq", split_axis=1, concat_axis=3, tiled=True
    ).reshape(rows, 3 * width)
    grad_query_bias = jnp.sum(projected_grad[:, :width].astype(jnp.float32), axis=0)
    grad_value_bias = jnp.sum(projected_grad[:, 2 * width :].astype(jnp.float32), axis=0)
    grad_input_weight = product_tn(start_low, projected_grad)
    input_grad = (start_grad + product_nt(projected_grad, full_input)).reshape(seqs, half, width)
    grads = (
        grad_input_weight,
        grad_query_bias,
        grad_value_bias,
        grad_output_weight,
        grad_output_bias,
        grad_first_gain,
        grad_first_shift,
        grad_expand_weight,
        grad_expand_bias,
        grad_contract_weight,
        grad_contract_bias,
        grad_second_gain,
        grad_second_shift,
    )
    owned = (
        lax.psum_scatter(grads[0], "dp", scatter_dimension=0, tiled=True),
        lax.psum_scatter(grads[1], "dp", scatter_dimension=0, tiled=True),
        lax.psum_scatter(grads[2], "dp", scatter_dimension=0, tiled=True),
        lax.psum_scatter(grads[3], "dp", scatter_dimension=0, tiled=True),
        lax.psum_scatter(grads[4], "dp", scatter_dimension=0, tiled=True),
        lax.psum_scatter(grads[5], "dp", scatter_dimension=0, tiled=True),
        lax.psum_scatter(grads[6], "dp", scatter_dimension=0, tiled=True),
        lax.psum_scatter(grads[7], "dp", scatter_dimension=0, tiled=True),
        lax.psum_scatter(grads[8], "dp", scatter_dimension=0, tiled=True),
        lax.psum_scatter(grads[9], "dp", scatter_dimension=0, tiled=True),
        lax.psum_scatter(grads[10], "dp", scatter_dimension=0, tiled=True),
        lax.psum_scatter(grads[11], "dp", scatter_dimension=0, tiled=True),
        lax.psum_scatter(grads[12], "dp", scatter_dimension=0, tiled=True),
    )
    summed = (
        lax.psum(owned[0].astype(jnp.bfloat16), "seq").astype(jnp.float32),
        lax.psum(owned[1].astype(jnp.bfloat16), "seq").astype(jnp.float32),
        lax.psum(owned[2].astype(jnp.bfloat16), "seq").astype(jnp.float32),
        lax.psum(owned[3].astype(jnp.bfloat16), "seq").astype(jnp.float32),
        lax.psum(owned[4].astype(jnp.bfloat16), "seq").astype(jnp.float32),
        lax.psum(owned[5].astype(jnp.bfloat16), "seq").astype(jnp.float32),
        lax.psum(owned[6].astype(jnp.bfloat16), "seq").astype(jnp.float32),
        lax.psum(owned[7].astype(jnp.bfloat16), "seq").astype(jnp.float32),
        lax.psum(owned[8].astype(jnp.bfloat16), "seq").astype(jnp.float32),
        lax.psum(owned[9].astype(jnp.bfloat16), "seq").astype(jnp.float32),
        lax.psum(owned[10].astype(jnp.bfloat16), "seq").astype(jnp.float32),
        lax.psum(owned[11].astype(jnp.bfloat16), "seq").astype(jnp.float32),
        lax.psum(owned[12].astype(jnp.bfloat16), "seq").astype(jnp.float32),
    )
    return (layer_output.reshape(seqs, half, width), input_grad) + tuple(summed)


def finish_kernel(lo, ig, gi, go, ge, gc, vec, lo_o, ig_o, gi_o, go_o, ge_o, gc_o, *rest):
    small, bufs, sems = rest[:9], rest[9:15], rest[15]
    pairs = list(zip((ig, lo, ge, gi, gc, go), (bufs[1], bufs[0], bufs[4], bufs[2], bufs[5], bufs[3])))
    results = (ig_o, lo_o, ge_o, gi_o, gc_o, go_o)
    loads = [pltpu.make_async_copy(a, b, sems.at[0, k]) for k, (a, b) in enumerate(pairs)]
    stores = [pltpu.make_async_copy(b, r, sems.at[1, k]) for k, ((_, b), r) in enumerate(zip(pairs, results))]
    for d in loads:
        d.start()
    own = small[0].shape[1]
    for k in range(8):
        small[k][...] = vec[k : k + 1, :own]
    for k in range(4):
        small[8][:, k * own : (k + 1) * own] = vec[k : k + 1, 64 : 64 + own]
    for a, b in zip(loads, stores):
        a.wait()
        b.start()
    for b in stores:
        b.wait()


def finish(lo, ig, gi, go, ge, gc, vec, own):
    sh = jax.ShapeDtypeStruct
    anyspec = pl.BlockSpec(memory_space=pl.ANY)
    vspec = pl.BlockSpec(memory_space=VM)
    big = (lo, ig, gi, go, ge, gc)
    return pl.pallas_call(
        finish_kernel,
        out_shape=[sh(v.shape, v.dtype) for v in big] + [sh((1, own), F32)] * 8 + [sh((1, 4 * own), F32)],
        in_specs=[anyspec] * 6 + [vspec],
        out_specs=[anyspec] * 6 + [vspec] * 9,
        scratch_shapes=[VM(v.shape, v.dtype) for v in big] + [DMA((2, 6))],
    )(*big, vec)


def fused_body(
    tokens, time_embed, segments, input_weight, query_bias, value_bias, output_weight, output_bias, first_gain,
    first_shift, expand_weight, expand_bias, contract_weight, contract_bias, second_gain, second_shift, cotangent,
):
    vectors = [
        query_bias, value_bias, output_bias, first_gain, first_shift, contract_bias, second_gain, second_shift,
        expand_bias,
    ]
    own = query_bias.shape[0]
    vectors = [v.reshape(1, own) for v in vectors[:8]] + [expand_bias]
    parts = fused_layer(
        tokens[0], time_embed, segments, input_weight, output_weight, expand_weight, contract_weight, vectors,
        cotangent[0],
    )[:7]
    layer_output, input_grad, g_in, g_out, g_exp, g_con, *row = finish(*parts, own)
    row = [v.reshape(v.shape[1]) for v in row]
    return (
        layer_output[None], input_grad[None], g_in, row[0], row[1], g_out, row[2], row[3], row[4],
        g_exp, row[8], g_con, row[5], row[6], row[7],
    )


def body(*args):
    if lax.axis_size("dp") == 16 and lax.axis_size("seq") == 2:
        return fused_body(*args)
    return plain_body(*args)


def solution(mesh):
    return jax.shard_map(
        body,
        mesh=mesh,
        in_specs=(
            P("dp", "seq", None),
            P("dp", None),
            P("dp", None),
            P("dp", None),
            P("dp"),
            P("dp"),
            P("dp", None),
            P("dp"),
            P("dp"),
            P("dp"),
            P("dp", None),
            P("dp"),
            P("dp", None),
            P("dp"),
            P("dp"),
            P("dp"),
            P("dp", "seq", None),
        ),
        out_specs=(
            P("dp", "seq", None),
            P("dp", "seq", None),
            P("dp", None),
            P("dp"),
            P("dp"),
            P("dp", None),
            P("dp"),
            P("dp"),
            P("dp"),
            P("dp", None),
            P("dp"),
            P("dp", None),
            P("dp"),
            P("dp"),
            P("dp"),
        ),
        check_vma=False,
    )
```

```python
import functools
import math

import jax
import jax.numpy as jnp
from jax import lax
from jax.experimental import pallas as pl
from jax.experimental.pallas import tpu as pltpu
from jax.sharding import PartitionSpec as P

HD = 64
DOCS = 4
BF = jnp.bfloat16
F32 = jnp.float32
MESH = pl.DeviceIdType.MESH
VM = pltpu.VMEM
DMA = pltpu.SemaphoreType.DMA


def nn(a, b):
    return jnp.dot(a, b, preferred_element_type=F32)


def nt(a, b):
    return lax.dot_general(a, b, (((1,), (1,)), ((), ())), preferred_element_type=F32)


def tn(a, b):
    return lax.dot_general(a, b, (((0,), (0,)), ((), ())), preferred_element_type=F32)


def fused_kernel(
    tokens, cot, te, seg, win_s, wout_s, wexp_s, wcon_s, v0, v1, v2, v3, v4, v5, v6, v7, v8,
    lo_o, ig_o, gin_o, gout_o, gexp_o, gcon_o, gvec_o, spill,
    wide, wcon, tok, tokr, cotn, cotr, vec, pack, fullv, fulle, fullp, proj, xl, n1, sg,
    sc1, heads, fl, hidden, slope, pslot, bg,
    gin, gcon, con_r, ry, gv, ge, vout, vsum, vr, fin, fout, fexp, fcon,
    swap_sem, sw3, ls, gs, gr, vs, ps, rs, rr, pd,
):
    vectors = (v0, v1, v2, v3, v4, v5, v6, v7, v8)
    T, D = tok.shape
    FF = wcon.shape[0]
    IN, OUT, EXP = 0, 3 * D, 4 * D
    bias, lonew, lor = sg, tok, tokr
    me = lax.axis_index("dp")
    c = lax.axis_index("seq")
    x = lax.rem(me, 2)
    y = lax.rem(me // 2, 2)
    xy = lax.rem(me, 4)
    z = me // 4
    flip_x = me + 1 - 2 * x
    flip_y = me + 2 - 4 * y
    near = (1 - c) * flip_x + c * flip_y
    far = (1 - c) * flip_y + c * flip_x
    other = 1 - c
    zs = [lax.rem(z + k, 4) * 4 + xy for k in (1, 2, 3)]

    def send(src, dst, s, r, dp, seq):
        return pltpu.make_async_remote_copy(
            src_ref=src, dst_ref=dst, send_sem=s, recv_sem=r,
            device_id={"dp": dp, "seq": seq}, device_id_type=MESH,
        )

    barrier = pltpu.get_barrier_semaphore()
    for dp, seq in [(me, other), (near, c), (far, c)] + [(q, c) for q in zs]:
        pl.semaphore_signal(
            barrier, inc=1, device_id={"dp": dp, "seq": seq}, device_id_type=MESH
        )

    def al(v, m):
        return pl.multiple_of(v, m)

    class Piece:
        def __init__(self, n, buf, rows, col, half, shards, whole=None):
            self.n, self.buf, self.rows, self.col, self.half, self.shards = n, buf, rows, col, half, shards
            self.whole = whole
            self.low = 1 if whole is None else 2

        def cols(self, core):
            return pl.ds(al(self.col + core * self.half, 128), self.half)

        def block(self, o):
            return self.buf.at[pl.ds(al(o * self.rows, 16), self.rows), self.cols(c)]

        def region(self, k, core=c):
            return self.buf.at[pl.ds(0, k * self.rows), self.cols(core)]

        def arrival(self, stage, k):
            if stage > 3:
                return gr.at[56 + self.whole * 3 + stage - 4]
            return gr.at[stage * 4 + k] if self.n == 0 and stage < 3 else gr.at[12 + self.n * 4 + stage]

        def push(self, src, dst, stage, k, dp):
            send(src, dst, gs.at[self.n], self.arrival(stage, k), dp, c).start()

        def got(self, stage, k, blocks):
            m = self.region(blocks)
            send(m, m, gs.at[self.n], self.arrival(stage, k), me, other).wait_recv()

        def own(self):
            base = pl.ds(al(me * self.rows, 16), self.rows)
            for i, (ref, first, width) in enumerate(self.shards):
                yield (
                    ref.at[:, pl.ds(al(first + c * width, 128), width)],
                    self.buf.at[base, pl.ds(al(self.col + c * self.half + i * width, 128), width)],
                )

        def s1(self):
            for k in range(self.low - 1, 3):
                for a, b in self.own():
                    self.push(a, b, 0, k + 1, zs[k])
            for a, b in self.own():
                pltpu.make_async_copy(a, b, ls.at[self.n]).start()

        def s2o(self):
            for a, b in self.own():
                self.push(a, b, 1 if self.whole is None else 4, 0, near)
                self.push(a, b, 2 if self.whole is None else 5, 0, far)

        def s2n(self):
            self.got(4, 0, 1)
            b = self.block(z * 4 + near_xy)
            self.push(b, b, 5, 0, far)

        def s5(self):
            self.got(5, 0, 2)
            m = self.block(me)
            pltpu.make_async_copy(m, m, ls.at[self.n]).wait()
            p = self.buf.at[pl.ds(al(z * 4 * self.rows, 16), 4 * self.rows), self.cols(c)]
            self.push(p, p, 6, 0, zs[0])

        def s2(self, k=None):
            if k is None:
                self.got(0, 0, 4 - self.low)
            else:
                self.got(0, k, 1)

            def one(i, _):
                b = self.block(lax.rem(z + 4 - i, 4) * 4 + xy)
                self.push(b, b, 1, i, near)
                self.push(b, b, 2, i, far)
                return 0

            if k is None:
                lax.fori_loop(self.low, 4, one, 0)
            else:
                one(k, 0)

        def s3(self, k=None):
            if k is None:
                self.got(1, 0, 4 if self.whole is None else 2)
            else:
                self.got(1, k, 1)

            def one(i, _):
                b = self.block(lax.rem(z + 4 - i, 4) * 4 + near_xy)
                self.push(b, b, 2, i, far)
                return 0

            if k is None:
                lax.fori_loop(0 if self.whole is None else 2, 4, one, 0)
            else:
                one(k, 0)

        def s4(self, k=None):
            if k is None:
                self.got(2, 0, 8 if self.whole is None else 4)
            else:
                self.got(2, k, 2)
            if self.whole is not None:
                self.got(6, 0, 4)
            elif not k:
                m = self.block(me)
                pltpu.make_async_copy(m, m, ls.at[self.n]).wait()
            if k is None:
                p = self.region(16)
            else:
                p = self.buf.at[pl.ds(al(lax.rem(z + 4 - k, 4) * 4 * self.rows, 16), 4 * self.rows), self.cols(c)]
            send(p, p, gs.at[self.n], self.arrival(3, 0), me, other).start()

        def done(self):
            m = self.region(16, other)
            send(m, m, gs.at[self.n], self.arrival(3, 0), me, other).wait_recv()

        def drain(self):
            m = wide.at[pl.ds(0, 496), pl.ds(0, self.rows * self.half // 16)]
            send(m, m, gs.at[self.n], self.arrival(3, 0), me, other).wait_send()

    near_xy = xy + (1 - c) * (1 - 2 * x) + c * (2 - 4 * y)
    whole = {8: 0, 9: 1, 10: 2}
    pieces = []
    for n in range(11):
        if n < 3:
            spec = (wide, 48, n * 768, 384, [(win_s, k * D + n * 256, 128) for k in range(3)])
        elif n == 3:
            spec = (wide, 48, OUT, 384, [(wout_s, 0, 384)])
        elif n < 8:
            spec = (wide, 48, EXP + (n - 4) * 768, 384, [(wexp_s, (n - 4) * 768, 384)])
        else:
            spec = (wcon, 192, (n - 8) * 256, 128, [(wcon_s, (n - 8) * 256, 128)])
        pieces.append(Piece(n, *spec, whole=whole.get(n)))

    loose = {}

    def run(ops):
        for op in ops:
            name, _, rest = op.partition(":")
            if op in loose:
                loose[op]()
            elif "." in rest:
                p, k = rest.split(".")
                getattr(pieces[int(p)], name)(int(k))
            else:
                getattr(pieces[int(rest)], name)()


    def small(stage, k, recv):
        d = send(vec.at[pl.ds(0, k)], vec.at[pl.ds(0, k)], vs.at[stage], vs.at[3 + stage], me, other)
        d.wait_recv() if recv else d.wait_send()

    swap_tok = send(tokens, tokr, swap_sem.at[0, 0], swap_sem.at[0, 1], me, other)
    swap_cot = send(cot, cotr, swap_sem.at[1, 0], swap_sem.at[1, 1], me, other)
    own_tok = pltpu.make_async_copy(tokens, tok, ls.at[11])
    own_cot = pltpu.make_async_copy(cot, cotn, ls.at[12])

    own_tok.start()
    pack[...] = jnp.zeros_like(pack)
    wide_bias = vectors[8][...].astype(F32).reshape(1, 192)
    for k in range(8):
        pack[k : k + 1, 0:48] = vectors[k][...].astype(F32)
    for k in range(4):
        pack[k : k + 1, 64:112] = wide_bias[:, k * 48 : (k + 1) * 48]
    vec[me] = pack[...].astype(BF)

    row = seg[...].astype(F32)
    first_row = jnp.zeros((1, 1), F32)
    for d in range(DOCS):
        size = jnp.sum(jnp.where(row == d, 1.0, 0.0), axis=1, keepdims=True)
        before = jnp.sum(jnp.where(row < d, 1.0, 0.0), axis=1, keepdims=True)
        first_row = first_row + jnp.where(size == T, before, 0.0)
    keep_row = lax.broadcasted_iota(jnp.int32, (1, T), 1).astype(F32) >= first_row
    mine = seg[:, pl.ds(al(c * T, 128), T)].astype(F32)
    theirs = seg[:, pl.ds(al(other * T, 128), T)].astype(F32)
    seg_row = jnp.where(keep_row, mine, theirs)
    seg_col = jnp.broadcast_to(seg_row, (128, T)).T[:, :1]
    keep_col = lax.broadcasted_iota(jnp.int32, (T, 1), 0).astype(F32) >= first_row
    keep_col = jnp.where(keep_col, 1.0, 0.0)
    sc1[...] = jnp.concatenate([keep_col, seg_col], axis=1)

    def mask_rows(i, _):
        r = pl.ds(al(i * 128, 128), 128)
        bias[r, :] = jnp.where(sc1[r, 1:2] == seg_row, 0.0, -1e30)
        return 0

    lax.fori_loop(0, T // 128, mask_rows, 0)
    pl.semaphore_wait(barrier, 6)
    for q in zs:
        send(vec.at[me], vec.at[me], vs.at[0], vs.at[3], q, c).start()
    loose["swap"] = swap_tok.start

    def swap_cotangent():
        swap_cot.start()
        own_cot.start()

    loose["swc"] = swap_cotangent

    def fill_start():
        own_tok.wait()
        swap_tok.wait_recv()

        def start_rows(i, _):
            r = pl.ds(al(i * 128, 128), 128)
            t = jnp.where(sc1[r, 0:1] > 0.5, tok[r, :].astype(F32), tokr[r, :].astype(F32)) + te[...]
            n1[r, :] = t
            xl[r, :] = t.astype(BF)
            return 0

        lax.fori_loop(0, T // 128, start_rows, 0)

    def small_near():
        small(0, 3, True)

        def one(k, _):
            b = vec.at[k * 4 + xy]
            send(b, b, vs.at[1], vs.at[4], near, c).start()
            return 0

        lax.fori_loop(0, 4, one, 0)

    def small_far():
        small(1, 4, True)

        def one(k, _):
            b = vec.at[(k // 2) * 4 + (1 - c) * 2 * y + c * x + lax.rem(k, 2) * (1 + c)]
            send(b, b, vs.at[2], vs.at[5], far, c).start()
            return 0

        lax.fori_loop(0, 8, one, 0)

    def fill_vectors():
        small(2, 8, True)
        for o in range(16):
            fullv[:, o * 48 : (o + 1) * 48] = vec[o][:, :48].astype(F32)
            for k in range(4):
                fulle[:, o * 192 + k * 48 : o * 192 + (k + 1) * 48] = vec[o][k : k + 1, 64:112].astype(F32)
        fullp[...] = jnp.concatenate([jnp.zeros_like(fullp[0:1, :]), jnp.ones_like(fullp[0:1, :])], axis=0)
        for h in range(D // 128):
            fullp[0:1, h * 384 : h * 384 + 128] = fullv[0:1, h * 128 : (h + 1) * 128]
            fullp[0:1, h * 384 + 256 : h * 384 + 384] = fullv[1:2, h * 128 : (h + 1) * 128]
            fullp[1:2, h * 384 : h * 384 + 128] = jnp.full((1, 128), HD**-0.5, F32)

    loose.update({"start": fill_start, "vec": fill_vectors, "vn": small_near, "vf": small_far})
    run(['s1:0', 's1:1', 's2o:9', 's1:2', 's2o:8', 'swap', 's2o:0', 's2o:10', 's2n:9', 's2o:2', 'start', 's1:3', 's2n:8', 's3:0.0', 's1:4', 's2o:1', 's2:0.1', 's2:0.2', 's2o:4', 's1:7', 's4:0.0', 's2o:7', 's2:0.3', 'vn', 'swc', 's3:0.1', 's2n:10', 's1:5', 's1:6', 's3:0.2', 's2:1', 's3:0.3', 'vf', 's4:0.1', 's2o:6', 's2o:3', 's2:2', 's4:0.2', 's3:1', 's4:0.3', 's2:3', 'vec'])

    def project(g):
        cs = pl.ds(al(g * 768, 768), 768)
        proj[:, cs] = ((nn(xl[...], wide[:, cs]) + fullp[0:1, cs]) * fullp[1:2, cs]).astype(BF)

    lane = lax.broadcasted_iota(jnp.int32, (1, 128), 1)
    halves = (lane < HD, lane >= HD)
    pairs = D // 128

    def keep(h, a):
        return pltpu.make_async_copy(pslot.at[a], spill.at[h * 2 + a], ps.at[a])

    tasks = [
        ['s4:1', 's3:3', 's2:7'],
        ['s1:9', 's2:5', 's4:2'],
        [],
        ['s5:9', 's3:5', 's3:6', 's3:7', 's2:8'],
        [],
        ['s4:5', 's3:8', 's3:9', 's2:10'],
    ]
    between = [['s2o:5', 's3:2', 's1:8', 's2:4'], ['s1:10', 's3:4', 's2:6'], ['s4:3', 's5:8', 's4:4', 's2:9', 's5:10']]

    def attend(h, _):
        for g in range(3):

            @pl.when(h == 2 * g)
            def _():
                pieces[g].done()

        @pl.when(lax.rem(h, 2) == 0)
        def _():
            project(h // 2)

        for g in range(3):
            if between[g]:

                @pl.when(h == 2 * g)
                def _():
                    run(between[g])

        cs = al(h * 384, 128)
        q2 = proj[:, pl.ds(cs, 128)]
        k2 = proj[:, pl.ds(cs + 128, 128)]
        v2 = proj[:, pl.ds(cs + 256, 128)]
        outs = []
        for a in range(2):
            s = nt(jnp.where(halves[a], q2, jnp.zeros_like(q2)), k2) + bias[...]
            e = jnp.exp(s - jnp.max(s, axis=-1, keepdims=True))
            p = (e * (1.0 / jnp.sum(e, axis=-1, keepdims=True))).astype(BF)

            @pl.when(h > 0)
            def _():
                keep(h - 1, a).wait()

            pslot[a] = p
            keep(h, a).start()
            outs.append(nn(p, v2))
        heads[:, pl.ds(al(h * 128, 128), 128)] = jnp.where(halves[0], outs[0], outs[1]).astype(BF)
        for k in range(pairs):

            @pl.when(h == k)
            def _():
                run(tasks[k])

        return 0

    lax.fori_loop(0, pairs, attend, 0)
    pieces[3].done()

    def load(h, a):
        return pltpu.make_async_copy(spill.at[h * 2 + a], pslot.at[a], pd.at[a])

    for a in range(2):
        keep(pairs - 1, a).wait()
        load(0, a).start()

    def normalize(v):
        centred = v - jnp.mean(v, axis=-1, keepdims=True)
        scale = lax.rsqrt(jnp.mean(centred * centred, axis=-1, keepdims=True) + 1e-5)
        return centred * scale, scale

    def first_rows(i, _):
        r = pl.ds(al(i * 256, 256), 256)
        v = n1[r, :] + (nn(heads[r, :], wide[:, OUT:EXP]) + fullv[2:3, :])
        n, s = normalize(v)
        n1[r, :] = n
        sc1[r, 1:2] = s
        fl[r, :] = (n * fullv[3:4, :] + fullv[4:5, :]).astype(BF)
        return 0

    lax.fori_loop(0, T // 256, first_rows, 0)
    run(['s4:7', 's4:6'])
    after = [
        [],
        ['s3:10', 's4:8'],
        ['s4:9'],
        ['s4:10'],
    ]

    def expand(i, _):
        for k in range(4):

            @pl.when(i == k)
            def _():
                pieces[4 + k].done()

        cs = pl.ds(al(i * 768, 768), 768)
        u = nn(fl[...], wide[:, pl.ds(al(EXP + i * 768, 768), 768)]) + fulle[:, cs]
        cdf = 0.5 * (1.0 + lax.erf(u * math.sqrt(0.5)))
        hidden[:, cs] = (u * cdf).astype(BF)
        slope[:, cs] = (cdf + u * jnp.exp(-0.5 * u * u) * (1.0 / math.sqrt(2.0 * math.pi))).astype(BF)
        for k in range(4):

            @pl.when(i == k)
            def _():
                run(after[k])

        return 0

    lax.fori_loop(0, FF // 768, expand, 0)

    pieces[8].done()
    sg[:, :256] = nn(hidden[...], wcon[:, :256]) + fullv[5:6, :256]
    run([])
    pieces[9].done()
    run([])
    pieces[10].done()
    run([])
    own_cot.wait()
    swap_cot.wait_recv()

    gv[...] = jnp.zeros_like(gv)

    def second_rows(i, _):
        r = pl.ds(al(i * 256, 256), 256)
        v = jnp.concatenate([sg[r, :256], nn(hidden[r, :], wcon[:, 256:]) + fullv[5:6, 256:]], axis=1)
        v = v + (n1[r, :] * fullv[3:4, :] + fullv[4:5, :])
        n, s = normalize(v)
        lonew[r, :] = (n * fullv[6:7, :] + fullv[7:8, :]).astype(BF)
        og = jnp.where(sc1[r, 0:1] > 0.5, cotn[r, :].astype(F32), cotr[r, :].astype(F32))
        gv[6:7, :] += jnp.sum(og * n, axis=0, keepdims=True)
        gv[7:8, :] += jnp.sum(og, axis=0, keepdims=True)
        w = og * fullv[6:7, :]
        g = s * (w - jnp.mean(w, axis=-1, keepdims=True) - n * jnp.mean(w * n, axis=-1, keepdims=True))
        sg[r, :] = g
        low = g.astype(BF)
        bg[r, :] = low
        gv[5:6, :] += jnp.sum(low.astype(F32), axis=0, keepdims=True)
        return 0

    lax.fori_loop(0, T // 256, second_rows, 0)
    swap_lo = send(lonew, lor, swap_sem.at[2, 0], swap_sem.at[2, 1], me, other)
    swap_lo.start()

    S = 384
    my_k = (1 - c) * x + c * y
    far_base = (1 - c) * (2 - 2 * y) + c * (1 - x)
    own_base = (1 - c) * 2 * y + c * x
    step_k = 1 + c

    def total(*refs):
        t = refs[0][...].astype(F32)
        for ref in refs[1:]:
            t = t + ref[...].astype(F32)
        return t

    class Red:
        def __init__(self, n, g, col, rows, recv, rcol, fsum, plane=None, width=384, parts=(), whole=None):
            self.n, self.g, self.col, self.rows, self.recv, self.rcol, self.fsum = n, g, col, rows, recv, rcol, fsum
            self.plane, self.width, self.parts, self.whole = plane, width, parts, whole
            self.paired = False

        def cols(self, core):
            return pl.ds(al(self.col + core * S, 128), self.width)

        def part(self, base, i, k=1, second=False):
            if self.plane is None:
                cs = pl.ds(self.rcol + (self.width if second else 0), self.width)
            else:
                cs = pl.ds(0, S)
                base = base + self.rcol
            return self.recv.at[pl.ds(al(base + i * self.rows, 16), k * self.rows), cs]

        def mine(self, o):
            base = 0 if self.plane is None else self.plane * 4
            return self.g.at[pl.ds(al((base + o) * self.rows, 16), self.rows), self.cols(c)]

        def planes(self):
            return 4 if self.plane is None else 1

        def rp(self, o, k=1):
            return self.part(0, o, k)

        def ra(self, i, k=1):
            return self.part(0 if self.plane is None else 768, i, k, True)

        def rb(self, i, k=1):
            return self.part(384 if self.plane is None else 1152, i, k, True)

        def rz(self, i, k=1):
            if self.plane is None:
                return self.part(576, i, k, True)
            return self.recv.at[pl.ds(al(5376 + i * self.rows, 16), k * self.rows), pl.ds(0, S)]

        def sem(self, stage):
            if stage > 4:
                return rs.at[self.n], rr.at[74 + self.whole * 3 + stage - 5]
            n = 0 if self.plane is not None and stage == 3 else self.n
            return rs.at[self.n], rr.at[n * 5 + stage]

        def got(self, stage, ref):
            s, r = self.sem(stage)
            send(ref, ref, s, r, me, other).wait_recv()

        def P(self):
            base = 0 if self.plane is None else self.plane * 4 * self.rows
            n = 4 * self.planes() * self.rows
            src = self.g.at[pl.ds(al(base, 16), n), self.cols(other)]
            s, r = self.sem(0)
            send(src, self.rp(0, 4 * self.planes()), s, r, me, other).start()

        def pair(self):
            if not self.paired:
                self.paired = True
                self.got(0, self.rp(0, 4 * self.planes()))

        def early(self, o, k=1):
            return [] if self.whole is None else [ry.at[pl.ds(al(self.whole * 192 + o * 48, 16), k * 48)]]

        def Y(self):
            self.pair()
            s, r = self.sem(5)
            p = lax.rem(z + 1, 4) * 4
            b = self.g.at[pl.ds(al(p * 48, 16), 192), self.cols(c)]
            b[...] = total(b, self.rp(p, 4)).astype(BF)
            send(b, self.early(0, 4)[0], s, r, zs[0], c).start()

        def A(self):
            self.pair()
            s, r = self.sem(1)

            def one(i, _):
                p = i // 2 if self.whole is None else lax.rem(z + 2 + i // 2, 4)
                o = p * 4 + far_base + lax.rem(i, 2) * step_k
                b = self.mine(o)
                b[...] = total(b, self.rp(o)).astype(BF)
                send(b, self.ra(p * 2 + lax.rem(i, 2)), s, r, far, c).start()
                return 0

            lax.fori_loop(0, 4 if self.whole is not None else 2 * self.planes(), one, 0)

        def A0(self):
            self.got(5, self.early(0, 4)[0])
            s, r = self.sem(6)
            for k in range(2):
                o = far_base + k * step_k
                b = self.mine(z * 4 + o)
                b[...] = total(b, self.rp(z * 4 + o), *self.early(o)).astype(BF)
                send(b, self.ra(z * 2 + k), s, r, far, c).start()

        def B(self):
            n = 2 if self.whole is not None else self.planes()
            self.got(1, self.ra(0, 2 * n))
            s, r = self.sem(2)

            def one(i, _):
                p = i if self.whole is None else lax.rem(z + 2 + i, 4)
                o = p * 4 + near_xy
                b = self.mine(o)
                b[...] = total(b, self.rp(o), self.ra(p * 2 + 1 - my_k)).astype(BF)
                send(b, self.rb(p), s, r, near, c).start()
                return 0

            lax.fori_loop(0, n, one, 0)

        def B0(self):
            self.got(6, self.ra(0, 2))
            s, r = self.sem(7)
            b = self.mine(z * 4 + near_xy)
            t = total(b, self.rp(z * 4 + near_xy), self.ra(z * 2 + 1 - my_k), *self.early(near_xy))
            b[...] = t.astype(BF)
            send(b, self.rb(z), s, r, near, c).start()

        def Z(self):
            self.got(2, self.rb(0, self.planes() if self.whole is None else 2))
            s, r = self.sem(3)
            if self.plane is None:
                for k in range(0 if self.whole is None else 1, 3):
                    p = lax.rem(z + k + 1, 4)
                    b = self.mine(p * 4 + xy)
                    b[...] = total(b, self.rp(p * 4 + xy), self.ra(p * 2 + my_k), self.rb(p)).astype(BF)
                    send(b, self.rz(k), s, r, zs[k], c).start()
            elif self.n > 0:
                b = self.mine(xy)
                b[...] = total(b, self.rp(xy), self.ra(my_k), self.rb(0)).astype(BF)
                send(b, self.rz(self.n - 1), s, r, zs[self.n - 1], c).start()

        def F(self):
            first = 0 if self.whole is None else 1
            self.got(3, self.rz(0, 3 - first))
            if first:
                self.got(7, self.rb(0))
            o, p = (z * 4 + xy, z) if self.plane is None else (xy, 0)
            last = [self.rz(k) for k in range(first, 3)] + self.early(xy)
            t = total(self.mine(o), self.rp(o), self.ra(p * 2 + my_k), self.rb(p), *last)
            s, r = self.sem(4)
            if self.parts:
                for i, k in enumerate(self.parts):
                    b = self.fsum.at[:, pl.ds(al(k + c * 128, 128), 128)]
                    b[...] = t[:, i * 128 : (i + 1) * 128]
                    send(b, b, s, r, me, other).start()
            else:
                b = self.fsum.at[:, pl.ds(al((self.n - 4 if 4 <= self.n < 8 else 0) * 768 + c * S, 128), S)]
                b[...] = t
                send(b, b, s, r, me, other).start()

        def end(self):
            if self.plane is None:
                m = wide.at[pl.ds(0, 528), pl.ds(0, 3 * self.width)]
            else:
                m = wide.at[pl.ds(0, 576 if self.n == 0 else 512), pl.ds(0, 1152)]
            send(m, m, rs.at[self.n], rr.at[self.n], me, other).wait_send()
            if self.plane is None or self.n == 0:
                self.got(4, self.fsum.at[:, pl.ds(0, self.width)])

    early = {0: 0, 1: 1}
    con = {j: Red(j, gcon, 0, 192, con_r, j * 1344, fcon, plane=lax.rem(z + j, 4)) for j in range(4)}
    exp = [Red(4 + k, wide, EXP + k * 768, 48, hidden, k * 768, fexp, whole=early.get(k)) for k in range(4)]
    out = Red(8, wide, OUT, 48, cotn, 0, fout)
    ins = [
        Red(9 + k, gin, k * 768, 48, slope, k * 768, fin, parts=[q * D + k * 256 for q in range(3)]) for k in range(2)
    ]
    for k, first in enumerate((512, 2 * D + 512, D + 512)):
        ins.append(Red(11 + k, gin, 1536 + (0, 256, 128)[k], 48, slope, 1536 + 256 * k, fin, width=128, parts=[first]))
    sums = {f"C{k}": con[k] for k in range(4)}
    sums.update({f"E{k}": exp[k] for k in range(4)})
    sums.update({f"I{k}": ins[k] for k in range(5)})
    sums["O"] = out

    def reduce(ops):
        for op in ops:
            name, _, rest = op.partition(":")
            if op in loose:
                loose[op]()
            else:
                getattr(sums[rest], name)()

    def steps(i, lists):
        for k, ops in enumerate(lists):
            if ops:

                @pl.when(i == k)
                def _():
                    reduce(ops)

    def send_back():
        def out_rows(i, _):
            r = pl.ds(al(i * 128, 128), 128)
            lonew[r, :] = jnp.where(sc1[r, 0:1] > 0.5, lonew[r, :].astype(F32), lor[r, :].astype(F32)).astype(BF)
            return 0

        swap_lo.wait()
        lax.fori_loop(0, T // 128, out_rows, 0)
        lo_done.start()

    lo_done = pltpu.make_async_copy(lonew, lo_o, ls.at[14])
    loose["lo"] = send_back

    def vsend(stage, src, dst, dp, seq):
        return send(src, dst, rs.at[14 + stage], rr.at[70 + stage], dp, seq)

    def v_partner():
        vout[...] = jnp.zeros_like(vout)
        for o in range(16):
            vout[o, :, 0:48] = gv[0:8, o * 48 : (o + 1) * 48]
            for k in range(4):
                vout[o, k : k + 1, 64:112] = ge[:, o * 192 + k * 48 : o * 192 + (k + 1) * 48]
        vsend(0, vout, vr.at[pl.ds(0, 16)], me, other).start()

    def v_flip_y():
        vsend(0, vout, vr.at[pl.ds(0, 16)], me, other).wait_recv()
        vsum[...] = vout[...] + vr[pl.ds(0, 16)]
        for i in range(8):
            vsend(1, vsum.at[(i // 2) * 4 + 2 - 2 * y + i % 2], vr.at[16 + i], flip_y, c).start()

    def v_flip_x():
        vsend(1, vr.at[pl.ds(16, 8)], vr.at[pl.ds(16, 8)], me, other).wait_recv()
        for i in range(8):
            o = (i // 2) * 4 + 2 * y + i % 2
            vsum[o] = vsum[o] + vr[16 + i]
        for i in range(4):
            vsend(2, vsum.at[i * 4 + 2 * y + 1 - x], vr.at[24 + i], flip_x, c).start()

    def v_planes():
        vsend(2, vr.at[pl.ds(24, 4)], vr.at[pl.ds(24, 4)], me, other).wait_recv()
        for i in range(4):
            vsum[i * 4 + xy] = vsum[i * 4 + xy] + vr[24 + i]
        for k in range(3):
            vsend(3, vsum.at[lax.rem(z + k + 1, 4) * 4 + xy], vr.at[28 + k], zs[k], c).start()

    def v_total():
        vsend(3, vr.at[pl.ds(28, 3)], vr.at[pl.ds(28, 3)], me, other).wait_recv()
        vr[31] = vsum[z * 4 + xy] + vr[28] + vr[29] + vr[30]
        v_done.start()

    v_done = pltpu.make_async_copy(vr.at[31], gvec_o, ls.at[16])
    loose.update({"vP": v_partner, "vA": v_flip_y, "vB": v_flip_x, "vZ": v_planes, "vF": v_total})

    ig_mine, ig_theirs = bg, fl
    swap_ig = [
        send(ig_mine.at[pl.ds(256 * k, 256)], ig_theirs.at[pl.ds(256 * k, 256)], sw3.at[0, k], sw3.at[1, k], me, other)
        for k in range(3)
    ]
    for k in range(3):
        loose[f"swg{k}"] = swap_ig[k].start
    ig_done = pltpu.make_async_copy(sg, ig_o, ls.at[15])

    def take_rows():
        for d in swap_ig:
            d.wait_recv()

        def grad_rows(i, _):
            r = pl.ds(al(i * 128, 128), 128)
            sg[r, :] = jnp.where(sc1[r, 0:1] > 0.5, sg[r, :], ig_theirs[r, :].astype(F32))
            return 0

        lax.fori_loop(0, T // 128, grad_rows, 0)
        ig_done.start()

    loose["sel"] = take_rows

    def grad_con(i, _):
        p = al(lax.rem(z + i + 1, 4) * 768, 768)
        gcon[pl.ds(p, 768), :] = tn(hidden[:, pl.ds(p, 768)], bg[...]).astype(BF)
        steps(i, [['P:C1'], ['P:C2'], [], ['A:C1', 'P:C3']])
        return 0

    lax.fori_loop(0, 4, grad_con, 0)

    def expand_back(i, _):
        cs = pl.ds(al(i * 768, 768), 768)
        g = (nt(bg[...], wcon[cs, :]) * slope[:, cs].astype(F32)).astype(BF)
        slope[:, cs] = g
        ge[:, cs] = jnp.sum(g.astype(F32), axis=0, keepdims=True)
        steps(i, [[], ['A:C2'], [], ['A:C3', 'P:C0']])
        return 0

    lax.fori_loop(0, FF // 768, expand_back, 0)

    def first_back(i, _):
        r = pl.ds(al(i * 256, 256), 256)
        g = sg[r, :] + nt(slope[r, :], wide[:, EXP:])
        n = n1[r, :]
        gv[3:4, :] += jnp.sum(g * n, axis=0, keepdims=True)
        gv[4:5, :] += jnp.sum(g, axis=0, keepdims=True)
        w = g * fullv[3:4, :]
        g = sc1[r, 1:2] * (w - jnp.mean(w, axis=-1, keepdims=True) - n * jnp.mean(w * n, axis=-1, keepdims=True))
        sg[r, :] = g
        low = g.astype(BF)
        bg[r, :] = low
        gv[2:3, :] += jnp.sum(low.astype(F32), axis=0, keepdims=True)
        steps(i, [['B:C1'], [], ['A:C0']])
        return 0

    lax.fori_loop(0, T // 256, first_back, 0)
    for p in pieces[4:8]:
        p.drain()

    def grad_exp(i, _):
        cs = pl.ds(al(i * 768, 768), 768)
        wide[:, pl.ds(al(EXP + i * 768, 768), 768)] = tn(fl[...], slope[:, cs]).astype(BF)
        steps(i, [[], ['B:C2', 'P:E0'], ['P:E1', 'Z:C1', 'B:C3'], []])
        return 0

    lax.fori_loop(0, 4, grad_exp, 0)
    hg = cotr
    hg[...] = nt(bg[...], wide[:, OUT:EXP]).astype(BF)
    reduce(['A:E0', 'Y:E0'])
    pieces[3].drain()
    wide[:, OUT:EXP] = tn(heads[...], bg[...]).astype(BF)
    reduce(['P:O', 'Y:E1', 'B:C0', 'A:E1', 'P:E2'])

    tasks = [['Z:C3', 'A:O'], [], ['B:E0', 'Z:C2', 'Z:C0', 'B:O'], ['A:I0'], ['A:E3'], []]
    after = [['A:E2', 'P:E3', 'P:I0'], ['B:E1'], ['P:I2', 'F:C0', 'Z:O', 'B:I0', 'P:I3', 'Z:E1', 'P:I4', 'P:I1']]

    def attend_back(h, _):
        cs = al(h * 384, 128)
        hs = pl.ds(al(h * 128, 128), 128)
        q2 = proj[:, pl.ds(cs, 128)]
        k2 = proj[:, pl.ds(cs + 128, 128)]
        v2 = proj[:, pl.ds(cs + 256, 128)]
        g2 = hg[:, hs]
        prod = g2.astype(F32) * heads[:, hs].astype(F32)
        qt = q2.astype(F32).T.astype(BF)
        gt = g2.astype(F32).T.astype(BF)
        dq, dk, dv = [], [], []
        for a in range(2):
            load(h, a).wait()
            rowdot = jnp.sum(jnp.where(halves[a], prod, 0.0), axis=-1, keepdims=True)
            p = pslot[a]
            dp = nt(jnp.where(halves[a], g2, jnp.zeros_like(g2)), v2)
            ds = (p.astype(F32) * (dp - rowdot)).astype(BF)
            dq.append(nn(ds, k2))
            dk.append(nn(qt[a * HD : (a + 1) * HD], ds))
            dv.append(nn(gt[a * HD : (a + 1) * HD], p))

            @pl.when(h + 1 < pairs)
            def _():
                load(h + 1, a).start()

        dq = (jnp.where(halves[0], dq[0], dq[1]) * HD**-0.5).astype(BF)
        dk = jnp.concatenate(dk, axis=0).T.astype(BF)
        dv = jnp.concatenate(dv, axis=0).T.astype(BF)
        proj[:, pl.ds(cs, 128)] = dq
        proj[:, pl.ds(cs + 128, 128)] = dk
        proj[:, pl.ds(cs + 256, 128)] = dv
        gv[0:1, hs] = jnp.sum(dq.astype(F32), axis=0, keepdims=True)
        gv[1:2, hs] = jnp.sum(dv.astype(F32), axis=0, keepdims=True)

        steps(h, tasks)

        @pl.when(lax.rem(h, 2) == 1)
        def _():
            cols = pl.ds(al((h // 2) * 768, 768), 768)
            gin[:, cols] = tn(xl[...], proj[:, cols]).astype(BF)

        steps((h - 1) // 2 + 8 * (1 - lax.rem(h, 2)), after)
        return 0

    lax.fori_loop(0, pairs, attend_back, 0)

    totals = [(fcon, gcon_o), (fexp, gexp_o), (fout, gout_o), (fin, gin_o)]
    sum_out = [pltpu.make_async_copy(v, o, ls.at[17 + k]) for k, (v, o) in enumerate(totals)]

    def first_totals():
        for k, group in ((0, [con[0]]), (1, exp)):
            for p in group:
                p.end()
            sum_out[k].start()

    loose["totals"] = first_totals

    def input_rows(i, _):
        r = pl.ds(al(i * 256, 256), 256)
        g = sg[r, :] + nt(proj[r, :], wide[:, IN:OUT])
        sg[r, :] = g
        ig_mine[r, :] = g.astype(BF)
        steps(i, [['vP', 'A:I2', 'Z:E0', 'A:I3', 'B:E3'], ['B:E2', 'A:I4', 'A:I1'], ['A0:E1', 'Z:I0', 'Z:E3', 'Z:E2', 'swg2', 'B:I2', 'B:I3', 'B:I4', 'B:I1', 'lo', 'swg0', 'swg1', 'F:I0', 'Z:I2', 'Z:I3', 'Z:I4', 'vA', 'Z:I1', 'sel', 'F:O', 'A0:E0', 'vB', 'B0:E1', 'B0:E0', 'F:E1', 'F:E2', 'vZ', 'F:I3', 'F:E0', 'F:I4', 'F:E3', 'F:I2', 'totals', 'F:I1', 'vF']])
        return 0

    lax.fori_loop(0, T // 256, input_rows, 0)
    outs = [lo_done, ig_done, v_done] + sum_out
    for k, group in ((2, [out]), (3, ins)):
        for p in group:
            p.end()
        sum_out[k].start()
    for k in (1, 2, 3):
        con[k].end()
    swap_tok.wait_send()
    swap_cot.wait_send()
    for d in swap_ig:
        d.wait_send()
    for p in pieces[0:3] + pieces[8:]:
        p.drain()
    for stage, k in ((0, 3), (1, 4), (2, 8)):
        small(stage, k, False)
        m = vr.at[pl.ds(0, (8, 4, 3)[stage])]
        vsend(stage + 1, m, m, me, other).wait_send()
    vsend(0, vout, vr.at[pl.ds(0, 16)], me, other).wait_send()
    for o in outs:
        o.wait()


def fused_layer(tokens, time_embed, segments, iw, ow, ew, cw, vectors, cot):
    T, D = tokens.shape
    FF = ew.shape[1]
    sh = jax.ShapeDtypeStruct
    anyspec = pl.BlockSpec(memory_space=pl.ANY)
    vspec = pl.BlockSpec(memory_space=VM)
    scratch = [
        VM((D, 4 * D + FF), BF), VM((FF, D), BF),
        VM((T, D), BF), VM((T, D), BF), VM((T, D), BF), VM((T, D), BF),
        VM((16, 16, 128), BF), VM((16, 128), F32), VM((16, D), F32), VM((1, FF), F32), VM((2, 3 * D), F32),
        VM((T, 3 * D), BF), VM((T, D), BF), VM((T, D), F32), VM((T, T), F32),
        VM((T, 2), F32), VM((T, D), BF), VM((T, D), BF), VM((T, FF), BF), VM((T, FF), BF),
        VM((2, T, T), BF), VM((T, D), BF),
        VM((D, 3 * D), BF), VM((FF, D), BF), VM((5952, 384), BF), VM((768, 384), BF), VM((8, D), F32), VM((1, FF), F32),
        VM((16, 8, 128), F32), VM((16, 8, 128), F32), VM((32, 8, 128), F32),
        VM(iw.shape, F32), VM(ow.shape, F32), VM(ew.shape, F32), VM(cw.shape, F32),
        DMA((3, 2)), DMA((2, 3)), DMA((21,)), DMA((11,)), DMA((65,)), DMA((6,)), DMA((2,)), DMA((18,)), DMA((80,)), DMA((2,)),
    ]
    return pl.pallas_call(
        fused_kernel,
        out_shape=(
            sh((T, D), BF), sh((T, D), F32), sh(iw.shape, F32), sh(ow.shape, F32), sh(ew.shape, F32),
            sh(cw.shape, F32), sh((8, 128), F32), sh((D // HD, T, T), BF),
        ),
        in_specs=[anyspec, anyspec, vspec, vspec, anyspec, anyspec, anyspec, anyspec] + [vspec] * 9,
        out_specs=(anyspec,) * 8,
        scratch_shapes=scratch,
        compiler_params=pltpu.CompilerParams(
            collective_id=0, has_side_effects=True, vmem_limit_bytes=67043328
        ),
    )(tokens, cot, time_embed, segments, iw, ow, ew, cw, *vectors)


epsilon = 1e-05
masked_score = -1e30


def matmul(left, right):
    return jnp.dot(left, right, preferred_element_type=jnp.float32)


def product_tn(left, right):
    return lax.dot_general(
        left, right, (((0,), (0,)), ((), ())), preferred_element_type=jnp.float32
    )


def product_nt(left, right):
    return lax.dot_general(
        left, right, (((1,), (1,)), ((), ())), preferred_element_type=jnp.float32
    )


def normalize(values):
    mean = jnp.mean(values, axis=-1, keepdims=True)
    centred = values - mean
    scale = lax.rsqrt(jnp.mean(centred * centred, axis=-1, keepdims=True) + epsilon)
    return (centred * scale, scale)


def norm_back(grad, normed, scale, gain):
    scaled = grad * gain
    return scale * (
        scaled
        - jnp.mean(scaled, axis=-1, keepdims=True)
        - normed * jnp.mean(scaled * normed, axis=-1, keepdims=True)
    )


def gelu_value(values):
    return 0.5 * values * (1.0 + lax.erf(values * math.sqrt(0.5)))


def gelu_slope(values):
    return 0.5 * (1.0 + lax.erf(values * math.sqrt(0.5))) + values * jnp.exp(
        -0.5 * values * values
    ) / math.sqrt(2.0 * math.pi)


def attend_forward(item):
    query, key, value, segment_row = item
    length, depth = query.shape
    block = min(512, length)
    blocks = length // block
    scale = depth ** (-0.5)

    def one_block(part):
        query_block, segment_block = part
        scores = product_nt(query_block, key) * scale
        scores = jnp.where(segment_block[:, None] == segment_row[None, :], scores, masked_score)
        top = jnp.max(scores, axis=-1, keepdims=True)
        expo = jnp.exp(scores - top)
        total = jnp.sum(expo, axis=-1, keepdims=True)
        probs_low = (expo / total).astype(jnp.bfloat16)
        return (matmul(probs_low, value).astype(jnp.bfloat16), (top + jnp.log(total))[:, 0])

    outputs, logsum = lax.map(
        one_block, (query.reshape(blocks, block, depth), segment_row.reshape(blocks, block))
    )
    return (outputs.reshape(length, depth), logsum.reshape(length))


def attend_backward(item):
    query, key, value, segment_row, logsum, out_grad = item
    length, depth = query.shape
    block = min(512, length)
    blocks = length // block
    scale = depth ** (-0.5)

    def one_block(carry, part):
        key_grad, value_grad = carry
        query_block, segment_block, logsum_block, grad_block = part
        scores = product_nt(query_block, key) * scale
        scores = jnp.where(segment_block[:, None] == segment_row[None, :], scores, masked_score)
        probs = jnp.exp(scores - logsum_block[:, None])
        probs_low = probs.astype(jnp.bfloat16)
        prob_grad = product_nt(grad_block, value)
        row_total = jnp.sum(probs * prob_grad, axis=-1, keepdims=True)
        score_grad = (probs * (prob_grad - row_total)).astype(jnp.bfloat16)
        query_grad = matmul(score_grad, key) * scale
        key_grad = key_grad + product_tn(score_grad, query_block) * scale
        value_grad = value_grad + product_tn(probs_low, grad_block)
        return ((key_grad, value_grad), query_grad.astype(jnp.bfloat16))

    zeros = jnp.zeros((length, depth), jnp.float32)
    parts = (
        query.reshape(blocks, block, depth),
        segment_row.reshape(blocks, block),
        logsum.reshape(blocks, block),
        out_grad.reshape(blocks, block, depth),
    )
    (key_grad, value_grad), query_grad = lax.scan(one_block, (zeros, zeros), parts)
    return (
        query_grad.reshape(length, depth),
        key_grad.astype(jnp.bfloat16),
        value_grad.astype(jnp.bfloat16),
    )


def plain_body(
    tokens,
    time_embed,
    segments,
    input_weight,
    query_bias,
    value_bias,
    output_weight,
    output_bias,
    first_gain,
    first_shift,
    expand_weight,
    expand_bias,
    contract_weight,
    contract_bias,
    second_gain,
    second_shift,
    cotangent,
):
    pairs = lax.axis_size("seq")
    seqs, half, width = tokens.shape
    length = half * pairs
    rows = seqs * half
    group = width // pairs
    heads_here = group // HD
    start = (tokens.astype(jnp.float32) + time_embed[:, None, :]).reshape(rows, width)
    start_low = start.astype(jnp.bfloat16)
    attention_set = (
        lax.all_gather(input_weight, "dp", axis=0, tiled=True),
        lax.all_gather(output_weight, "dp", axis=0, tiled=True),
        lax.all_gather(query_bias, "dp", axis=0, tiled=True),
        lax.all_gather(value_bias, "dp", axis=0, tiled=True),
        lax.all_gather(output_bias, "dp", axis=0, tiled=True),
        lax.all_gather(first_gain, "dp", axis=0, tiled=True),
        lax.all_gather(first_shift, "dp", axis=0, tiled=True),
    )
    (
        full_input,
        full_output,
        full_query_bias,
        full_value_bias,
        full_output_bias,
        full_first_gain,
        full_first_shift,
    ) = attention_set
    bias_row = jnp.concatenate(
        [
            full_query_bias.astype(jnp.float32),
            jnp.zeros((width,), jnp.float32),
            full_value_bias.astype(jnp.float32),
        ]
    )
    projected_low = (matmul(start_low, full_input) + bias_row).astype(jnp.bfloat16)
    regrouped = lax.all_to_all(
        projected_low.reshape(seqs, half, 3, pairs, group),
        "seq",
        split_axis=3,
        concat_axis=1,
        tiled=True,
    )
    split = regrouped.reshape(seqs, length, 3, heads_here, HD).transpose(2, 0, 3, 1, 4)
    split = split.reshape(3, seqs * heads_here, length, HD)
    query_heads, key_heads, value_heads = (split[0], split[1], split[2])
    segment_heads = jnp.repeat(segments, heads_here, axis=0)
    heads_out, logsum = lax.map(
        attend_forward, (query_heads, key_heads, value_heads, segment_heads)
    )
    heads_tokens = (
        heads_out.reshape(seqs, heads_here, length, HD)
        .transpose(0, 2, 1, 3)
        .reshape(seqs, length, 1, group)
    )
    heads_low = lax.all_to_all(
        heads_tokens, "seq", split_axis=1, concat_axis=2, tiled=True
    ).reshape(rows, width)
    attention = matmul(heads_low, full_output) + full_output_bias.astype(jnp.float32)
    normed_one, scale_one = normalize(start + attention)
    gain_one = full_first_gain.astype(jnp.float32)
    first = normed_one * gain_one + full_first_shift.astype(jnp.float32)
    first_low = first.astype(jnp.bfloat16)
    network_set = (
        lax.all_gather(expand_weight, "dp", axis=0, tiled=True),
        lax.all_gather(contract_weight, "dp", axis=0, tiled=True),
        lax.all_gather(expand_bias, "dp", axis=0, tiled=True),
        lax.all_gather(contract_bias, "dp", axis=0, tiled=True),
        lax.all_gather(second_gain, "dp", axis=0, tiled=True),
        lax.all_gather(second_shift, "dp", axis=0, tiled=True),
    )
    (
        full_expand,
        full_contract,
        full_expand_bias,
        full_contract_bias,
        full_second_gain,
        full_second_shift,
    ) = network_set
    expand = matmul(first_low, full_expand) + full_expand_bias.astype(jnp.float32)
    hidden = gelu_value(expand).astype(jnp.bfloat16)
    second_sum = first + matmul(hidden, full_contract) + full_contract_bias.astype(jnp.float32)
    normed_two, scale_two = normalize(second_sum)
    gain_two = full_second_gain.astype(jnp.float32)
    layer_output = (normed_two * gain_two + full_second_shift.astype(jnp.float32)).astype(
        jnp.bfloat16
    )
    network_set = (
        lax.all_gather(expand_weight, "dp", axis=0, tiled=True),
        lax.all_gather(contract_weight, "dp", axis=0, tiled=True),
        lax.all_gather(expand_bias, "dp", axis=0, tiled=True),
        lax.all_gather(contract_bias, "dp", axis=0, tiled=True),
        lax.all_gather(second_gain, "dp", axis=0, tiled=True),
        lax.all_gather(second_shift, "dp", axis=0, tiled=True),
    )
    full_expand, full_contract = (network_set[0], network_set[1])
    out_grad = cotangent.astype(jnp.float32).reshape(rows, width)
    grad_second_gain = jnp.sum(out_grad * normed_two, axis=0)
    grad_second_shift = jnp.sum(out_grad, axis=0)
    second_grad = norm_back(out_grad, normed_two, scale_two, gain_two)
    branch_grad = second_grad.astype(jnp.bfloat16)
    grad_contract_bias = jnp.sum(branch_grad.astype(jnp.float32), axis=0)
    grad_contract_weight = product_tn(hidden, branch_grad)
    expand_grad = (product_nt(branch_grad, full_contract) * gelu_slope(expand)).astype(jnp.bfloat16)
    grad_expand_bias = jnp.sum(expand_grad.astype(jnp.float32), axis=0)
    grad_expand_weight = product_tn(first_low, expand_grad)
    first_grad = second_grad + product_nt(expand_grad, full_expand)
    grad_first_gain = jnp.sum(first_grad * normed_one, axis=0)
    grad_first_shift = jnp.sum(first_grad, axis=0)
    start_grad = norm_back(first_grad, normed_one, scale_one, gain_one)
    attention_set = (
        lax.all_gather(input_weight, "dp", axis=0, tiled=True),
        lax.all_gather(output_weight, "dp", axis=0, tiled=True),
        lax.all_gather(query_bias, "dp", axis=0, tiled=True),
        lax.all_gather(value_bias, "dp", axis=0, tiled=True),
        lax.all_gather(output_bias, "dp", axis=0, tiled=True),
        lax.all_gather(first_gain, "dp", axis=0, tiled=True),
        lax.all_gather(first_shift, "dp", axis=0, tiled=True),
    )
    full_input, full_output = (attention_set[0], attention_set[1])
    attention_grad = start_grad.astype(jnp.bfloat16)
    grad_output_bias = jnp.sum(attention_grad.astype(jnp.float32), axis=0)
    grad_output_weight = product_tn(heads_low, attention_grad)
    heads_grad = product_nt(attention_grad, full_output).astype(jnp.bfloat16)
    grad_heads = lax.all_to_all(
        heads_grad.reshape(seqs, half, pairs, group), "seq", split_axis=2, concat_axis=1, tiled=True
    )
    grad_heads = (
        grad_heads.reshape(seqs, length, heads_here, HD)
        .transpose(0, 2, 1, 3)
        .reshape(seqs * heads_here, length, HD)
    )
    query_grad, key_grad, value_grad = lax.map(
        attend_backward, (query_heads, key_heads, value_heads, segment_heads, logsum, grad_heads)
    )
    stacked = jnp.stack([query_grad, key_grad, value_grad]).reshape(3, seqs, heads_here, length, HD)
    stacked = stacked.transpose(1, 3, 0, 2, 4).reshape(seqs, length, 3, 1, group)
    projected_grad = lax.all_to_all(
        stacked, "seq", split_axis=1, concat_axis=3, tiled=True
    ).reshape(rows, 3 * width)
    grad_query_bias = jnp.sum(projected_grad[:, :width].astype(jnp.float32), axis=0)
    grad_value_bias = jnp.sum(projected_grad[:, 2 * width :].astype(jnp.float32), axis=0)
    grad_input_weight = product_tn(start_low, projected_grad)
    input_grad = (start_grad + product_nt(projected_grad, full_input)).reshape(seqs, half, width)
    grads = (
        grad_input_weight,
        grad_query_bias,
        grad_value_bias,
        grad_output_weight,
        grad_output_bias,
        grad_first_gain,
        grad_first_shift,
        grad_expand_weight,
        grad_expand_bias,
        grad_contract_weight,
        grad_contract_bias,
        grad_second_gain,
        grad_second_shift,
    )
    owned = (
        lax.psum_scatter(grads[0], "dp", scatter_dimension=0, tiled=True),
        lax.psum_scatter(grads[1], "dp", scatter_dimension=0, tiled=True),
        lax.psum_scatter(grads[2], "dp", scatter_dimension=0, tiled=True),
        lax.psum_scatter(grads[3], "dp", scatter_dimension=0, tiled=True),
        lax.psum_scatter(grads[4], "dp", scatter_dimension=0, tiled=True),
        lax.psum_scatter(grads[5], "dp", scatter_dimension=0, tiled=True),
        lax.psum_scatter(grads[6], "dp", scatter_dimension=0, tiled=True),
        lax.psum_scatter(grads[7], "dp", scatter_dimension=0, tiled=True),
        lax.psum_scatter(grads[8], "dp", scatter_dimension=0, tiled=True),
        lax.psum_scatter(grads[9], "dp", scatter_dimension=0, tiled=True),
        lax.psum_scatter(grads[10], "dp", scatter_dimension=0, tiled=True),
        lax.psum_scatter(grads[11], "dp", scatter_dimension=0, tiled=True),
        lax.psum_scatter(grads[12], "dp", scatter_dimension=0, tiled=True),
    )
    summed = (
        lax.psum(owned[0].astype(jnp.bfloat16), "seq").astype(jnp.float32),
        lax.psum(owned[1].astype(jnp.bfloat16), "seq").astype(jnp.float32),
        lax.psum(owned[2].astype(jnp.bfloat16), "seq").astype(jnp.float32),
        lax.psum(owned[3].astype(jnp.bfloat16), "seq").astype(jnp.float32),
        lax.psum(owned[4].astype(jnp.bfloat16), "seq").astype(jnp.float32),
        lax.psum(owned[5].astype(jnp.bfloat16), "seq").astype(jnp.float32),
        lax.psum(owned[6].astype(jnp.bfloat16), "seq").astype(jnp.float32),
        lax.psum(owned[7].astype(jnp.bfloat16), "seq").astype(jnp.float32),
        lax.psum(owned[8].astype(jnp.bfloat16), "seq").astype(jnp.float32),
        lax.psum(owned[9].astype(jnp.bfloat16), "seq").astype(jnp.float32),
        lax.psum(owned[10].astype(jnp.bfloat16), "seq").astype(jnp.float32),
        lax.psum(owned[11].astype(jnp.bfloat16), "seq").astype(jnp.float32),
        lax.psum(owned[12].astype(jnp.bfloat16), "seq").astype(jnp.float32),
    )
    return (layer_output.reshape(seqs, half, width), input_grad) + tuple(summed)


def finish_kernel(lo, ig, gi, go, ge, gc, vec, lo_o, ig_o, gi_o, go_o, ge_o, gc_o, *rest):
    small, bufs, sems = rest[:9], rest[9:15], rest[15]
    pairs = list(zip((ig, lo, ge, gi, gc, go), (bufs[1], bufs[0], bufs[4], bufs[2], bufs[5], bufs[3])))
    results = (ig_o, lo_o, ge_o, gi_o, gc_o, go_o)
    loads = [pltpu.make_async_copy(a, b, sems.at[0, k]) for k, (a, b) in enumerate(pairs)]
    stores = [pltpu.make_async_copy(b, r, sems.at[1, k]) for k, ((_, b), r) in enumerate(zip(pairs, results))]
    for d in loads:
        d.start()
    own = small[0].shape[1]
    for k in range(8):
        small[k][...] = vec[k : k + 1, :own]
    for k in range(4):
        small[8][:, k * own : (k + 1) * own] = vec[k : k + 1, 64 : 64 + own]
    for a, b in zip(loads, stores):
        a.wait()
        b.start()
    for b in stores:
        b.wait()


def finish(lo, ig, gi, go, ge, gc, vec, own):
    sh = jax.ShapeDtypeStruct
    anyspec = pl.BlockSpec(memory_space=pl.ANY)
    vspec = pl.BlockSpec(memory_space=VM)
    big = (lo, ig, gi, go, ge, gc)
    return pl.pallas_call(
        finish_kernel,
        out_shape=[sh(v.shape, v.dtype) for v in big] + [sh((1, own), F32)] * 8 + [sh((1, 4 * own), F32)],
        in_specs=[anyspec] * 6 + [vspec],
        out_specs=[anyspec] * 6 + [vspec] * 9,
        scratch_shapes=[VM(v.shape, v.dtype) for v in big] + [DMA((2, 6))],
    )(*big, vec)


def fused_body(
    tokens, time_embed, segments, input_weight, query_bias, value_bias, output_weight, output_bias, first_gain,
    first_shift, expand_weight, expand_bias, contract_weight, contract_bias, second_gain, second_shift, cotangent,
):
    vectors = [
        query_bias, value_bias, output_bias, first_gain, first_shift, contract_bias, second_gain, second_shift,
        expand_bias,
    ]
    own = query_bias.shape[0]
    vectors = [v.reshape(1, own) for v in vectors[:8]] + [expand_bias]
    parts = fused_layer(
        tokens[0], time_embed, segments, input_weight, output_weight, expand_weight, contract_weight, vectors,
        cotangent[0],
    )[:7]
    layer_output, input_grad, g_in, g_out, g_exp, g_con, *row = finish(*parts, own)
    row = [v.reshape(v.shape[1]) for v in row]
    return (
        layer_output[None], input_grad[None], g_in, row[0], row[1], g_out, row[2], row[3], row[4],
        g_exp, row[8], g_con, row[5], row[6], row[7],
    )


def body(*args):
    if lax.axis_size("dp") == 16 and lax.axis_size("seq") == 2:
        return fused_body(*args)
    return plain_body(*args)


def solution(mesh):
    return jax.shard_map(
        body,
        mesh=mesh,
        in_specs=(
            P("dp", "seq", None),
            P("dp", None),
            P("dp", None),
            P("dp", None),
            P("dp"),
            P("dp"),
            P("dp", None),
            P("dp"),
            P("dp"),
            P("dp"),
            P("dp", None),
            P("dp"),
            P("dp", None),
            P("dp"),
            P("dp"),
            P("dp"),
            P("dp", "seq", None),
        ),
        out_specs=(
            P("dp", "seq", None),
            P("dp", "seq", None),
            P("dp", None),
            P("dp"),
            P("dp"),
            P("dp", None),
            P("dp"),
            P("dp"),
            P("dp"),
            P("dp", None),
            P("dp"),
            P("dp", None),
            P("dp"),
            P("dp"),
            P("dp"),
        ),
        check_vma=False,
    )
```
